768 devices in a mesh: sec: 2 (over x_hi), gx: 24 (over x_lo, z), az: 16 (over y, core).
Axes of the slice: x: 4 (x_hi: 2, x_lo: 2; x = x_hi * 2 + x_lo), y: 8, z: 12, core: 2. Of those that a mesh axis runs over, the one named last changes fastest.
Arguments:
- les_velocity: float32 [3, 8, 256, 6144], P(None, None, 'az', ('sec', 'gx')), may hold values from -6 to 6
- les_metric: float32 [3, 8, 256, 6144], P(None, None, 'az', ('sec', 'gx')), may hold values from 0.5 to 1.5
- caa_state: float32 [4, 8, 256, 6144], P(None, None, 'az', ('sec', 'gx')), may hold values from -6 to 6
- caa_metric: float32 [3, 8, 256, 6144], P(None, None, 'az', ('sec', 'gx')), may hold values from 0.5 to 1.5
- intersection_refs: int32 [768, 4], P(('sec', 'gx')), may hold values from 0 to 23, as said below
- offsets: int32 [768], P(('sec', 'gx')), may hold values from 0 to 8
- send_list: int32 [48, 24, 2], replicated, may hold values from -1 to 15, as said below
Outputs:
- les_out: float32 [3, 8, 256, 6144], P(None, None, 'az', ('sec', 'gx'))
- caa_out: float32 [4, 8, 256, 6144], P(None, None, 'az', ('sec', 'gx'))
The draws below stay inside these ranges and needn't reach their ends.
Inputs may be any that keep to these rules, and one draw needn't show every extreme that they name: `intersection_refs`: row j belongs to slab r = j // 16; columns 0 and 2 are slabs of r's section (0 to 23), columns 1 and 3 slots (0 to 1). Among the 32 pairs of one slab no (slab, slot) pair repeats, at most 2 name one slab and exactly 2 name some slab, the slots towards one slab are filled from 0 upward, and send_list holds a block (not -1) at every named pair. send_list[s, d, c] is a block of slab s (0 to 15) for slot c of slab d of the same section, and -1 exactly where no row of slab d names (s, c).
All inputs are finite; a program needn't handle non-finite values.
Results may differ from the reference program's by a relative error of at most 0.00081.
Values may be sent and summed in bfloat16 or wider, within the bound.
No kernel may reach another device: no remote copies, remote signals or barrier semaphores. Data moves between devices by JAX's collectives and lax.ppermute only.
A program may use at most 32 MiB of HBM per device.

```python
import math
import jax
import jax.numpy as jnp
import numpy as np
from jax import lax

NR = 8
B = 16
LES_STEPS = 2
CAA_SUB = 4
CAP = 2
NA = 256
NS = 6144
SLOTS = 768
N_SEC = 2
N_GX = 24


def intersection_tables(key):
    base_key = jax.random.fold_in(key, 7177)
    row_count = N_SEC * N_GX
    row_keys = jax.random.split(base_key, row_count)

    def one_row(row_key):
        first_key, second_key, third_key, fourth_key = jax.random.split(row_key, 4)
        forced = jax.random.randint(first_key, (), 0, N_GX).astype(jnp.int32)
        others = jnp.arange(N_GX - 1, dtype=jnp.int32)
        others = jnp.where(others >= forced, others + 1, others)
        candidates = jax.random.permutation(second_key, jnp.repeat(others, CAP))
        chosen = jnp.concatenate([jnp.full((CAP,), forced, jnp.int32), candidates])[:2 * B]
        chosen = jax.random.permutation(third_key, chosen)
        earlier = jnp.tril(jnp.ones((2 * B, 2 * B), jnp.int32), -1)
        matching = (chosen[:, None] == chosen[None, :]).astype(jnp.int32)
        slot_index = jnp.sum(matching * earlier, axis=1).astype(jnp.int32)
        block_index = jax.random.randint(fourth_key, (2 * B,), 0, B).astype(jnp.int32)
        return (chosen, slot_index, block_index)
    chosen, slot_index, block_index = jax.vmap(one_row)(row_keys)
    ref_table = jnp.stack([chosen[:, 0::2], slot_index[:, 0::2], chosen[:, 1::2], slot_index[:, 1::2]], axis=-1)
    ref_table = ref_table.reshape(row_count * B, 4).astype(jnp.int32)
    rows_all = jnp.arange(row_count, dtype=jnp.int32)
    section = rows_all // N_GX
    target = jnp.broadcast_to((rows_all % N_GX)[:, None], chosen.shape)
    owner_row = section[:, None] * N_GX + chosen
    send_table = jnp.full((row_count, N_GX, CAP), -1, jnp.int32)
    send_table = send_table.at[owner_row, target, slot_index].set(block_index)
    return (ref_table, send_table)


def draw_intersection_refs(key, part):
    return intersection_tables(key)[0]


def draw_send_list(key, part):
    return intersection_tables(key)[1]


def plant(entries, rng, low, top_value):
    shape = entries.shape
    place = [jax.random.randint(jax.random.fold_in(rng, axis), (), 0, shape[axis]) for axis in range(len(shape))]
    entries = entries.at[tuple(place)].set(low)
    longest = shape.index(max(shape))
    place[longest] = (place[longest] + 1) % shape[longest]
    return entries.at[tuple(place)].set(top_value)


def level_of(rng, dims, cuts, least, high):
    level = 1.0
    for axis_at, shards_of in cuts:
        steps = jax.random.uniform(jax.random.fold_in(jax.random.fold_in(rng, 6), axis_at), (shards_of,), jnp.float32, least / len(cuts), high / len(cuts))
        level = level * jnp.repeat(jnp.exp(steps), dims[axis_at] // shards_of).reshape((-1,) + (1,) * (len(dims) - 1 - axis_at))
    return level


def scatter_about(key, shape, width, most, pieces=(), kind=jnp.bfloat16):
    entries = width * jax.random.normal(key, shape, jnp.float32)
    if pieces:
        entries = entries * level_of(key, shape, pieces, -0.22, 0.18)
    return jnp.clip(entries, -most, most).astype(kind)


def setup_inputs(seed: int = 0) -> dict:
    splits = jax.random.split(jax.random.key(seed), 8)
    return {
        "les_velocity": scatter_about(splits[0], (3, NR, NA, NS), 1.0, 6.0, ((2, 16), (3, 48)), jnp.float32),
        "les_metric": jnp.clip(jnp.exp(math.log(1.5) - 1.0986123 * jax.random.uniform(splits[1], (3, NR, NA, NS), jnp.float32) ** level_of(splits[1], (3, NR, NA, NS), ((2, 16), (3, 48)), -0.2, 0.2)), 0.5, 1.5),
        "caa_state": scatter_about(splits[2], (4, NR, NA, NS), 1.0, 6.0, ((2, 16), (3, 48)), jnp.float32),
        "caa_metric": jnp.clip(jnp.exp(math.log(1.5) - 1.0986123 * jax.random.uniform(splits[3], (3, NR, NA, NS), jnp.float32) ** level_of(splits[3], (3, NR, NA, NS), ((2, 16), (3, 48)), -0.2, 0.2)), 0.5, 1.5),
        "intersection_refs": draw_intersection_refs(jax.random.fold_in(splits[7], 71), 0),
        "offsets": plant(jax.random.randint(splits[5], (SLOTS,), 0, 9), jax.random.fold_in(splits[5], 1), 0, 8).astype(jnp.int32),
        "send_list": draw_send_list(jax.random.fold_in(splits[7], 71), 0),
    }


les_step = 0.02
caa_step = 0.01
mach_number = 0.5
directions = ((3, False), (2, True), (1, False))


def slope_table():
    points = np.array([-1.0, -(0.2 ** 0.5), 0.2 ** 0.5, 1.0])
    identity = np.eye(4)
    differences = points[:, None] - points[None, :] + identity
    inverse_weights = 1.0 / np.prod(differences, axis=1)
    slope_matrix = (inverse_weights[None, :] / inverse_weights[:, None]) / differences
    slope_matrix = slope_matrix * (1.0 - identity)
    return slope_matrix - identity * slope_matrix.sum(axis=1)[:, None]


def line_slope(quantity, ghost_low, ghost_high):
    slope_matrix = jnp.asarray(slope_table(), jnp.float32)
    element_count = quantity.shape[-1] // 4
    elements = quantity.reshape(quantity.shape[:-1] + (element_count, 4))
    interior = jnp.einsum("...ej,ij->...ei", elements, slope_matrix, precision=lax.Precision.HIGHEST)
    leading = elements[..., 0]
    trailing = elements[..., 3]
    preceding = jnp.concatenate([ghost_low[..., None], trailing[..., :-1]], axis=-1)
    following = jnp.concatenate([leading[..., 1:], ghost_high[..., None]], axis=-1)
    interior = interior.at[..., 0].add(3.0 * (leading - preceding))
    interior = interior.at[..., 3].add(3.0 * (following - trailing))
    return interior.reshape(quantity.shape)


def slope(quantity, axis_dim, periodic):
    lined_up = jnp.moveaxis(quantity, axis_dim, -1)
    if periodic:
        ghost_low = lined_up[..., -1]
        ghost_high = lined_up[..., 0]
    else:
        ghost_low = jnp.zeros_like(lined_up[..., 0])
        ghost_high = jnp.zeros_like(lined_up[..., 0])
    return jnp.moveaxis(line_slope(lined_up, ghost_low, ghost_high), -1, axis_dim)


def les_rates(velocity, metric):
    slopes = []
    fluxes = []
    for direction, (axis_dim, periodic) in enumerate(directions):
        slopes.append(metric[direction][None] * slope(velocity, axis_dim, periodic))
        fluxes.append(metric[direction][None] * slope(velocity[direction][None] * velocity, axis_dim, periodic))
    change = -0.5 * sum(fluxes[j] + velocity[j][None] * slopes[j] for j in range(3))
    omega_first = slopes[1][2] - slopes[2][1]
    omega_second = slopes[2][0] - slopes[0][2]
    omega_third = slopes[0][1] - slopes[1][0]
    lamb_vector = jnp.stack([
        omega_second * velocity[2] - omega_third * velocity[1],
        omega_third * velocity[0] - omega_first * velocity[2],
        omega_first * velocity[1] - omega_second * velocity[0]])
    return change, lamb_vector


def caa_rates(acoustic, metric, source):
    stream_slope = metric[0][None] * slope(acoustic, 3, False)
    azimuth_slope = metric[1][None] * slope(jnp.stack([acoustic[0], acoustic[2]]), 2, True)
    radial_slope = metric[2][None] * slope(jnp.stack([acoustic[0], acoustic[3]]), 1, False)
    return jnp.stack([
        -(mach_number * stream_slope[0] + stream_slope[1] + azimuth_slope[1] + radial_slope[1]),
        -(mach_number * stream_slope[1] + stream_slope[0]) + source[0],
        -(mach_number * stream_slope[2] + azimuth_slope[0]) + source[1],
        -(mach_number * stream_slope[3] + radial_slope[0]) + source[2]])


def couple(lamb_vector, intersection_refs, offsets, send_list):
    rounded = lamb_vector.astype(jnp.bfloat16)
    components, radial_nodes, sector_nodes, length = rounded.shape
    block_count = length // 8
    blocks = rounded.reshape(components, radial_nodes, sector_nodes, block_count, 8).transpose(3, 0, 1, 2, 4)
    slot_rows = jnp.arange(block_count, dtype=jnp.int32) // B
    section = slot_rows // N_GX
    target = slot_rows % N_GX

    def fetch_block(owner_slab, slot_index):
        owner_row = section * N_GX + owner_slab
        return blocks[owner_row * B + send_list[owner_row, target, slot_index]].astype(jnp.float32)

    leading = fetch_block(intersection_refs[:, 0], intersection_refs[:, 1])
    trailing = fetch_block(intersection_refs[:, 2], intersection_refs[:, 3])
    fraction = offsets.astype(jnp.float32)[:, None, None, None, None]
    blended = ((8.0 - fraction) * leading + fraction * trailing) / 8.0
    return blended.transpose(1, 2, 3, 0, 4).reshape(components, radial_nodes, sector_nodes, length)


def reference(les_velocity, les_metric, caa_state, caa_metric, intersection_refs, offsets, send_list):
    velocity = les_velocity
    acoustic = caa_state
    for les_round in range(LES_STEPS):
        change, lamb_vector = les_rates(velocity, les_metric)
        source = couple(lamb_vector, intersection_refs, offsets, send_list)
        velocity = velocity + les_step * change
        for substep in range(CAA_SUB):
            acoustic = acoustic + caa_step * caa_rates(acoustic, caa_metric, source)
    return velocity, acoustic
```

```python
import functools

import jax
import jax.numpy as jnp
import numpy as np
from jax import lax
from jax.experimental import pallas as pl
from jax.experimental.pallas import tpu as pltpu
from jax.sharding import PartitionSpec as P


les_step = 0.02
caa_step = 0.01
mach_number = 0.5

STREAM = ("sec", "gx")
F32 = jnp.float32
BF16 = jnp.bfloat16
VMEM_LIMIT = 24 * 1024 * 1024


def slope_table():
    points = np.array([-1.0, -(0.2**0.5), 0.2**0.5, 1.0])
    identity = np.eye(4)
    differences = points[:, None] - points[None, :] + identity
    inverse_weights = 1.0 / np.prod(differences, axis=1)
    slope_matrix = inverse_weights[None, :] / inverse_weights[:, None] / differences
    slope_matrix = slope_matrix * (1.0 - identity)
    return slope_matrix - identity * slope_matrix.sum(axis=1)[:, None]


DM = slope_table() + np.diag([3.0, 0.0, 0.0, -3.0])
DM[np.abs(DM) < 1e-12] = 0.0


def lane_matrix(run):
    result = np.zeros((128, 128))
    for e in range(32):
        result[4 * e : 4 * e + 4, 4 * e : 4 * e + 4] = DM.T
        if (4 * e) % run:
            result[4 * e - 1, 4 * e] = -3.0
        if (4 * e + 4) % run:
            result[4 * e + 4, 4 * e + 3] = 3.0
    return result


def split_matrix(run):
    full = lane_matrix(run).astype(np.float32)
    high = full.astype(jnp.bfloat16)
    low = (full - high.astype(np.float32)).astype(jnp.bfloat16)
    return np.block([[high, low], [high, np.zeros_like(low)]])


OFFSETS = (-3, -2, -1, 1, 2, 3)
RAD, AZT, AZP, AZN, EDGE_M, EDGE_T = 0, 6, 12, 13, 14, 15


def coefficients():
    c = np.zeros((16, 8, 128), np.float32)
    for n, k in enumerate(OFFSETS):
        for s in range(8):
            i = s % 4
            if 0 <= i + k <= 3:
                c[RAD + n, s, :] = DM[i, i + k]
        for lane in range(128):
            i = (lane % 64) // 16
            if 0 <= i + k <= 3:
                c[AZT + n, :, lane] = DM[i, i + k]
    c[RAD + OFFSETS.index(1), 3, :] = 3.0
    c[RAD + OFFSETS.index(-1), 4, :] = -3.0
    for lane in range(128):
        i = (lane % 64) // 16
        if i == 0:
            c[AZP, :, lane] = -3.0
        if i == 3:
            c[AZN, :, lane] = 3.0
    c[EDGE_M, :, 127] = 3.0
    c[EDGE_M, :, 0] = -3.0
    for i in range(4):
        c[EDGE_T, :, 16 * i] = -3.0
        c[EDGE_T, :, 79 + 16 * i] = 3.0
    return c


def lanes_of():
    return lax.broadcasted_iota(jnp.int32, (8, 128), 1)


def lane_roll(x, shift):
    shift %= 128
    return pltpu.roll(x, shift, axis=1) if shift else x


def times(rows, weights):
    x = jnp.concatenate(rows, axis=0)
    high = x.astype(BF16)
    low = (x - high.astype(F32)).astype(BF16)
    y = jnp.dot(jnp.concatenate([high, low], axis=1), weights, preferred_element_type=F32)
    y = y[:, :128] + y[:, 128:]
    return [y[8 * n : 8 * n + 8] for n in range(len(rows))]


def stream_main(fields, halos, weights, coef):
    lane = lanes_of()
    out = times([row for rows in fields for row in rows], weights)
    results = []
    at = 0
    for rows, tiles in zip(fields, halos):
        result = []
        for n in range(len(rows)):
            tile, i = tiles[n // 4], n % 4
            edge = jnp.where(lane == 127, lane_roll(tile, 127 - 16 * i), lane_roll(tile, 49 - 16 * i))
            result.append(out[at] + coef[EDGE_M] * edge)
            at += 1
        results.append(result)
    return results


def stream_halo(fields, halos, weights, coef):
    lane = lanes_of()
    out = times([tile for tiles in halos for tile in tiles], weights)
    results = []
    at = 0
    for rows, tiles in zip(fields, halos):
        result = []
        for e in range(len(tiles)):
            edge = None
            for i in range(4):
                low, high = lane_roll(rows[4 * e + i], 16 * i + 1), lane_roll(rows[4 * e + i], 79 + 16 * i)
                edge = low if edge is None else jnp.where(lane == 16 * i, low, edge)
                edge = jnp.where(lane == 79 + 16 * i, high, edge)
            result.append(out[at] + coef[EDGE_T] * edge)
            at += 1
        results.append(result)
    return results


def azimuth_main(rows, before, after):
    out = []
    for e in range(len(rows) // 4):
        f = rows[4 * e : 4 * e + 4]
        prev = before if e == 0 else rows[4 * e - 1]
        following = after if 4 * e + 4 == len(rows) else rows[4 * e + 4]
        a, b, c = float(DM[0, 1]), float(DM[0, 2]), float(DM[0, 3])
        d, g, h = float(DM[1, 0]), float(DM[1, 2]), float(DM[1, 3])
        out.append(a * f[1] + b * f[2] + c * f[3] - 3.0 * prev)
        out.append(d * f[0] + g * f[2] + h * f[3])
        out.append(-(h * f[0] + g * f[1] + d * f[3]))
        out.append(3.0 * following - (c * f[0] + b * f[1] + a * f[2]))
    return out


def azimuth_halo(tiles, before, after, coef):
    out = []
    for e, tile in enumerate(tiles):
        prev = before if e == 0 else tiles[e - 1]
        following = after if e + 1 == len(tiles) else tiles[e + 1]
        total = coef[AZP] * lane_roll(prev, -48) + coef[AZN] * lane_roll(following, 48)
        for n, k in enumerate(OFFSETS):
            total = total + coef[AZT + n] * lane_roll(tile, -16 * k)
        out.append(total)
    return out


def radial(tiles, coef):
    out = []
    for tile in tiles:
        total = None
        for n, k in enumerate(OFFSETS):
            term = coef[RAD + n] * pltpu.roll(tile, (-k) % 8, axis=0)
            total = term if total is None else total + term
        out.append(total)
    return out


def pack(rows, last):
    lane = lanes_of()
    out = None
    for g, row in enumerate(rows):
        moved = lane_roll(row, 16 * g + (16 if last else 0))
        out = moved if out is None else jnp.where(lane >= 16 * g, moved, out)
    return out


def halo_tile(from_left, from_right, n):
    left, right = from_left[n // 2].astype(F32), from_right[n // 2].astype(F32)
    if n % 2:
        right = lane_roll(right, 64)
    else:
        left = lane_roll(left, 64)
    return jnp.where(lanes_of() < 64, right, left)


def turn(tiles):
    group = lanes_of() // 8
    tiles = list(tiles)
    for bit in range(4):
        step = 1 << bit
        high = (group & step) != 0
        for p in range(16):
            if p & step:
                continue
            x, y = tiles[p], tiles[p | step]
            tiles[p] = jnp.where(high, lane_roll(y, 8 * step), x)
            tiles[p | step] = jnp.where(high, y, lane_roll(x, -8 * step))
    return tiles


def column(ref, c, az, sector):
    return ref[c, pl.ds(az, 8, stride=sector), :]


def first_kernel(sector, u, lm, w, m, low, high, both):
    for c in range(3):
        for i in range(4):
            low[4 * c + i] = column(u, c, i, sector)
            high[4 * c + i] = column(u, c, sector - 4 + i, sector)
        low[12 + c] = column(lm, c, 0, sector)
        high[12 + c] = column(lm, c, sector - 1, sector)
    for f in range(7):
        for az in range(sector):
            value = column(w, f, az, sector) if f < 4 else column(m, f - 4, az, sector)
            both[f * sector + az] = value.astype(BF16)


def les_pack_kernel(sector, u, lm, before, after, first, last):
    entries = []
    for c in range(3):
        for e in range(-1, 5):
            if e < 0:
                entries.append([before[4 * c + i] for i in range(4)])
            elif e == 4:
                entries.append([after[4 * c + i] for i in range(4)])
            else:
                entries.append([column(u, c, 4 * e + i, sector) for i in range(4)])
    for c in range(3):
        for e in range(4):
            entries.append([column(lm, c, 4 * e + i, sector) for i in range(4)])
    for n in range(len(entries) // 2):
        rows = entries[2 * n] + entries[2 * n + 1]
        first[n] = pack(rows, False)
        last[n] = pack(rows, True)


def les_kernel(sector, sends, u, lm, before, after, from_left, from_right, weights, coef, out, sent, um, ut, mm, mt, lamb, blk):
    w_main, w_halo = weights[0], weights[1]
    zero = jnp.zeros((8, 128), F32)
    for c in range(3):
        for i in range(4):
            um[0, c, i] = before[4 * c + i]
            um[0, c, 4 + sector + i] = after[4 * c + i]
            mm[c, i] = before[12 + c] if i == 3 else zero
            mm[c, 4 + sector + i] = after[12 + c] if i == 0 else zero
        for az in range(sector):
            um[0, c, 4 + az] = column(u, c, az, sector)
            mm[c, 4 + az] = column(lm, c, az, sector)
        for e in range(6):
            ut[0, c, e] = halo_tile(from_left, from_right, 6 * c + e)
            mt[c, e] = halo_tile(from_left, from_right, 18 + 4 * c + e - 1) if 1 <= e <= 4 else zero

    def element(step, e):
        rows = [[um[step, c, 4 * e + i] for i in range(4)] for c in range(3)]
        tiles = [[ut[step, c, e]] for c in range(3)]
        if isinstance(e, int):
            below, above, tile_below, tile_above = max(4 * e - 1, 0), min(4 * e + 4, sector + 7), max(e - 1, 0), min(e + 1, 5)
        else:
            below, above = jnp.maximum(4 * e - 1, 0), jnp.minimum(4 * e + 4, sector + 7)
            tile_below, tile_above = jnp.maximum(e - 1, 0), jnp.minimum(e + 1, 5)
        prev = [um[step, c, below] for c in range(3)]
        following = [um[step, c, above] for c in range(3)]
        metric = [[mm[c, 4 * e + i] for i in range(4)] for c in range(3)]

        fields = rows + [[x * y for x, y in zip(rows[0], rows[c])] for c in range(3)]
        halos = tiles + [[tiles[0][0] * tiles[c][0]] for c in range(3)]
        stream = stream_main(fields, halos, w_main, coef)
        slopes = [[[a * b for a, b in zip(metric[0], stream[c])] for c in range(3)]]
        fluxes = [[[a * b for a, b in zip(metric[0], stream[3 + c])] for c in range(3)]]
        slopes.append([])
        fluxes.append([])
        for c in range(3):
            slopes[1].append([a * b for a, b in zip(metric[1], azimuth_main(rows[c], prev[c], following[c]))])
            product = [x * y for x, y in zip(rows[1], rows[c])]
            product = azimuth_main(product, prev[1] * prev[c], following[1] * following[c])
            fluxes[1].append([a * b for a, b in zip(metric[1], product)])
        slopes.append([])
        fluxes.append([])
        for c in range(3):
            slopes[2].append([a * b for a, b in zip(metric[2], radial(rows[c], coef))])
            product = radial([x * y for x, y in zip(rows[2], rows[c])], coef)
            fluxes[2].append([a * b for a, b in zip(metric[2], product)])
        for i in range(4):
            first = slopes[1][2][i] - slopes[2][1][i]
            second = slopes[2][0][i] - slopes[0][2][i]
            third = slopes[0][1][i] - slopes[1][0][i]
            at = 4 * e + i
            lamb[0, at] = second * rows[2][i] - third * rows[1][i]
            lamb[1, at] = third * rows[0][i] - first * rows[2][i]
            lamb[2, at] = first * rows[1][i] - second * rows[0][i]
            for c in range(3):
                total = None
                for j in range(3):
                    term = fluxes[j][c][i] + rows[j][i] * slopes[j][c][i]
                    total = term if total is None else total + term
                value = rows[c][i] - (0.5 * les_step) * total
                if step == 0:
                    um[1, c, at] = value
                else:
                    out[c, pl.ds(at - 4, 8, stride=sector), :] = value
        if step == 0:
            low = [ut[step, c, tile_below] for c in range(3)]
            high = [ut[step, c, tile_above] for c in range(3)]
            metric = [mt[c, e] for c in range(3)]
            stream = stream_halo(fields, halos, w_halo, coef)
            for c in range(3):
                total = metric[0] * (stream[3 + c][0] + tiles[0][0] * stream[c][0])
                slope = azimuth_halo(tiles[c], low[c], high[c], coef)[0]
                flux = azimuth_halo([tiles[1][0] * tiles[c][0]], low[1] * low[c], high[1] * high[c], coef)[0]
                total = total + metric[1] * (flux + tiles[1][0] * slope)
                slope = radial(tiles[c], coef)[0]
                flux = radial([tiles[2][0] * tiles[c][0]], coef)[0]
                total = total + metric[2] * (flux + tiles[2][0] * slope)
                ut[1, c, e] = tiles[c][0] - (0.5 * les_step) * total

    for step in range(2):

        @pl.loop(0 if step == 0 else 1, 6 if step == 0 else 5)
        def _(e):
            element(step, e)

        for c in range(3):
            blocks = turn([lamb[c, 4 + az] for az in range(sector)])
            for j in range(16):
                blk[j, 3 * step + c] = blocks[j].astype(BF16)

    @pl.loop(0, sends.shape[0])
    def _(n):
        index = jnp.clip(sends[n], 0, 15)
        slab, slot = n // 2, n % 2
        for step in range(2):
            for c in range(3):
                sent[4 * slab + 2 * step + slot, c] = blk[index, 3 * step + c]


def blend_kernel(sector, slabs, refs, offsets, got, own, up, down):
    for step in range(2):
        for c in range(3):
            tiles = []
            for j in range(16):
                a = jnp.clip(refs[4 * j], 0, slabs - 1) * 4 + 2 * step + jnp.clip(refs[4 * j + 1], 0, 1)
                b = jnp.clip(refs[4 * j + 2], 0, slabs - 1) * 4 + 2 * step + jnp.clip(refs[4 * j + 3], 0, 1)
                fraction = offsets[j].astype(F32)
                blend = (8.0 - fraction) * got[a, c].astype(F32) + fraction * got[b, c].astype(F32)
                tiles.append(blend * 0.125)
            tiles = turn(tiles)
            for az in range(sector):
                own[step, c, az] = tiles[az]
                narrow = tiles[az].astype(BF16)
                if step == 0:
                    up[c * 16 + az] = narrow
                    down[c * 16 + az] = narrow
                else:
                    if az >= 8:
                        up[48 + c * 8 + az - 8] = narrow
                    else:
                        down[48 + c * 8 + az] = narrow


def caa_pack_kernel(sector, own, below, above, w, m, caa_below, caa_above, first, last):
    entries = []
    for c in range(3):
        for e in range(12):
            if e < 4:
                entries.append([(below, c * 16 + 4 * e + i) for i in range(4)])
            elif e < 8:
                entries.append([(own, (0, c, 4 * (e - 4) + i)) for i in range(4)])
            else:
                entries.append([(above, c * 16 + 4 * (e - 8) + i) for i in range(4)])
    for c in range(3):
        for e in range(2, 10):
            if e < 4:
                entries.append([(below, 48 + c * 8 + 4 * (e - 2) + i) for i in range(4)])
            elif e < 8:
                entries.append([(own, (1, c, 4 * (e - 4) + i)) for i in range(4)])
            else:
                entries.append([(above, 48 + c * 8 + 4 * (e - 8) + i) for i in range(4)])
    for f in range(7):
        for e in range(12):
            if e < 4:
                entries.append([(caa_below, f * sector + 4 * e + i) for i in range(4)])
            elif e < 8:
                ref, c = (w, f) if f < 4 else (m, f - 4)
                entries.append([(ref, (c, pl.ds(4 * (e - 4) + i, 8, stride=sector), slice(None))) for i in range(4)])
            else:
                entries.append([(caa_above, f * sector + 4 * (e - 8) + i) for i in range(4)])
    for n in range(len(entries) // 2):
        rows = [ref[at].astype(F32) for ref, at in entries[2 * n] + entries[2 * n + 1]]
        first[n] = pack(rows, False).astype(BF16)
        last[n] = pack(rows, True).astype(BF16)


CAA_RANGES = ((0, 12), (1, 11), (1, 11), (2, 10), (2, 10), (3, 9), (3, 9), (4, 8))


def caa_kernel(sector, w, m, own, below, above, caa_below, caa_above, from_left, from_right, weights, coef, out, wm, wt, mm, mt, sm, st):
    w_main, w_halo = weights[0], weights[1]

    for f in range(7):
        for az in range(3 * sector):
            if az < sector:
                value = caa_below[f * sector + az].astype(F32)
            elif az < 2 * sector:
                value = column(w, f, az - sector, sector) if f < 4 else column(m, f - 4, az - sector, sector)
            else:
                value = caa_above[f * sector + az - 2 * sector].astype(F32)
            if f < 4:
                wm[0, f, az] = value
            else:
                mm[f - 4, az] = value * caa_step
        for e in range(12):
            value = halo_tile(from_left, from_right, 60 + 12 * f + e)
            if f < 4:
                wt[0, f, e] = value
            else:
                mt[f - 4, e] = value * caa_step
    for c in range(3):
        for az in range(16):
            sm[0, c, az] = below[c * 16 + az].astype(F32) * caa_step
            sm[0, c, 16 + az] = own[0, c, az] * caa_step
            sm[0, c, 32 + az] = above[c * 16 + az].astype(F32) * caa_step
            sm[1, c, 16 + az] = own[1, c, az] * caa_step
        for az in range(8):
            sm[1, c, 8 + az] = below[48 + c * 8 + az].astype(F32) * caa_step
            sm[1, c, 32 + az] = above[48 + c * 8 + az].astype(F32) * caa_step
        for e in range(12):
            st[0, c, e] = halo_tile(from_left, from_right, 12 * c + e) * caa_step
        for e in range(8):
            st[1, c, 2 + e] = halo_tile(from_left, from_right, 36 + 8 * c + e) * caa_step

    def pair(now, source, e, final):
        rows = [[wm[now, f, 4 * e + i] for i in range(8)] for f in range(4)]
        tiles = [[wt[now, f, e + n] for n in range(2)] for f in range(4)]
        below, above = jnp.maximum(4 * e - 1, 0), jnp.minimum(4 * e + 8, 47)
        tile_below, tile_above = jnp.maximum(e - 1, 0), jnp.minimum(e + 2, 11)

        def rates(values, metric, sources, stream, around, up):
            p, v0, v1, v2 = values
            count = len(p)
            azimuth_p, azimuth_v = around
            radial_p, radial_v = up
            for n in range(count):
                m0, m1, m2 = metric[0](n), metric[1](n), metric[2](n)
                half = mach_number * m0
                yield (
                    n,
                    p[n] - m0 * stream[0][n] - m1 * azimuth_v[n] - m2 * radial_v[n],
                    v0[n] - m0 * stream[1][n] + sources[0](n),
                    v1[n] - half * stream[2][n] - m1 * azimuth_p[n] + sources[1](n),
                    v2[n] - half * stream[3][n] - m2 * radial_p[n] + sources[2](n),
                )

        def mixed(values):
            p, v0, v1, v2 = values
            return [
                [mach_number * a + b for a, b in zip(p, v0)],
                [mach_number * b + a for a, b in zip(p, v0)],
                v1,
                v2,
            ]

        fields, halos = mixed(rows), mixed(tiles)
        stream = stream_main(fields, halos, w_main, coef)
        around = [azimuth_main(rows[f], wm[now, f, below], wm[now, f, above]) for f in (0, 2)]
        up = [radial(rows[f], coef) for f in (0, 3)]
        metric = [lambda n, c=c: mm[c, 4 * e + n] for c in range(3)]
        sources = [lambda n, c=c: sm[source, c, 4 * e + n] for c in range(3)]
        for n, *values in rates(rows, metric, sources, stream, around, up):
            for f in range(4):
                if final:
                    out[f, pl.ds(4 * e + n - 16, 8, stride=sector), :] = values[f]
                else:
                    wm[1 - now, f, 4 * e + n] = values[f]
        if not final:
            stream = stream_halo(fields, halos, w_halo, coef)
            around = [azimuth_halo(tiles[f], wt[now, f, tile_below], wt[now, f, tile_above], coef) for f in (0, 2)]
            up = [radial(tiles[f], coef) for f in (0, 3)]
            metric = [lambda n, c=c: mt[c, e + n] for c in range(3)]
            sources = [lambda n, c=c: st[source, c, e + n] for c in range(3)]
            for n, *values in rates(tiles, metric, sources, stream, around, up):
                for f in range(4):
                    wt[1 - now, f, e + n] = values[f]

    for step, (start, stop) in enumerate(CAA_RANGES):

        @pl.loop(0, (stop - start) // 2)
        def _(n):
            pair(step % 2, step // 4, start + 2 * n, step == 7)


def call(kernel, name, outs, *args, smem=0, scratch=()):
    whole = pl.BlockSpec(memory_space=pltpu.VMEM)
    return pl.pallas_call(
        kernel,
        name=name,
        out_shape=[jax.ShapeDtypeStruct(shape, dtype) for shape, dtype in outs],
        in_specs=[pl.BlockSpec(memory_space=pltpu.SMEM)] * smem + [whole] * (len(args) - smem),
        out_specs=[whole] * len(outs),
        scratch_shapes=[pltpu.VMEM(shape, dtype) for shape, dtype in scratch],
        compiler_params=pltpu.CompilerParams(vmem_limit_bytes=VMEM_LIMIT),
    )(*args)


def both_ways(low, high, axis, closed):
    count = lax.axis_size(axis)
    ends = count if closed else count - 1
    below = lax.ppermute(high, axis, [(i, (i + 1) % count) for i in range(ends)])
    above = lax.ppermute(low, axis, [((i + 1) % count, i) for i in range(ends)])
    return below, above


def body(les_velocity, les_metric, caa_state, caa_metric, intersection_refs, offsets, send_list):
    _, radial_nodes, sector, length = les_velocity.shape
    slabs = lax.axis_size("gx")
    assert (radial_nodes, sector, length) == (8, 16, 128)
    lines = radial_nodes * sector
    u, lm, w, m = (x.reshape(-1, lines, length) for x in (les_velocity, les_metric, caa_state, caa_metric))
    weights = jnp.asarray(np.stack([split_matrix(128), split_matrix(16)]))
    coef = jnp.asarray(coefficients())
    own_row = lax.axis_index("sec") * slabs + lax.axis_index("gx")
    sends = lax.dynamic_slice_in_dim(send_list, own_row, 1, axis=0).reshape(-1)
    tile = (8, 128)

    low, high, both = call(
        functools.partial(first_kernel, sector),
        "first",
        [((15, *tile), F32), ((15, *tile), F32), ((7 * sector, *tile), BF16)],
        u, lm, w, m,
    )
    before, after = both_ways(low, high, "az", True)
    caa_below, caa_above = both_ways(both, both, "az", True)
    first, last = call(
        functools.partial(les_pack_kernel, sector),
        "les_pack",
        [((15, *tile), F32)] * 2,
        u, lm, before, after,
    )
    from_left, from_right = both_ways(first, last, STREAM, False)
    les_out, sent = call(
        functools.partial(les_kernel, sector),
        "les",
        [((3, lines, length), F32), ((slabs * 4, 3, *tile), BF16)],
        sends, u, lm, before, after, from_left, from_right, weights, coef,
        smem=1,
        scratch=[
            ((2, 3, 24, *tile), F32),
            ((2, 3, 6, *tile), F32),
            ((3, 24, *tile), F32),
            ((3, 6, *tile), F32),
            ((3, 24, *tile), F32),
            ((16, 6, *tile), BF16),
        ],
    )
    got = lax.all_to_all(sent.reshape(slabs, 96, 128), "gx", 0, 0, tiled=True).reshape(slabs * 4, 3, *tile)
    own, up, down = call(
        functools.partial(blend_kernel, sector, slabs),
        "blend",
        [((2, 3, sector, *tile), F32), ((72, *tile), BF16), ((72, *tile), BF16)],
        intersection_refs.reshape(-1), offsets, got,
        smem=2,
    )
    below, above = both_ways(down, up, "az", True)
    first, last = call(
        functools.partial(caa_pack_kernel, sector),
        "caa_pack",
        [((72, *tile), BF16)] * 2,
        own, below, above, w, m, caa_below, caa_above,
    )
    from_left, from_right = both_ways(first, last, STREAM, False)
    (caa_out,) = call(
        functools.partial(caa_kernel, sector),
        "caa",
        [((4, lines, length), F32)],
        w, m, own, below, above, caa_below, caa_above, from_left, from_right, weights, coef,
        scratch=[
            ((2, 4, 48, *tile), F32),
            ((2, 4, 12, *tile), F32),
            ((3, 48, *tile), F32),
            ((3, 12, *tile), F32),
            ((2, 3, 48, *tile), F32),
            ((2, 3, 12, *tile), F32),
        ],
    )
    return les_out.reshape(les_velocity.shape), caa_out.reshape(caa_state.shape)


def solution(mesh):
    field = P(None, None, "az", STREAM)
    in_specs = (field, field, field, field, P(STREAM, None), P(STREAM), P())
    return jax.shard_map(body, mesh=mesh, in_specs=in_specs, out_specs=(field, field), check_vma=False)
```

```python
import functools

import jax
import jax.numpy as jnp
import numpy as np
from jax import lax
from jax.experimental import pallas as pl
from jax.experimental.pallas import tpu as pltpu
from jax.sharding import PartitionSpec as P


les_step = 0.02
caa_step = 0.01
mach_number = 0.5

STREAM = ("sec", "gx")
F32 = jnp.float32
BF16 = jnp.bfloat16
VMEM_LIMIT = 24 * 1024 * 1024


def slope_table():
    points = np.array([-1.0, -(0.2**0.5), 0.2**0.5, 1.0])
    identity = np.eye(4)
    differences = points[:, None] - points[None, :] + identity
    inverse_weights = 1.0 / np.prod(differences, axis=1)
    slope_matrix = inverse_weights[None, :] / inverse_weights[:, None] / differences
    slope_matrix = slope_matrix * (1.0 - identity)
    return slope_matrix - identity * slope_matrix.sum(axis=1)[:, None]


DM = slope_table() + np.diag([3.0, 0.0, 0.0, -3.0])
DM[np.abs(DM) < 1e-12] = 0.0


def lane_matrix(run):
    result = np.zeros((128, 128))
    for e in range(32):
        result[4 * e : 4 * e + 4, 4 * e : 4 * e + 4] = DM.T
        if (4 * e) % run:
            result[4 * e - 1, 4 * e] = -3.0
        if (4 * e + 4) % run:
            result[4 * e + 4, 4 * e + 3] = 3.0
    return result


def split_matrix(run):
    full = lane_matrix(run).astype(np.float32)
    high = full.astype(jnp.bfloat16)
    low = (full - high.astype(np.float32)).astype(jnp.bfloat16)
    return np.block([[high, low], [high, np.zeros_like(low)]])


OFFSETS = (-3, -2, -1, 1, 2, 3)
RAD, AZT, AZP, AZN, EDGE_M, EDGE_T = 0, 6, 12, 13, 14, 15
LES_WIDTH, CAA_WIDTH = 4, 16


def coefficients(width):
    c = np.zeros((16, 8, 128), np.float32)
    for n, k in enumerate(OFFSETS):
        for s in range(8):
            i = s % 4
            if 0 <= i + k <= 3:
                c[RAD + n, s, :] = DM[i, i + k]
        for lane in range(128):
            i = (lane % 64) // width
            if i <= 3 and 0 <= i + k <= 3:
                c[AZT + n, :, lane] = DM[i, i + k]
    c[RAD + OFFSETS.index(1), 3, :] = 3.0
    c[RAD + OFFSETS.index(-1), 4, :] = -3.0
    for lane in range(128):
        i = (lane % 64) // width
        if i == 0:
            c[AZP, :, lane] = -3.0
        if i == 3:
            c[AZN, :, lane] = 3.0
    c[EDGE_M, :, 127] = 3.0
    c[EDGE_M, :, 0] = -3.0
    for i in range(4):
        c[EDGE_T, :, width * i] = -3.0
        c[EDGE_T, :, 63 + width * (i + 1)] = 3.0
    return c


def lanes_of():
    return lax.broadcasted_iota(jnp.int32, (8, 128), 1)


def lane_roll(x, shift):
    shift %= 128
    return pltpu.roll(x, shift, axis=1) if shift else x


def times(rows, weights):
    x = jnp.concatenate(rows, axis=0)
    high = x.astype(BF16)
    low = (x - high.astype(F32)).astype(BF16)
    y = jnp.dot(jnp.concatenate([high, low], axis=1), weights, preferred_element_type=F32)
    y = y[:, :128] + y[:, 128:]
    return [y[8 * n : 8 * n + 8] for n in range(len(rows))]


def edge_main(tile, i, width):
    return jnp.where(lanes_of() == 127, lane_roll(tile, 127 - width * i), lane_roll(tile, 65 - width * (i + 1)))


def stream_main(fields, halos, weights, coef, width):
    out = times([row for rows in fields for row in rows], weights)
    results = []
    at = 0
    for rows, tiles in zip(fields, halos):
        result = []
        for n in range(len(rows)):
            result.append(out[at] + coef[EDGE_M] * edge_main(tiles[n // 4], n % 4, width))
            at += 1
        results.append(result)
    return results


def stream_halo(fields, halos, weights, coef, width):
    lane = lanes_of()
    out = times([tile for tiles in halos for tile in tiles], weights)
    results = []
    at = 0
    for rows, tiles in zip(fields, halos):
        result = []
        for e in range(len(tiles)):
            edge = None
            for i in range(4):
                row, near, far = rows[4 * e + i], width * i, 63 + width * (i + 1)
                low, high = lane_roll(row, near + 1), lane_roll(row, far)
                edge = low if edge is None else jnp.where(lane == near, low, edge)
                edge = jnp.where(lane == far, high, edge)
            result.append(out[at] + coef[EDGE_T] * edge)
            at += 1
        results.append(result)
    return results


def azimuth_main(rows, before, after):
    out = []
    for e in range(len(rows) // 4):
        f = rows[4 * e : 4 * e + 4]
        prev = before if e == 0 else rows[4 * e - 1]
        following = after if 4 * e + 4 == len(rows) else rows[4 * e + 4]
        a, b, c = float(DM[0, 1]), float(DM[0, 2]), float(DM[0, 3])
        d, g, h = float(DM[1, 0]), float(DM[1, 2]), float(DM[1, 3])
        out.append(a * f[1] + b * f[2] + c * f[3] - 3.0 * prev)
        out.append(d * f[0] + g * f[2] + h * f[3])
        out.append(-(h * f[0] + g * f[1] + d * f[3]))
        out.append(3.0 * following - (c * f[0] + b * f[1] + a * f[2]))
    return out


def azimuth_halo(tiles, before, after, coef, width):
    out = []
    for e, tile in enumerate(tiles):
        prev = before if e == 0 else tiles[e - 1]
        following = after if e + 1 == len(tiles) else tiles[e + 1]
        total = coef[AZP] * lane_roll(prev, -3 * width) + coef[AZN] * lane_roll(following, 3 * width)
        for n, k in enumerate(OFFSETS):
            total = total + coef[AZT + n] * lane_roll(tile, -width * k)
        out.append(total)
    return out


def radial(tiles, coef):
    out = []
    for tile in tiles:
        total = None
        for n, k in enumerate(OFFSETS):
            term = coef[RAD + n] * pltpu.roll(tile, (-k) % 8, axis=0)
            total = term if total is None else total + term
        out.append(total)
    return out


def pack(rows, last, width):
    lane = lanes_of()
    out = None
    for g, row in enumerate(rows):
        moved = lane_roll(row, width * g + (width if last else 0))
        out = moved if out is None else jnp.where(lane >= width * g, moved, out)
    return out


def halo_tile(from_left, from_right, n, width):
    count = 32 // width
    left, right = from_left[n // count].astype(F32), from_right[n // count].astype(F32)
    shift = 4 * width * (n % count)
    left, right = lane_roll(left, 64 - shift), lane_roll(right, -shift)
    lane = lanes_of()
    if width == 16:
        return jnp.where(lane < 64, right, left)
    both = jnp.where(lane < 64, right, left)
    return jnp.where(lane % 64 < 4 * width, both, 0.0)


def turn(tiles):
    group = lanes_of() // 8
    tiles = list(tiles)
    for bit in range(4):
        step = 1 << bit
        high = (group & step) != 0
        for p in range(16):
            if p & step:
                continue
            x, y = tiles[p], tiles[p | step]
            tiles[p] = jnp.where(high, lane_roll(y, 8 * step), x)
            tiles[p | step] = jnp.where(high, y, lane_roll(x, -8 * step))
    return tiles


def column(ref, c, az, sector):
    return ref[c, pl.ds(az, 8, stride=sector), :]


def first_kernel(sector, u_far, lm_far, low, high, u, lm, arrived):
    copies = [pltpu.make_async_copy(a, b, arrived.at[n]) for n, (a, b) in enumerate([(u_far, u), (lm_far, lm)])]
    for copy in copies:
        copy.start()
    for copy in copies:
        copy.wait()
    for c in range(3):
        for i in range(4):
            low[4 * c + i] = column(u, c, i, sector)
            high[4 * c + i] = column(u, c, sector - 4 + i, sector)
        low[12 + c] = column(lm, c, 0, sector)
        high[12 + c] = column(lm, c, sector - 1, sector)


def narrow_kernel(sector, w, m, both):
    for f in range(7):
        for az in range(sector):
            value = column(w, f, az, sector) if f < 4 else column(m, f - 4, az, sector)
            both[f * sector + az] = value.astype(BF16)


def les_pack_kernel(sector, u, lm, before, after, first, last):
    entries = []
    for c in range(3):
        for e in range(-1, 5):
            if e < 0:
                entries.append([(before, 4 * c + i) for i in range(4)])
            elif e == 4:
                entries.append([(after, 4 * c + i) for i in range(4)])
            else:
                entries.append([(u, (c, pl.ds(4 * e + i, 8, stride=sector), slice(None))) for i in range(4)])
    for c in range(3):
        for e in range(4):
            entries.append([(lm, (c, pl.ds(4 * e + i, 8, stride=sector), slice(None))) for i in range(4)])
    for n in range(4):
        rows = [ref[at] for entry in entries[8 * n : 8 * n + 8] for ref, at in entry]
        first[n] = pack(rows, False, LES_WIDTH)
        last[n] = pack(rows, True, LES_WIDTH)


def les_element(um, ut, mm, e, weights, coef, with_flux):
    rows = [[um[c, 4 * e + i] for i in range(4)] for c in range(3)]
    tiles = [[ut[c, e]] for c in range(3)]
    prev = [um[c, 4 * e - 1] for c in range(3)]
    following = [um[c, 4 * e + 4] for c in range(3)]
    metric = [[mm[c, 4 * e + i] for i in range(4)] for c in range(3)]
    fields, halos = list(rows), list(tiles)
    if with_flux:
        fields += [[x * y for x, y in zip(rows[0], rows[c])] for c in range(3)]
        halos += [[tiles[0][0] * tiles[c][0]] for c in range(3)]
    stream = stream_main(fields, halos, weights[0], coef, LES_WIDTH)
    scaled = lambda j, values: [a * b for a, b in zip(metric[j], values)]
    slopes = [[scaled(0, stream[c]) for c in range(3)], [], []]
    fluxes = [[scaled(0, stream[3 + c]) for c in range(3)] if with_flux else [], [], []]
    for c in range(3):
        slopes[1].append(scaled(1, azimuth_main(rows[c], prev[c], following[c])))
        slopes[2].append(scaled(2, radial(rows[c], coef)))
        if with_flux:
            product = [x * y for x, y in zip(rows[1], rows[c])]
            fluxes[1].append(scaled(1, azimuth_main(product, prev[1] * prev[c], following[1] * following[c])))
            fluxes[2].append(scaled(2, radial([x * y for x, y in zip(rows[2], rows[c])], coef)))
    return rows, tiles, fields, halos, slopes, fluxes


def les_change(rows, slopes, fluxes, c, i):
    total = None
    for j in range(3):
        term = fluxes[j][c][i] + rows[j][i] * slopes[j][c][i]
        total = term if total is None else total + term
    return (0.5 * les_step) * total


def lamb_of(rows, slopes, lamb, e):
    for i in range(4):
        first = slopes[1][2][i] - slopes[2][1][i]
        second = slopes[2][0][i] - slopes[0][2][i]
        third = slopes[0][1][i] - slopes[1][0][i]
        lamb[0, 4 * e + i] = second * rows[2][i] - third * rows[1][i]
        lamb[1, 4 * e + i] = third * rows[0][i] - first * rows[2][i]
        lamb[2, 4 * e + i] = first * rows[1][i] - second * rows[0][i]


def les_kernel(sector, sends, u, lm, before, after, from_left, from_right, weights, coef, sent, um1, ut1, um, ut, mm, mt, lamb, blk):
    for c in range(3):
        for i in range(4):
            um[c, i] = before[4 * c + i]
            um[c, 4 + sector + i] = after[4 * c + i]
        mm[c, 3] = before[12 + c]
        mm[c, 4 + sector] = after[12 + c]
        for az in range(sector):
            um[c, 4 + az] = column(u, c, az, sector)
            mm[c, 4 + az] = column(lm, c, az, sector)
        for e in range(6):
            ut[c, e] = halo_tile(from_left, from_right, 6 * c + e, LES_WIDTH)
        for e in range(4):
            mt[c, e + 1] = halo_tile(from_left, from_right, 18 + 4 * c + e, LES_WIDTH)

    tiles, fields, ends = [], [], []
    for e, i in ((0, 3), (5, 0)):
        near = 4 if e == 0 else 3 + sector
        rows = [um[c, 4 * e + i] for c in range(3)]
        others = [[um[c, 4 * e + k] for k in range(4)] for c in range(3)]
        beyond = [um[c, near] for c in range(3)]
        halo = [ut[c, e] for c in range(3)]
        fields += rows + [rows[0] * rows[c] for c in range(3)]
        tiles += [(t, i) for t in halo + [halo[0] * halo[c] for c in range(3)]]
        ends.append((4 * e + i, i, rows, others, beyond))
    out = times(fields, weights[0])
    out = [y + coef[EDGE_M] * edge_main(t, i, LES_WIDTH) for y, (t, i) in zip(out, tiles)]
    for n, (at, i, rows, others, beyond) in enumerate(ends):
        metric = [mm[j, at] for j in range(3)]
        for c in range(3):
            slope = azimuth_main(others[c], beyond[c], beyond[c])[i]
            flux = azimuth_main([x * y for x, y in zip(others[1], others[c])], *[beyond[1] * beyond[c]] * 2)[i]
            total = metric[0] * (out[6 * n + 3 + c] + rows[0] * out[6 * n + c]) + metric[1] * (flux + rows[1] * slope)
            slope, flux = radial([rows[c], rows[2] * rows[c]], coef)
            total = total + metric[2] * (flux + rows[2] * slope)
            um1[c, at] = rows[c] - (0.5 * les_step) * total
        if i == 3:
            for c in range(3):
                for k in range(3):
                    um1[c, k] = rows[c]
                    um1[c, 5 + sector + k] = rows[c]

    @pl.loop(1, 5)
    def _(e):
        rows, tiles, fields, halos, slopes, fluxes = les_element(um, ut, mm, e, weights, coef, True)
        lamb_of(rows, slopes, lamb, e)
        for c in range(3):
            for i in range(4):
                um1[c, 4 * e + i] = rows[c][i] - les_change(rows, slopes, fluxes, c, i)
        low = [ut[c, e - 1] for c in range(3)]
        high = [ut[c, e + 1] for c in range(3)]
        metric = [mt[c, e] for c in range(3)]
        stream = stream_halo(fields, halos, weights[1], coef, LES_WIDTH)
        for c in range(3):
            total = metric[0] * (stream[3 + c][0] + tiles[0][0] * stream[c][0])
            slope = azimuth_halo(tiles[c], low[c], high[c], coef, LES_WIDTH)[0]
            product = tiles[1][0] * tiles[c][0]
            flux = azimuth_halo([product], low[1] * low[c], high[1] * high[c], coef, LES_WIDTH)[0]
            total = total + metric[1] * (flux + tiles[1][0] * slope)
            slope, flux = radial([tiles[c][0], tiles[2][0] * tiles[c][0]], coef)
            total = total + metric[2] * (flux + tiles[2][0] * slope)
            ut1[c, e - 1] = tiles[c][0] - (0.5 * les_step) * total

    def blocks(step):
        for c in range(3):
            tiles = turn([lamb[c, 4 + az] for az in range(sector)])
            for j in range(16):
                blk[j, 3 * step + c] = tiles[j].astype(BF16)

    blocks(0)

    @pl.loop(1, 5)
    def _(e):
        rows, _, _, _, slopes, _ = les_element(um1, Shifted(ut1), mm, e, weights, coef, False)
        lamb_of(rows, slopes, lamb, e)

    blocks(1)
    for n in range(sends.shape[0]):
        index = jnp.maximum(sends[n], 0)
        for k in range(6):
            sent[n, k] = blk[index, k]


class Shifted:
    def __init__(self, ref):
        self.ref = ref

    def __getitem__(self, at):
        return self.ref[at[0], at[1] - 1]


def les_out_kernel(sector, lm, um1, ut1, weights, coef, out, mm):
    for c in range(3):
        for az in range(sector):
            mm[c, 4 + az] = column(lm, c, az, sector)

    @pl.loop(1, 5)
    def _(e):
        rows, _, _, _, slopes, fluxes = les_element(um1, Shifted(ut1), mm, e, weights, coef, True)
        for c in range(3):
            for i in range(4):
                out[c, pl.ds(4 * (e - 1) + i, 8, stride=sector), :] = rows[c][i] - les_change(rows, slopes, fluxes, c, i)


def blend_kernel(sector, refs, offsets, got, own, up, down, mixed):
    for j in range(16):
        a = jnp.clip(refs[4 * j] * 2 + refs[4 * j + 1], 0, got.shape[0] - 1)
        b = jnp.clip(refs[4 * j + 2] * 2 + refs[4 * j + 3], 0, got.shape[0] - 1)
        fraction = offsets[j].astype(F32)
        for k in range(6):
            blend = (8.0 - fraction) * got[a, k].astype(F32) + fraction * got[b, k].astype(F32)
            mixed[k, j] = blend * 0.125
    for step in range(2):
        for c in range(3):
            tiles = turn([mixed[3 * step + c, j] for j in range(16)])
            for az in range(sector):
                own[step, c, az] = tiles[az]
                narrow = tiles[az].astype(BF16)
                if step == 0:
                    up[c * 16 + az] = narrow
                    down[c * 16 + az] = narrow
                elif az >= 8:
                    up[48 + c * 8 + az - 8] = narrow
                else:
                    down[48 + c * 8 + az] = narrow


def pack_entries(entries, first, last):
    for n in range(len(entries) // 2):
        rows = [ref[at].astype(F32) for ref, at in entries[2 * n] + entries[2 * n + 1]]
        first[n] = pack(rows, False, CAA_WIDTH).astype(BF16)
        last[n] = pack(rows, True, CAA_WIDTH).astype(BF16)


def state_pack_kernel(sector, below, above, both, first, last):
    entries = []
    for f in range(7):
        for e in range(12):
            ref = (below, both, above)[e // 4]
            entries.append([(ref, f * sector + 4 * (e % 4) + i) for i in range(4)])
    pack_entries(entries, first, last)


def source_pack_kernel(sector, own, below, above, first, last):
    entries = []
    for c in range(3):
        for e in range(12):
            if 4 <= e < 8:
                entries.append([(own, (0, c, 4 * (e - 4) + i)) for i in range(4)])
            else:
                entries.append([(below if e < 4 else above, c * 16 + 4 * (e % 4) + i) for i in range(4)])
    for c in range(3):
        for e in range(2, 10):
            if 4 <= e < 8:
                entries.append([(own, (1, c, 4 * (e - 4) + i)) for i in range(4)])
            elif e < 4:
                entries.append([(below, 48 + c * 8 + 4 * (e - 2) + i) for i in range(4)])
            else:
                entries.append([(above, 48 + c * 8 + 4 * (e - 8) + i) for i in range(4)])
    pack_entries(entries, first, last)


CAA_RANGES = ((0, 12), (1, 11), (1, 11), (2, 10), (2, 10), (3, 9), (3, 9), (4, 8))


def caa_kernel(
    sector, w, m, own, below, above, caa_below, caa_above, state_left, state_right, from_left, from_right, weights, coef,
    out, wm, wt, mm, mt, sm, st,
):
    w_main, w_halo = weights[0], weights[1]

    for f in range(7):
        for az in range(3 * sector):
            if az < sector:
                value = caa_below[f * sector + az].astype(F32)
            elif az < 2 * sector:
                value = column(w, f, az - sector, sector) if f < 4 else column(m, f - 4, az - sector, sector)
            else:
                value = caa_above[f * sector + az - 2 * sector].astype(F32)
            if f < 4:
                wm[0, f, az] = value
            else:
                mm[f - 4, az] = value * caa_step
        for e in range(12):
            value = halo_tile(state_left, state_right, 12 * f + e, CAA_WIDTH)
            if f < 4:
                wt[0, f, e] = value
            else:
                mt[f - 4, e] = value * caa_step
    for c in range(3):
        for az in range(16):
            sm[0, c, az] = below[c * 16 + az].astype(F32) * caa_step
            sm[0, c, 16 + az] = own[0, c, az] * caa_step
            sm[0, c, 32 + az] = above[c * 16 + az].astype(F32) * caa_step
            sm[1, c, 16 + az] = own[1, c, az] * caa_step
        for az in range(8):
            sm[1, c, 8 + az] = below[48 + c * 8 + az].astype(F32) * caa_step
            sm[1, c, 32 + az] = above[48 + c * 8 + az].astype(F32) * caa_step
        for e in range(12):
            st[0, c, e] = halo_tile(from_left, from_right, 12 * c + e, CAA_WIDTH) * caa_step
        for e in range(8):
            st[1, c, 2 + e] = halo_tile(from_left, from_right, 36 + 8 * c + e, CAA_WIDTH) * caa_step

    def pair(now, source, e, final):
        rows = [[wm[now, f, 4 * e + i] for i in range(8)] for f in range(4)]
        tiles = [[wt[now, f, e + n] for n in range(2)] for f in range(4)]
        below, above = jnp.maximum(4 * e - 1, 0), jnp.minimum(4 * e + 8, 47)
        tile_below, tile_above = jnp.maximum(e - 1, 0), jnp.minimum(e + 2, 11)

        def rates(values, metric, sources, stream, around, up):
            p, v0, v1, v2 = values
            count = len(p)
            azimuth_p, azimuth_v = around
            radial_p, radial_v = up
            for n in range(count):
                m0, m1, m2 = metric[0](n), metric[1](n), metric[2](n)
                half = mach_number * m0
                yield (
                    n,
                    p[n] - m0 * stream[0][n] - m1 * azimuth_v[n] - m2 * radial_v[n],
                    v0[n] - m0 * stream[1][n] + sources[0](n),
                    v1[n] - half * stream[2][n] - m1 * azimuth_p[n] + sources[1](n),
                    v2[n] - half * stream[3][n] - m2 * radial_p[n] + sources[2](n),
                )

        def mixed(values):
            p, v0, v1, v2 = values
            return [
                [mach_number * a + b for a, b in zip(p, v0)],
                [mach_number * b + a for a, b in zip(p, v0)],
                v1,
                v2,
            ]

        fields, halos = mixed(rows), mixed(tiles)
        stream = stream_main(fields, halos, w_main, coef, CAA_WIDTH)
        around = [azimuth_main(rows[f], wm[now, f, below], wm[now, f, above]) for f in (0, 2)]
        up = [radial(rows[f], coef) for f in (0, 3)]
        metric = [lambda n, c=c: mm[c, 4 * e + n] for c in range(3)]
        sources = [lambda n, c=c: sm[source, c, 4 * e + n] for c in range(3)]
        for n, *values in rates(rows, metric, sources, stream, around, up):
            for f in range(4):
                if final:
                    out[f, pl.ds(4 * e + n - 16, 8, stride=sector), :] = values[f]
                else:
                    wm[1 - now, f, 4 * e + n] = values[f]
        if not final:
            stream = stream_halo(fields, halos, w_halo, coef, CAA_WIDTH)
            around = [azimuth_halo(tiles[f], wt[now, f, tile_below], wt[now, f, tile_above], coef, CAA_WIDTH) for f in (0, 2)]
            up = [radial(tiles[f], coef) for f in (0, 3)]
            metric = [lambda n, c=c: mt[c, e + n] for c in range(3)]
            sources = [lambda n, c=c: st[source, c, e + n] for c in range(3)]
            for n, *values in rates(tiles, metric, sources, stream, around, up):
                for f in range(4):
                    wt[1 - now, f, e + n] = values[f]

    for step, (start, stop) in enumerate(CAA_RANGES):

        @pl.loop(0, (stop - start) // 2)
        def _(n):
            pair(step % 2, step // 4, start + 2 * n, step == 7)


def call(kernel, name, outs, *args, smem=0, far=0, scratch=()):
    whole = pl.BlockSpec(memory_space=pltpu.VMEM)
    specs = [pl.BlockSpec(memory_space=pltpu.SMEM)] * smem + [pl.BlockSpec(memory_space=pltpu.HBM)] * far
    return pl.pallas_call(
        kernel,
        name=name,
        out_shape=[jax.ShapeDtypeStruct(shape, dtype) for shape, dtype in outs],
        in_specs=specs + [whole] * (len(args) - smem - far),
        out_specs=[whole] * len(outs),
        scratch_shapes=list(scratch),
        compiler_params=pltpu.CompilerParams(vmem_limit_bytes=None if far else VMEM_LIMIT),
    )(*args)


def both_ways(low, high, axis, closed):
    count = lax.axis_size(axis)
    ends = count if closed else count - 1
    below = lax.ppermute(high, axis, [(i, (i + 1) % count) for i in range(ends)])
    above = lax.ppermute(low, axis, [((i + 1) % count, i) for i in range(ends)])
    return below, above


def body(les_velocity, les_metric, caa_state, caa_metric, intersection_refs, offsets, send_list):
    _, radial_nodes, sector, length = les_velocity.shape
    slabs = lax.axis_size("gx")
    assert (radial_nodes, sector, length) == (8, 16, 128)
    lines = radial_nodes * sector
    u, lm, w, m = (x.reshape(-1, lines, length) for x in (les_velocity, les_metric, caa_state, caa_metric))
    les_weights = jnp.asarray(np.stack([split_matrix(128), split_matrix(LES_WIDTH)]))
    caa_weights = jnp.asarray(np.stack([split_matrix(128), split_matrix(CAA_WIDTH)]))
    les_coef, caa_coef = jnp.asarray(coefficients(LES_WIDTH)), jnp.asarray(coefficients(CAA_WIDTH))
    own_row = lax.axis_index("sec") * slabs + lax.axis_index("gx")
    sends = lax.dynamic_slice_in_dim(send_list, own_row, 1, axis=0).reshape(-1)
    tile = (8, 128)
    vmem = lambda *shape, dtype=F32: pltpu.VMEM((*shape, *tile), dtype)

    low, high = call(
        functools.partial(first_kernel, sector),
        "first",
        [((15, *tile), F32)] * 2,
        u, lm,
        far=2,
        scratch=[pltpu.VMEM(u.shape, F32), pltpu.VMEM(lm.shape, F32), pltpu.SemaphoreType.DMA((2,))],
    )
    before, after = both_ways(low, high, "az", True)
    first, last = call(
        functools.partial(les_pack_kernel, sector),
        "les_pack",
        [((4, *tile), F32)] * 2,
        u, lm, before, after,
    )
    from_left, from_right = both_ways(first, last, STREAM, False)
    sent, um1, ut1 = call(
        functools.partial(les_kernel, sector),
        "les",
        [((slabs * 2, 6, *tile), BF16), ((3, 24, *tile), F32), ((3, 4, *tile), F32)],
        sends, u, lm, before, after, from_left, from_right, les_weights, les_coef,
        smem=1,
        scratch=[vmem(3, 24), vmem(3, 6), vmem(3, 24), vmem(3, 6), vmem(3, 24), vmem(16, 6, dtype=BF16)],
    )
    got = lax.all_to_all(sent.reshape(slabs, 96, 128), "gx", 0, 0, tiled=True).reshape(slabs * 2, 6, *tile)

    (both,) = call(functools.partial(narrow_kernel, sector), "narrow", [((7 * sector, *tile), BF16)], w, m)
    caa_below, caa_above = both_ways(both, both, "az", True)
    (les_out,) = call(
        functools.partial(les_out_kernel, sector),
        "les_out",
        [((3, lines, length), F32)],
        lm, um1, ut1, les_weights, les_coef,
        scratch=[vmem(3, 24)],
    )
    first, last = call(
        functools.partial(state_pack_kernel, sector),
        "state_pack",
        [((42, *tile), BF16)] * 2,
        caa_below, caa_above, both,
    )
    state_left, state_right = both_ways(first, last, STREAM, False)
    got, state_left, state_right, les_out = lax.optimization_barrier((got, state_left, state_right, les_out))

    own, up, down = call(
        functools.partial(blend_kernel, sector),
        "blend",
        [((2, 3, sector, *tile), F32), ((72, *tile), BF16), ((72, *tile), BF16)],
        intersection_refs.reshape(-1), offsets, got,
        smem=2,
        scratch=[vmem(6, 16)],
    )
    below, above = both_ways(down, up, "az", True)
    first, last = call(
        functools.partial(source_pack_kernel, sector),
        "source_pack",
        [((30, *tile), BF16)] * 2,
        own, below, above,
    )
    from_left, from_right = both_ways(first, last, STREAM, False)
    (caa_out,) = call(
        functools.partial(caa_kernel, sector),
        "caa",
        [((4, lines, length), F32)],
        w, m, own, below, above, caa_below, caa_above, state_left, state_right, from_left, from_right, caa_weights, caa_coef,
        scratch=[vmem(2, 4, 48), vmem(2, 4, 12), vmem(3, 48), vmem(3, 12), vmem(2, 3, 48), vmem(2, 3, 12)],
    )
    return les_out.reshape(les_velocity.shape), caa_out.reshape(caa_state.shape)


def solution(mesh):
    field = P(None, None, "az", STREAM)
    in_specs = (field, field, field, field, P(STREAM, None), P(STREAM), P())
    return jax.shard_map(body, mesh=mesh, in_specs=in_specs, out_specs=(field, field), check_vma=False)
```

```python
import functools

import jax
import jax.numpy as jnp
import numpy as np
from jax import lax
from jax.experimental import pallas as pl
from jax.experimental.pallas import tpu as pltpu
from jax.sharding import PartitionSpec as P


les_step = 0.02
caa_step = 0.01
mach_number = 0.5

STREAM = ("sec", "gx")
F32 = jnp.float32
BF16 = jnp.bfloat16
VMEM_LIMIT = 24 * 1024 * 1024


def slope_table():
    points = np.array([-1.0, -(0.2**0.5), 0.2**0.5, 1.0])
    identity = np.eye(4)
    differences = points[:, None] - points[None, :] + identity
    inverse_weights = 1.0 / np.prod(differences, axis=1)
    slope_matrix = inverse_weights[None, :] / inverse_weights[:, None] / differences
    slope_matrix = slope_matrix * (1.0 - identity)
    return slope_matrix - identity * slope_matrix.sum(axis=1)[:, None]


DM = slope_table() + np.diag([3.0, 0.0, 0.0, -3.0])
DM[np.abs(DM) < 1e-12] = 0.0


def lane_matrix(run):
    result = np.zeros((128, 128))
    for e in range(32):
        result[4 * e : 4 * e + 4, 4 * e : 4 * e + 4] = DM.T
        if (4 * e) % run:
            result[4 * e - 1, 4 * e] = -3.0
        if (4 * e + 4) % run:
            result[4 * e + 4, 4 * e + 3] = 3.0
    return result


def split_matrix(run):
    full = lane_matrix(run).astype(np.float32)
    high = full.astype(jnp.bfloat16)
    low = (full - high.astype(np.float32)).astype(jnp.bfloat16)
    return np.block([[high, low], [high, np.zeros_like(low)]])


OFFSETS = (-3, -2, -1, 1, 2, 3)
RAD, AZT, AZP, AZN, EDGE_M, EDGE_T = 0, 6, 12, 13, 14, 15
LES_WIDTH, CAA_WIDTH = 4, 16


def coefficients(width):
    c = np.zeros((16, 8, 128), np.float32)
    for n, k in enumerate(OFFSETS):
        for s in range(8):
            i = s % 4
            if 0 <= i + k <= 3:
                c[RAD + n, s, :] = DM[i, i + k]
        for lane in range(128):
            i = (lane % 64) // width
            if i <= 3 and 0 <= i + k <= 3:
                c[AZT + n, :, lane] = DM[i, i + k]
    c[RAD + OFFSETS.index(1), 3, :] = 3.0
    c[RAD + OFFSETS.index(-1), 4, :] = -3.0
    for lane in range(128):
        i = (lane % 64) // width
        if i == 0:
            c[AZP, :, lane] = -3.0
        if i == 3:
            c[AZN, :, lane] = 3.0
    c[EDGE_M, :, 127] = 3.0
    c[EDGE_M, :, 0] = -3.0
    for i in range(4):
        c[EDGE_T, :, width * i] = -3.0
        c[EDGE_T, :, 63 + width * (i + 1)] = 3.0
    return c


WHOLE_T, WHOLE_P, WHOLE_N = 0, 6, 7


def acoustic_coefficients():
    c = np.zeros((10, 8, 128), np.float32)
    for lane in range(128):
        i = lane // 32
        for n, k in enumerate(OFFSETS):
            if 0 <= i + k <= 3:
                c[WHOLE_T + n, :, lane] = DM[i, i + k]
        if i == 0:
            c[WHOLE_P, :, lane] = -3.0
        if i == 3:
            c[WHOLE_N, :, lane] = 3.0
    c[8, :, 127], c[8, :, 0] = 3.0, -3.0
    for i in range(4):
        c[9, :, 32 * i + 15], c[9, :, 32 * i + 16] = -3.0, 3.0
    return c


def two_terms(full):
    full = full.astype(np.float32)
    high = full.astype(jnp.bfloat16)
    return high, (full - high.astype(np.float32)).astype(jnp.bfloat16)


def acoustic_weights():
    natural = lane_matrix(16)
    lane = np.arange(128)
    reverse = 16 * (lane // 16) + 15 - lane % 16
    return np.stack([np.concatenate(two_terms(full), axis=1) for full in (lane_matrix(128), natural[np.ix_(reverse, reverse)])])


def radial_matrix(count):
    block = np.zeros((8, 8))
    block[:4, :4] = block[4:, 4:] = DM
    block[3, 4], block[4, 3] = 3.0, -3.0
    return np.concatenate(two_terms(np.kron(np.eye(count), block)), axis=0)


def halo_order():
    order = np.zeros((2, 128, 128), np.float32)
    for lane in range(128):
        i, half, k = lane // 32, (lane // 16) % 2, 15 - lane % 16
        order[0, 64 * half + 16 * i + k, lane] = 1.0
        order[1, 64 * (1 - half) + 16 * i + k, lane] = 1.0
    return order.astype(jnp.bfloat16)


def lanes_of():
    return lax.broadcasted_iota(jnp.int32, (8, 128), 1)


def lane_roll(x, shift):
    shift %= 128
    return pltpu.roll(x, shift, axis=1) if shift else x


def times(rows, weights):
    x = jnp.concatenate(rows, axis=0)
    high = x.astype(BF16)
    low = (x - high.astype(F32)).astype(BF16)
    y = jnp.dot(jnp.concatenate([high, low], axis=1), weights, preferred_element_type=F32)
    y = y[:, :128] + y[:, 128:]
    return [y[8 * n : 8 * n + 8] for n in range(len(rows))]


def edge_main(tile, i, width):
    return jnp.where(lanes_of() == 127, lane_roll(tile, 127 - width * i), lane_roll(tile, 65 - width * (i + 1)))


def stream_main(fields, halos, weights, coef, width):
    out = times([row for rows in fields for row in rows], weights)
    results = []
    at = 0
    for rows, tiles in zip(fields, halos):
        result = []
        for n in range(len(rows)):
            result.append(out[at] + coef[EDGE_M] * edge_main(tiles[n // 4], n % 4, width))
            at += 1
        results.append(result)
    return results


def stream_halo(fields, halos, weights, coef, width):
    lane = lanes_of()
    out = times([tile for tiles in halos for tile in tiles], weights)
    results = []
    at = 0
    for rows, tiles in zip(fields, halos):
        result = []
        for e in range(len(tiles)):
            edge = None
            for i in range(4):
                row, near, far = rows[4 * e + i], width * i, 63 + width * (i + 1)
                low, high = lane_roll(row, near + 1), lane_roll(row, far)
                edge = low if edge is None else jnp.where(lane == near, low, edge)
                edge = jnp.where(lane == far, high, edge)
            result.append(out[at] + coef[EDGE_T] * edge)
            at += 1
        results.append(result)
    return results


def azimuth_main(rows, before, after):
    out = []
    for e in range(len(rows) // 4):
        f = rows[4 * e : 4 * e + 4]
        prev = before if e == 0 else rows[4 * e - 1]
        following = after if 4 * e + 4 == len(rows) else rows[4 * e + 4]
        a, b, c = float(DM[0, 1]), float(DM[0, 2]), float(DM[0, 3])
        d, g, h = float(DM[1, 0]), float(DM[1, 2]), float(DM[1, 3])
        out.append(a * f[1] + b * f[2] + c * f[3] - 3.0 * prev)
        out.append(d * f[0] + g * f[2] + h * f[3])
        out.append(-(h * f[0] + g * f[1] + d * f[3]))
        out.append(3.0 * following - (c * f[0] + b * f[1] + a * f[2]))
    return out


def azimuth_halo(tiles, before, after, coef, width):
    out = []
    for e, tile in enumerate(tiles):
        prev = before if e == 0 else tiles[e - 1]
        following = after if e + 1 == len(tiles) else tiles[e + 1]
        total = coef[AZP] * lane_roll(prev, -3 * width) + coef[AZN] * lane_roll(following, 3 * width)
        for n, k in enumerate(OFFSETS):
            total = total + coef[AZT + n] * lane_roll(tile, -width * k)
        out.append(total)
    return out


def radial(tiles, coef):
    out = []
    for tile in tiles:
        total = None
        for n, k in enumerate(OFFSETS):
            term = coef[RAD + n] * pltpu.roll(tile, (-k) % 8, axis=0)
            total = term if total is None else total + term
        out.append(total)
    return out


def pack(rows, last, width):
    lane = lanes_of()
    out = None
    for g, row in enumerate(rows):
        moved = lane_roll(row, width * g + (width if last else 0))
        out = moved if out is None else jnp.where(lane >= width * g, moved, out)
    return out


def halo_tile(from_left, from_right, n, width):
    count = 32 // width
    left, right = from_left[n // count].astype(F32), from_right[n // count].astype(F32)
    shift = 4 * width * (n % count)
    left, right = lane_roll(left, 64 - shift), lane_roll(right, -shift)
    lane = lanes_of()
    both = jnp.where(lane < 64, right, left)
    return jnp.where(lane % 64 < 4 * width, both, 0.0)


def acoustic_tile(from_left, from_right, n):
    left, right = from_left[n // 2].astype(F32), from_right[n // 2].astype(F32)
    if n % 2:
        left, right = lane_roll(left, 16), lane_roll(right, -16)
    return jnp.where(lanes_of() % 32 < 16, right, left)


def turn(tiles):
    group = lanes_of() // 8
    tiles = list(tiles)
    for bit in range(4):
        step = 1 << bit
        high = (group & step) != 0
        for p in range(16):
            if p & step:
                continue
            x, y = tiles[p], tiles[p | step]
            tiles[p] = jnp.where(high, lane_roll(y, 8 * step), x)
            tiles[p | step] = jnp.where(high, y, lane_roll(x, -8 * step))
    return tiles


def column(ref, c, az, sector):
    return ref[c, pl.ds(az, 8, stride=sector), :]


def first_kernel(sector, u_far, lm_far, low, high, u, lm, arrived):
    copies = [pltpu.make_async_copy(a, b, arrived.at[n]) for n, (a, b) in enumerate([(u_far, u), (lm_far, lm)])]
    for copy in copies:
        copy.start()
    for copy in copies:
        copy.wait()
    for c in range(3):
        for i in range(4):
            low[4 * c + i] = column(u, c, i, sector)
            high[4 * c + i] = column(u, c, sector - 4 + i, sector)
        low[12 + c] = column(lm, c, 0, sector)
        high[12 + c] = column(lm, c, sector - 1, sector)


def narrow_kernel(sector, w, m, both):
    for f in range(7):
        for az in range(sector):
            value = column(w, f, az, sector) if f < 4 else column(m, f - 4, az, sector)
            both[f * sector + az] = value.astype(BF16)


def les_pack_kernel(sector, u, lm, before, after, first, last):
    entries = []
    for c in range(3):
        for e in range(-1, 5):
            if e < 0:
                entries.append([(before, 4 * c + i) for i in range(4)])
            elif e == 4:
                entries.append([(after, 4 * c + i) for i in range(4)])
            else:
                entries.append([(u, (c, pl.ds(4 * e + i, 8, stride=sector), slice(None))) for i in range(4)])
    for c in range(3):
        for e in range(4):
            entries.append([(lm, (c, pl.ds(4 * e + i, 8, stride=sector), slice(None))) for i in range(4)])
    for n in range(4):
        rows = [ref[at] for entry in entries[8 * n : 8 * n + 8] for ref, at in entry]
        first[n] = pack(rows, False, LES_WIDTH)
        last[n] = pack(rows, True, LES_WIDTH)


def les_element(um, ut, mm, e, weights, coef, with_flux):
    rows = [[um[c, 4 * e + i] for i in range(4)] for c in range(3)]
    tiles = [[ut[c, e]] for c in range(3)]
    prev = [um[c, 4 * e - 1] for c in range(3)]
    following = [um[c, 4 * e + 4] for c in range(3)]
    metric = [[mm[c, 4 * e + i] for i in range(4)] for c in range(3)]
    fields, halos = list(rows), list(tiles)
    if with_flux:
        fields += [[x * y for x, y in zip(rows[0], rows[c])] for c in range(3)]
        halos += [[tiles[0][0] * tiles[c][0]] for c in range(3)]
    stream = stream_main(fields, halos, weights[0], coef, LES_WIDTH)
    scaled = lambda j, values: [a * b for a, b in zip(metric[j], values)]
    slopes = [[scaled(0, stream[c]) for c in range(3)], [], []]
    fluxes = [[scaled(0, stream[3 + c]) for c in range(3)] if with_flux else [], [], []]
    for c in range(3):
        slopes[1].append(scaled(1, azimuth_main(rows[c], prev[c], following[c])))
        slopes[2].append(scaled(2, radial(rows[c], coef)))
        if with_flux:
            product = [x * y for x, y in zip(rows[1], rows[c])]
            fluxes[1].append(scaled(1, azimuth_main(product, prev[1] * prev[c], following[1] * following[c])))
            fluxes[2].append(scaled(2, radial([x * y for x, y in zip(rows[2], rows[c])], coef)))
    return rows, tiles, fields, halos, slopes, fluxes


def les_change(rows, slopes, fluxes, c, i):
    total = None
    for j in range(3):
        term = fluxes[j][c][i] + rows[j][i] * slopes[j][c][i]
        total = term if total is None else total + term
    return (0.5 * les_step) * total


def lamb_of(rows, slopes, lamb, e):
    for i in range(4):
        first = slopes[1][2][i] - slopes[2][1][i]
        second = slopes[2][0][i] - slopes[0][2][i]
        third = slopes[0][1][i] - slopes[1][0][i]
        lamb[0, 4 * e + i] = second * rows[2][i] - third * rows[1][i]
        lamb[1, 4 * e + i] = third * rows[0][i] - first * rows[2][i]
        lamb[2, 4 * e + i] = first * rows[1][i] - second * rows[0][i]


def les_kernel(sector, sends, u, lm, before, after, from_left, from_right, weights, coef, sent, um1, ut1, um, ut, mm, mt, lamb, blk):
    for c in range(3):
        for i in range(4):
            um[c, i] = before[4 * c + i]
            um[c, 4 + sector + i] = after[4 * c + i]
        mm[c, 3] = before[12 + c]
        mm[c, 4 + sector] = after[12 + c]
        for az in range(sector):
            um[c, 4 + az] = column(u, c, az, sector)
            mm[c, 4 + az] = column(lm, c, az, sector)
        for e in range(6):
            ut[c, e] = halo_tile(from_left, from_right, 6 * c + e, LES_WIDTH)
        for e in range(4):
            mt[c, e + 1] = halo_tile(from_left, from_right, 18 + 4 * c + e, LES_WIDTH)

    tiles, fields, ends = [], [], []
    for e, i in ((0, 3), (5, 0)):
        near = 4 if e == 0 else 3 + sector
        rows = [um[c, 4 * e + i] for c in range(3)]
        others = [[um[c, 4 * e + k] for k in range(4)] for c in range(3)]
        beyond = [um[c, near] for c in range(3)]
        halo = [ut[c, e] for c in range(3)]
        fields += rows + [rows[0] * rows[c] for c in range(3)]
        tiles += [(t, i) for t in halo + [halo[0] * halo[c] for c in range(3)]]
        ends.append((4 * e + i, i, rows, others, beyond))
    out = times(fields, weights[0])
    out = [y + coef[EDGE_M] * edge_main(t, i, LES_WIDTH) for y, (t, i) in zip(out, tiles)]
    for n, (at, i, rows, others, beyond) in enumerate(ends):
        metric = [mm[j, at] for j in range(3)]
        for c in range(3):
            slope = azimuth_main(others[c], beyond[c], beyond[c])[i]
            flux = azimuth_main([x * y for x, y in zip(others[1], others[c])], *[beyond[1] * beyond[c]] * 2)[i]
            total = metric[0] * (out[6 * n + 3 + c] + rows[0] * out[6 * n + c]) + metric[1] * (flux + rows[1] * slope)
            slope, flux = radial([rows[c], rows[2] * rows[c]], coef)
            total = total + metric[2] * (flux + rows[2] * slope)
            um1[c, at] = rows[c] - (0.5 * les_step) * total
        if i == 3:
            for c in range(3):
                for k in range(3):
                    um1[c, k] = rows[c]
                    um1[c, 5 + sector + k] = rows[c]

    for e in range(1, 5):
        rows, tiles, fields, halos, slopes, fluxes = les_element(um, ut, mm, e, weights, coef, True)
        lamb_of(rows, slopes, lamb, e)
        for c in range(3):
            for i in range(4):
                um1[c, 4 * e + i] = rows[c][i] - les_change(rows, slopes, fluxes, c, i)
        low = [ut[c, e - 1] for c in range(3)]
        high = [ut[c, e + 1] for c in range(3)]
        metric = [mt[c, e] for c in range(3)]
        stream = stream_halo(fields, halos, weights[1], coef, LES_WIDTH)
        for c in range(3):
            total = metric[0] * (stream[3 + c][0] + tiles[0][0] * stream[c][0])
            slope = azimuth_halo(tiles[c], low[c], high[c], coef, LES_WIDTH)[0]
            product = tiles[1][0] * tiles[c][0]
            flux = azimuth_halo([product], low[1] * low[c], high[1] * high[c], coef, LES_WIDTH)[0]
            total = total + metric[1] * (flux + tiles[1][0] * slope)
            slope, flux = radial([tiles[c][0], tiles[2][0] * tiles[c][0]], coef)
            total = total + metric[2] * (flux + tiles[2][0] * slope)
            ut1[c, e - 1] = tiles[c][0] - (0.5 * les_step) * total

    def blocks(step):
        for c in range(3):
            tiles = turn([lamb[c, 4 + az] for az in range(sector)])
            for j in range(16):
                blk[j, 3 * step + c] = tiles[j].astype(BF16)

    blocks(0)

    for e in range(1, 5):
        rows, _, _, _, slopes, _ = les_element(um1, Shifted(ut1), mm, e, weights, coef, False)
        lamb_of(rows, slopes, lamb, e)

    blocks(1)
    for n in range(sends.shape[0]):
        index = jnp.maximum(sends[n], 0)
        for k in range(6):
            sent[n, k] = blk[index, k]


class Shifted:
    def __init__(self, ref):
        self.ref = ref

    def __getitem__(self, at):
        return self.ref[at[0], at[1] - 1]


def les_out_kernel(sector, lm, um1, ut1, weights, coef, out, mm):
    for c in range(3):
        for az in range(sector):
            mm[c, 4 + az] = column(lm, c, az, sector)

    @pl.loop(1, 5)
    def _(e):
        rows, _, _, _, slopes, fluxes = les_element(um1, Shifted(ut1), mm, e, weights, coef, True)
        for c in range(3):
            for i in range(4):
                out[c, pl.ds(4 * (e - 1) + i, 8, stride=sector), :] = rows[c][i] - les_change(rows, slopes, fluxes, c, i)


def blend_kernel(sector, refs, got, own, up, down, mixed):
    for j in range(16):
        a = jnp.clip(refs[4 * j] * 2 + refs[4 * j + 1], 0, got.shape[0] - 1)
        b = jnp.clip(refs[4 * j + 2] * 2 + refs[4 * j + 3], 0, got.shape[0] - 1)
        fraction = refs[64 + j].astype(F32)
        for k in range(6):
            blend = (8.0 - fraction) * got[a, k].astype(F32) + fraction * got[b, k].astype(F32)
            mixed[k, j] = blend * 0.125
    for step in range(2):
        for c in range(3):
            tiles = turn([mixed[3 * step + c, j] for j in range(16)])
            for az in range(sector):
                own[step, c, az] = tiles[az]
                narrow = tiles[az].astype(BF16)
                if step == 0:
                    up[c * 16 + az] = narrow
                    down[c * 16 + az] = narrow
                elif az >= 8:
                    up[48 + c * 8 + az - 8] = narrow
                else:
                    down[48 + c * 8 + az] = narrow


def pack_entries(entries, order, first, last):
    for way, to in enumerate((first, last)):
        tiles = []
        for n in range(len(entries) // 2):
            rows = [ref[at].astype(F32) for ref, at in entries[2 * n] + entries[2 * n + 1]]
            tiles.append(pack(rows, way == 1, CAA_WIDTH))
        x = jnp.concatenate(tiles, axis=0).astype(BF16)
        y = jnp.dot(x, order[way], preferred_element_type=F32)
        for n in range(len(tiles)):
            to[n] = y[8 * n : 8 * n + 8].astype(BF16)


def state_pack_kernel(sector, below, above, both, order, first, last):
    entries = []
    for f in range(7):
        for e in range(12):
            ref = (below, both, above)[e // 4]
            entries.append([(ref, f * sector + 4 * (e % 4) + i) for i in range(4)])
    pack_entries(entries, order, first, last)


def source_pack_kernel(sector, own, below, above, order, first, last):
    entries = []
    for c in range(3):
        for e in range(12):
            if 4 <= e < 8:
                entries.append([(own, (0, c, 4 * (e - 4) + i)) for i in range(4)])
            else:
                entries.append([(below if e < 4 else above, c * 16 + 4 * (e % 4) + i) for i in range(4)])
    for c in range(3):
        for e in range(2, 10):
            if 4 <= e < 8:
                entries.append([(own, (1, c, 4 * (e - 4) + i)) for i in range(4)])
            elif e < 4:
                entries.append([(below, 48 + c * 8 + 4 * (e - 2) + i) for i in range(4)])
            else:
                entries.append([(above, 48 + c * 8 + 4 * (e - 8) + i) for i in range(4)])
    pack_entries(entries, order, first, last)


CAA_RANGES = ((0, 12), (1, 11), (1, 11), (2, 10), (2, 10), (3, 9), (3, 9), (4, 8))


def caa_kernel(
    sector, w, m, own, below, above, caa_below, caa_above, state_left, state_right, from_left, from_right, weights, coef, upward,
    out, wm, wt, mm, mt, sm, st,
):
    for f in range(7):
        for az in range(3 * sector):
            if az < sector:
                value = caa_below[f * sector + az].astype(F32)
            elif az < 2 * sector:
                value = column(w, f, az - sector, sector) if f < 4 else column(m, f - 4, az - sector, sector)
            else:
                value = caa_above[f * sector + az - 2 * sector].astype(F32)
            if f < 4:
                wm[0, f, az] = value
            else:
                mm[f - 4, az] = value * caa_step
        for e in range(12):
            value = acoustic_tile(state_left, state_right, 12 * f + e)
            if f < 4:
                wt[0, f, e] = value
            else:
                mt[f - 4, e] = value * caa_step
    for c in range(3):
        for az in range(16):
            sm[0, c, az] = below[c * 16 + az].astype(F32) * caa_step
            sm[0, c, 16 + az] = own[0, c, az] * caa_step
            sm[0, c, 32 + az] = above[c * 16 + az].astype(F32) * caa_step
            sm[1, c, 16 + az] = own[1, c, az] * caa_step
        for az in range(8):
            sm[1, c, 8 + az] = below[48 + c * 8 + az].astype(F32) * caa_step
            sm[1, c, 32 + az] = above[48 + c * 8 + az].astype(F32) * caa_step
        for e in range(12):
            st[0, c, e] = acoustic_tile(from_left, from_right, 12 * c + e) * caa_step
        for e in range(8):
            st[1, c, 2 + e] = acoustic_tile(from_left, from_right, 36 + 8 * c + e) * caa_step

    def along(tiles, which):
        x = jnp.concatenate(tiles, axis=0).astype(BF16)
        y = jnp.dot(x, weights[which], preferred_element_type=F32)
        y = y[:, :128] + y[:, 128:]
        return [y[8 * n : 8 * n + 8] for n in range(len(tiles))]

    def pair(now, source, e, final):
        rows = [[wm[now, f, 4 * e + i] for i in range(8)] for f in range(4)]
        tiles = [[wt[now, f, e + n] for n in range(2)] for f in range(4)]
        below, above, tile_below, tile_above = max(4 * e - 1, 0), min(4 * e + 8, 47), max(e - 1, 0), min(e + 2, 11)

        def mixed(values):
            p, v0, v1, v2 = values
            return [
                [mach_number * a + b for a, b in zip(p, v0)],
                [mach_number * b + a for a, b in zip(p, v0)],
                v1,
                v2,
            ]

        def update(values, metric, sources, stream, around, up, store):
            p, v0, v1, v2 = values
            for n in range(len(p)):
                m0, m1, m2 = metric(0, n), metric(1, n), metric(2, n)
                half = mach_number * m0
                store(0, n, p[n] - m0 * stream[0][n] - m1 * around[1][n] - m2 * up[1][n])
                store(1, n, v0[n] - m0 * stream[1][n] + sources(0, n))
                store(2, n, v1[n] - half * stream[2][n] - m1 * around[0][n] + sources(1, n))
                store(3, n, v2[n] - half * stream[3][n] - m2 * up[0][n] + sources(2, n))

        fields, halos = mixed(rows), mixed(tiles)
        x = [jnp.concatenate(rows[f] + tiles[f], axis=0).astype(BF16) for f in (0, 3)]
        y = jnp.dot(upward[...], jnp.concatenate(x, axis=1), preferred_element_type=F32)
        y = y[:80] + y[80:]
        up = [[y[8 * n : 8 * n + 8, 128 * f : 128 * f + 128] for n in range(10)] for f in range(2)]

        stream = along([row for values in fields for row in values], 0)
        stream = [[stream[8 * f + n] for n in range(8)] for f in range(4)]
        for f in range(4):
            for n in range(8):
                edge = lane_roll(halos[f][n // 4], -32 * (n % 4) - 16)
                stream[f][n] = stream[f][n] + coef[8] * edge
        around = [azimuth_main(rows[f], wm[now, f, below], wm[now, f, above]) for f in (0, 2)]

        def store(f, n, value):
            if final:
                out[f, pl.ds(4 * e + n - 16, 8, stride=sector), :] = value
            else:
                wm[1 - now, f, 4 * e + n] = value

        update(rows, lambda c, n: mm[c, 4 * e + n], lambda c, n: sm[source, c, 4 * e + n], stream, around, up, store)
        if final:
            return

        stream = along([tile for values in halos for tile in values], 1)
        stream = [[stream[2 * f + n] for n in range(2)] for f in range(4)]
        run = lanes_of() // 32
        for f in range(4):
            for n in range(2):
                edge = None
                for i in range(4):
                    moved = lane_roll(fields[f][4 * n + i], 32 * i + 16)
                    edge = moved if edge is None else jnp.where(run == i, moved, edge)
                stream[f][n] = stream[f][n] + coef[9] * edge
        around = []
        for f in (0, 2):
            values = []
            for n in range(2):
                before = wt[now, f, tile_below] if n == 0 else tiles[f][0]
                after = wt[now, f, tile_above] if n == 1 else tiles[f][1]
                total = coef[WHOLE_P] * lane_roll(before, -96) + coef[WHOLE_N] * lane_roll(after, 96)
                for k, offset in enumerate(OFFSETS):
                    total = total + coef[WHOLE_T + k] * lane_roll(tiles[f][n], -32 * offset)
                values.append(total)
            around.append(values)

        def store(f, n, value):
            wt[1 - now, f, e + n] = value

        up = [values[8:] for values in up]
        update(tiles, lambda c, n: mt[c, e + n], lambda c, n: st[source, c, e + n], stream, around, up, store)

    for step, (start, stop) in enumerate(CAA_RANGES):
        for e in range(start, stop, 2):
            pair(step % 2, step // 4, e, step == 7)


def call(kernel, name, outs, *args, smem=0, far=0, scratch=()):
    whole = pl.BlockSpec(memory_space=pltpu.VMEM)
    specs = [pl.BlockSpec(memory_space=pltpu.SMEM)] * smem + [pl.BlockSpec(memory_space=pltpu.HBM)] * far
    return pl.pallas_call(
        kernel,
        name=name,
        out_shape=[jax.ShapeDtypeStruct(shape, dtype) for shape, dtype in outs],
        in_specs=specs + [whole] * (len(args) - smem - far),
        out_specs=[whole] * len(outs),
        scratch_shapes=list(scratch),
        compiler_params=pltpu.CompilerParams(vmem_limit_bytes=None if far else VMEM_LIMIT),
    )(*args)


def both_ways(low, high, axis, closed):
    count = lax.axis_size(axis)
    ends = count if closed else count - 1
    below = lax.ppermute(high, axis, [(i, (i + 1) % count) for i in range(ends)])
    above = lax.ppermute(low, axis, [((i + 1) % count, i) for i in range(ends)])
    return below, above


def body(les_velocity, les_metric, caa_state, caa_metric, intersection_refs, offsets, send_list):
    _, radial_nodes, sector, length = les_velocity.shape
    slabs = lax.axis_size("gx")
    assert (radial_nodes, sector, length) == (8, 16, 128)
    lines = radial_nodes * sector
    u, lm, w, m = (x.reshape(-1, lines, length) for x in (les_velocity, les_metric, caa_state, caa_metric))
    les_weights = jnp.asarray(np.stack([split_matrix(128), split_matrix(LES_WIDTH)]))
    les_coef = jnp.asarray(coefficients(LES_WIDTH))
    caa_weights, caa_coef = jnp.asarray(acoustic_weights()), jnp.asarray(acoustic_coefficients())
    upward, order = jnp.asarray(radial_matrix(10)), jnp.asarray(halo_order())
    own_row = lax.axis_index("sec") * slabs + lax.axis_index("gx")
    sends = lax.dynamic_slice_in_dim(send_list, own_row, 1, axis=0).reshape(-1)
    tile = (8, 128)
    vmem = lambda *shape, dtype=F32: pltpu.VMEM((*shape, *tile), dtype)

    low, high = call(
        functools.partial(first_kernel, sector),
        "first",
        [((15, *tile), F32)] * 2,
        u, lm,
        far=2,
        scratch=[pltpu.VMEM(u.shape, F32), pltpu.VMEM(lm.shape, F32), pltpu.SemaphoreType.DMA((2,))],
    )
    before, after = both_ways(low, high, "az", True)
    first, last = call(
        functools.partial(les_pack_kernel, sector),
        "les_pack",
        [((4, *tile), F32)] * 2,
        u, lm, before, after,
    )
    from_left, from_right = both_ways(first, last, STREAM, False)
    sent, um1, ut1 = call(
        functools.partial(les_kernel, sector),
        "les",
        [((slabs * 2, 6, *tile), BF16), ((3, 24, *tile), F32), ((3, 4, *tile), F32)],
        sends, u, lm, before, after, from_left, from_right, les_weights, les_coef,
        smem=1,
        scratch=[vmem(3, 24), vmem(3, 6), vmem(3, 24), vmem(3, 6), vmem(3, 24), vmem(16, 6, dtype=BF16)],
    )
    got = lax.all_to_all(sent.reshape(slabs, 96, 128), "gx", 0, 0, tiled=True).reshape(slabs * 2, 6, *tile)

    (both,) = call(functools.partial(narrow_kernel, sector), "narrow", [((7 * sector, *tile), BF16)], w, m)
    caa_below, caa_above = both_ways(both, both, "az", True)
    (les_out,) = call(
        functools.partial(les_out_kernel, sector),
        "les_out",
        [((3, lines, length), F32)],
        lm, um1, ut1, les_weights, les_coef,
        scratch=[vmem(3, 24)],
    )
    first, last = call(
        functools.partial(state_pack_kernel, sector),
        "state_pack",
        [((42, *tile), BF16)] * 2,
        caa_below, caa_above, both, order,
    )
    state_left, state_right = both_ways(first, last, STREAM, False)
    table = jnp.concatenate([intersection_refs.reshape(-1), offsets])
    got, table, state_left, state_right, les_out = lax.optimization_barrier((got, table, state_left, state_right, les_out))

    own, up, down = call(
        functools.partial(blend_kernel, sector),
        "blend",
        [((2, 3, sector, *tile), F32), ((72, *tile), BF16), ((72, *tile), BF16)],
        table, got,
        smem=1,
        scratch=[vmem(6, 16)],
    )
    below, above = both_ways(down, up, "az", True)
    first, last = call(
        functools.partial(source_pack_kernel, sector),
        "source_pack",
        [((30, *tile), BF16)] * 2,
        own, below, above, order,
    )
    from_left, from_right = both_ways(first, last, STREAM, False)
    (caa_out,) = call(
        functools.partial(caa_kernel, sector),
        "caa",
        [((4, lines, length), F32)],
        w, m, own, below, above, caa_below, caa_above, state_left, state_right, from_left, from_right, caa_weights, caa_coef, upward,
        scratch=[vmem(2, 4, 48), vmem(2, 4, 12), vmem(3, 48), vmem(3, 12), vmem(2, 3, 48), vmem(2, 3, 12)],
    )
    return les_out.reshape(les_velocity.shape), caa_out.reshape(caa_state.shape)


def solution(mesh):
    field = P(None, None, "az", STREAM)
    in_specs = (field, field, field, field, P(STREAM, None), P(STREAM), P())
    return jax.shard_map(body, mesh=mesh, in_specs=in_specs, out_specs=(field, field), check_vma=False)
```

```python
import functools

import jax
import jax.numpy as jnp
import numpy as np
from jax import lax
from jax.experimental import pallas as pl
from jax.experimental.pallas import tpu as pltpu
from jax.sharding import PartitionSpec as P


les_step = 0.02
caa_step = 0.01
mach_number = 0.5

STREAM = ("sec", "gx")
F32 = jnp.float32
BF16 = jnp.bfloat16
VMEM_LIMIT = 24 * 1024 * 1024


def slope_table():
    points = np.array([-1.0, -(0.2**0.5), 0.2**0.5, 1.0])
    identity = np.eye(4)
    differences = points[:, None] - points[None, :] + identity
    inverse_weights = 1.0 / np.prod(differences, axis=1)
    slope_matrix = inverse_weights[None, :] / inverse_weights[:, None] / differences
    slope_matrix = slope_matrix * (1.0 - identity)
    return slope_matrix - identity * slope_matrix.sum(axis=1)[:, None]


DM = slope_table() + np.diag([3.0, 0.0, 0.0, -3.0])
DM[np.abs(DM) < 1e-12] = 0.0


def lane_matrix(run):
    result = np.zeros((128, 128))
    for e in range(32):
        result[4 * e : 4 * e + 4, 4 * e : 4 * e + 4] = DM.T
        if (4 * e) % run:
            result[4 * e - 1, 4 * e] = -3.0
        if (4 * e + 4) % run:
            result[4 * e + 4, 4 * e + 3] = 3.0
    return result


def split_matrix(run):
    full = lane_matrix(run).astype(np.float32)
    high = full.astype(jnp.bfloat16)
    low = (full - high.astype(np.float32)).astype(jnp.bfloat16)
    return np.block([[high, low], [high, np.zeros_like(low)]])


OFFSETS = (-3, -2, -1, 1, 2, 3)
RAD, AZT, AZP, AZN, EDGE_M, EDGE_T = 0, 6, 12, 13, 14, 15
LES_WIDTH, CAA_WIDTH = 4, 16


def coefficients(width):
    c = np.zeros((16, 8, 128), np.float32)
    for n, k in enumerate(OFFSETS):
        for s in range(8):
            i = s % 4
            if 0 <= i + k <= 3:
                c[RAD + n, s, :] = DM[i, i + k]
        for lane in range(128):
            i = (lane % 64) // width
            if i <= 3 and 0 <= i + k <= 3:
                c[AZT + n, :, lane] = DM[i, i + k]
    c[RAD + OFFSETS.index(1), 3, :] = 3.0
    c[RAD + OFFSETS.index(-1), 4, :] = -3.0
    for lane in range(128):
        i = (lane % 64) // width
        if i == 0:
            c[AZP, :, lane] = -3.0
        if i == 3:
            c[AZN, :, lane] = 3.0
    c[EDGE_M, :, 127] = 3.0
    c[EDGE_M, :, 0] = -3.0
    for i in range(4):
        c[EDGE_T, :, width * i] = -3.0
        c[EDGE_T, :, 63 + width * (i + 1)] = 3.0
    return c


WHOLE_T, WHOLE_P, WHOLE_N = 0, 6, 7


def acoustic_coefficients():
    c = np.zeros((10, 8, 128), np.float32)
    for lane in range(128):
        i = lane // 32
        for n, k in enumerate(OFFSETS):
            if 0 <= i + k <= 3:
                c[WHOLE_T + n, :, lane] = DM[i, i + k]
        if i == 0:
            c[WHOLE_P, :, lane] = -3.0
        if i == 3:
            c[WHOLE_N, :, lane] = 3.0
    c[8, :, 127], c[8, :, 0] = 3.0, -3.0
    for i in range(4):
        c[9, :, 32 * i + 15], c[9, :, 32 * i + 16] = -3.0, 3.0
    return c


def two_terms(full):
    full = full.astype(np.float32)
    high = full.astype(jnp.bfloat16)
    return high, (full - high.astype(np.float32)).astype(jnp.bfloat16)


def acoustic_weights():
    natural = lane_matrix(16)
    lane = np.arange(128)
    reverse = 16 * (lane // 16) + 15 - lane % 16
    return np.stack([np.concatenate(two_terms(full), axis=1) for full in (lane_matrix(128), natural[np.ix_(reverse, reverse)])])


def radial_matrix(count):
    block = np.zeros((8, 8))
    block[:4, :4] = block[4:, 4:] = DM
    block[3, 4], block[4, 3] = 3.0, -3.0
    return np.concatenate(two_terms(np.kron(np.eye(count), block)), axis=0)


def halo_order():
    order = np.zeros((2, 128, 128), np.float32)
    for lane in range(128):
        i, half, k = lane // 32, (lane // 16) % 2, 15 - lane % 16
        order[0, 64 * half + 16 * i + k, lane] = 1.0
        order[1, 64 * (1 - half) + 16 * i + k, lane] = 1.0
    return order.astype(jnp.bfloat16)


def lanes_of():
    return lax.broadcasted_iota(jnp.int32, (8, 128), 1)


def lane_roll(x, shift):
    shift %= 128
    return pltpu.roll(x, shift, axis=1) if shift else x


def times(rows, weights):
    x = jnp.concatenate(rows, axis=0)
    high = x.astype(BF16)
    low = (x - high.astype(F32)).astype(BF16)
    y = jnp.dot(jnp.concatenate([high, low], axis=1), weights, preferred_element_type=F32)
    y = y[:, :128] + y[:, 128:]
    return [y[8 * n : 8 * n + 8] for n in range(len(rows))]


def edge_main(tile, i, width):
    return jnp.where(lanes_of() == 127, lane_roll(tile, 127 - width * i), lane_roll(tile, 65 - width * (i + 1)))


def stream_main(fields, halos, weights, coef, width):
    out = times([row for rows in fields for row in rows], weights)
    results = []
    at = 0
    for rows, tiles in zip(fields, halos):
        result = []
        for n in range(len(rows)):
            result.append(out[at] + coef[EDGE_M] * edge_main(tiles[n // 4], n % 4, width))
            at += 1
        results.append(result)
    return results


def stream_halo(fields, halos, weights, coef, width):
    lane = lanes_of()
    out = times([tile for tiles in halos for tile in tiles], weights)
    results = []
    at = 0
    for rows, tiles in zip(fields, halos):
        result = []
        for e in range(len(tiles)):
            edge = None
            for i in range(4):
                row, near, far = rows[4 * e + i], width * i, 63 + width * (i + 1)
                low, high = lane_roll(row, near + 1), lane_roll(row, far)
                edge = low if edge is None else jnp.where(lane == near, low, edge)
                edge = jnp.where(lane == far, high, edge)
            result.append(out[at] + coef[EDGE_T] * edge)
            at += 1
        results.append(result)
    return results


def azimuth_main(rows, before, after):
    out = []
    for e in range(len(rows) // 4):
        f = rows[4 * e : 4 * e + 4]
        prev = before if e == 0 else rows[4 * e - 1]
        following = after if 4 * e + 4 == len(rows) else rows[4 * e + 4]
        a, b, c = float(DM[0, 1]), float(DM[0, 2]), float(DM[0, 3])
        d, g, h = float(DM[1, 0]), float(DM[1, 2]), float(DM[1, 3])
        out.append(a * f[1] + b * f[2] + c * f[3] - 3.0 * prev)
        out.append(d * f[0] + g * f[2] + h * f[3])
        out.append(-(h * f[0] + g * f[1] + d * f[3]))
        out.append(3.0 * following - (c * f[0] + b * f[1] + a * f[2]))
    return out


def azimuth_halo(tiles, before, after, coef, width):
    out = []
    for e, tile in enumerate(tiles):
        prev = before if e == 0 else tiles[e - 1]
        following = after if e + 1 == len(tiles) else tiles[e + 1]
        total = coef[AZP] * lane_roll(prev, -3 * width) + coef[AZN] * lane_roll(following, 3 * width)
        for n, k in enumerate(OFFSETS):
            total = total + coef[AZT + n] * lane_roll(tile, -width * k)
        out.append(total)
    return out


def radial(tiles, coef):
    out = []
    for tile in tiles:
        total = None
        for n, k in enumerate(OFFSETS):
            term = coef[RAD + n] * pltpu.roll(tile, (-k) % 8, axis=0)
            total = term if total is None else total + term
        out.append(total)
    return out


def pack(rows, last, width):
    lane = lanes_of()
    out = None
    for g, row in enumerate(rows):
        moved = lane_roll(row, width * g + (width if last else 0))
        out = moved if out is None else jnp.where(lane >= width * g, moved, out)
    return out


class Side:
    def __init__(self, mask, first, second):
        self.mask, self.first, self.second = mask[...] > 0.5, first, second

    def __getitem__(self, at):
        return jnp.where(self.mask, self.first[at].astype(F32), self.second[at].astype(F32))


def sides(mask, even, odd):
    return Side(mask, odd, even), Side(mask, even, odd)


def halo_tile(from_left, from_right, n, width):
    count = 32 // width
    left, right = from_left[n // count].astype(F32), from_right[n // count].astype(F32)
    shift = 4 * width * (n % count)
    left, right = lane_roll(left, 64 - shift), lane_roll(right, -shift)
    lane = lanes_of()
    both = jnp.where(lane < 64, right, left)
    return jnp.where(lane % 64 < 4 * width, both, 0.0)


def acoustic_tile(from_left, from_right, n):
    left, right = from_left[n // 2].astype(F32), from_right[n // 2].astype(F32)
    if n % 2:
        left, right = lane_roll(left, 16), lane_roll(right, -16)
    return jnp.where(lanes_of() % 32 < 16, right, left)


def turn(tiles):
    group = lanes_of() // 8
    tiles = list(tiles)
    for bit in range(4):
        step = 1 << bit
        high = (group & step) != 0
        for p in range(16):
            if p & step:
                continue
            x, y = tiles[p], tiles[p | step]
            tiles[p] = jnp.where(high, lane_roll(y, 8 * step), x)
            tiles[p | step] = jnp.where(high, y, lane_roll(x, -8 * step))
    return tiles


def column(ref, c, az, sector):
    return ref[c, pl.ds(az, 8, stride=sector), :]


def first_kernel(sector, u_far, lm_far, low, high, u, lm, arrived):
    copies = [pltpu.make_async_copy(a, b, arrived.at[n]) for n, (a, b) in enumerate([(u_far, u), (lm_far, lm)])]
    for copy in copies:
        copy.start()
    for copy in copies:
        copy.wait()
    for c in range(3):
        for i in range(4):
            low[4 * c + i] = column(u, c, i, sector)
            high[4 * c + i] = column(u, c, sector - 4 + i, sector)
        low[12 + c] = column(lm, c, 0, sector)
        high[12 + c] = column(lm, c, sector - 1, sector)


def narrow_kernel(sector, w, m, both):
    for f in range(7):
        for az in range(sector):
            value = column(w, f, az, sector) if f < 4 else column(m, f - 4, az, sector)
            both[f * sector + az] = value.astype(BF16)


def les_pack_kernel(sector, u, lm, before, after, mask, even, odd):
    right = mask[...] > 0.5
    entries = []
    for c in range(3):
        for e in range(-1, 5):
            if e < 0:
                entries.append([(before, 4 * c + i) for i in range(4)])
            elif e == 4:
                entries.append([(after, 4 * c + i) for i in range(4)])
            else:
                entries.append([(u, (c, pl.ds(4 * e + i, 8, stride=sector), slice(None))) for i in range(4)])
    for c in range(3):
        for e in range(4):
            entries.append([(lm, (c, pl.ds(4 * e + i, 8, stride=sector), slice(None))) for i in range(4)])
    for n in range(4):
        rows = [ref[at] for entry in entries[8 * n : 8 * n + 8] for ref, at in entry]
        first, last = pack(rows, False, LES_WIDTH), pack(rows, True, LES_WIDTH)
        even[n] = jnp.where(right, last, first)
        odd[n] = jnp.where(right, first, last)


def les_element(um, ut, mm, e, weights, coef, with_flux):
    rows = [[um[c, 4 * e + i] for i in range(4)] for c in range(3)]
    tiles = [[ut[c, e]] for c in range(3)]
    prev = [um[c, 4 * e - 1] for c in range(3)]
    following = [um[c, 4 * e + 4] for c in range(3)]
    metric = [[mm[c, 4 * e + i] for i in range(4)] for c in range(3)]
    fields, halos = list(rows), list(tiles)
    if with_flux:
        fields += [[x * y for x, y in zip(rows[0], rows[c])] for c in range(3)]
        halos += [[tiles[0][0] * tiles[c][0]] for c in range(3)]
    stream = stream_main(fields, halos, weights[0], coef, LES_WIDTH)
    scaled = lambda j, values: [a * b for a, b in zip(metric[j], values)]
    slopes = [[scaled(0, stream[c]) for c in range(3)], [], []]
    fluxes = [[scaled(0, stream[3 + c]) for c in range(3)] if with_flux else [], [], []]
    for c in range(3):
        slopes[1].append(scaled(1, azimuth_main(rows[c], prev[c], following[c])))
        slopes[2].append(scaled(2, radial(rows[c], coef)))
        if with_flux:
            product = [x * y for x, y in zip(rows[1], rows[c])]
            fluxes[1].append(scaled(1, azimuth_main(product, prev[1] * prev[c], following[1] * following[c])))
            fluxes[2].append(scaled(2, radial([x * y for x, y in zip(rows[2], rows[c])], coef)))
    return rows, tiles, fields, halos, slopes, fluxes


def les_change(rows, slopes, fluxes, c, i):
    total = None
    for j in range(3):
        term = fluxes[j][c][i] + rows[j][i] * slopes[j][c][i]
        total = term if total is None else total + term
    return (0.5 * les_step) * total


def lamb_of(rows, slopes, lamb, e):
    for i in range(4):
        first = slopes[1][2][i] - slopes[2][1][i]
        second = slopes[2][0][i] - slopes[0][2][i]
        third = slopes[0][1][i] - slopes[1][0][i]
        lamb[0, 4 * e + i] = second * rows[2][i] - third * rows[1][i]
        lamb[1, 4 * e + i] = third * rows[0][i] - first * rows[2][i]
        lamb[2, 4 * e + i] = first * rows[1][i] - second * rows[0][i]


def les_kernel(
    sector, sends_far, u, lm, before, after, odd, even, mask, weights, coef, sent, um1, ut1, um, ut, mm, mt, lamb, blk, sends, arrived, gone,
):
    fetch = pltpu.make_async_copy(sends_far, sends, arrived)
    fetch.start()
    from_left, from_right = sides(mask, even, odd)
    for c in range(3):
        for i in range(4):
            um[c, i] = before[4 * c + i]
            um[c, 4 + sector + i] = after[4 * c + i]
        mm[c, 3] = before[12 + c]
        mm[c, 4 + sector] = after[12 + c]
        for az in range(sector):
            um[c, 4 + az] = column(u, c, az, sector)
            mm[c, 4 + az] = column(lm, c, az, sector)
        for e in range(6):
            ut[c, e] = halo_tile(from_left, from_right, 6 * c + e, LES_WIDTH)
        for e in range(4):
            mt[c, e + 1] = halo_tile(from_left, from_right, 18 + 4 * c + e, LES_WIDTH)

    tiles, fields, ends = [], [], []
    for e, i in ((0, 3), (5, 0)):
        near = 4 if e == 0 else 3 + sector
        rows = [um[c, 4 * e + i] for c in range(3)]
        others = [[um[c, 4 * e + k] for k in range(4)] for c in range(3)]
        beyond = [um[c, near] for c in range(3)]
        halo = [ut[c, e] for c in range(3)]
        fields += rows + [rows[0] * rows[c] for c in range(3)]
        tiles += [(t, i) for t in halo + [halo[0] * halo[c] for c in range(3)]]
        ends.append((4 * e + i, i, rows, others, beyond))
    out = times(fields, weights[0])
    out = [y + coef[EDGE_M] * edge_main(t, i, LES_WIDTH) for y, (t, i) in zip(out, tiles)]
    for n, (at, i, rows, others, beyond) in enumerate(ends):
        metric = [mm[j, at] for j in range(3)]
        for c in range(3):
            slope = azimuth_main(others[c], beyond[c], beyond[c])[i]
            flux = azimuth_main([x * y for x, y in zip(others[1], others[c])], *[beyond[1] * beyond[c]] * 2)[i]
            total = metric[0] * (out[6 * n + 3 + c] + rows[0] * out[6 * n + c]) + metric[1] * (flux + rows[1] * slope)
            slope, flux = radial([rows[c], rows[2] * rows[c]], coef)
            total = total + metric[2] * (flux + rows[2] * slope)
            um1[c, at] = rows[c] - (0.5 * les_step) * total
        if i == 3:
            for c in range(3):
                for k in range(3):
                    um1[c, k] = rows[c]
                    um1[c, 5 + sector + k] = rows[c]

    for e in range(1, 5):
        rows, tiles, fields, halos, slopes, fluxes = les_element(um, ut, mm, e, weights, coef, True)
        lamb_of(rows, slopes, lamb, e)
        for c in range(3):
            for i in range(4):
                um1[c, 4 * e + i] = rows[c][i] - les_change(rows, slopes, fluxes, c, i)
        low = [ut[c, e - 1] for c in range(3)]
        high = [ut[c, e + 1] for c in range(3)]
        metric = [mt[c, e] for c in range(3)]
        stream = stream_halo(fields, halos, weights[1], coef, LES_WIDTH)
        for c in range(3):
            total = metric[0] * (stream[3 + c][0] + tiles[0][0] * stream[c][0])
            slope = azimuth_halo(tiles[c], low[c], high[c], coef, LES_WIDTH)[0]
            product = tiles[1][0] * tiles[c][0]
            flux = azimuth_halo([product], low[1] * low[c], high[1] * high[c], coef, LES_WIDTH)[0]
            total = total + metric[1] * (flux + tiles[1][0] * slope)
            slope, flux = radial([tiles[c][0], tiles[2][0] * tiles[c][0]], coef)
            total = total + metric[2] * (flux + tiles[2][0] * slope)
            ut1[c, e - 1] = tiles[c][0] - (0.5 * les_step) * total

    def blocks(step):
        for c in range(3):
            tiles = turn([lamb[c, 4 + az] for az in range(sector)])
            for j in range(16):
                blk[j, 3 * step + c] = tiles[j].astype(BF16)

    def send(step):
        part = pl.ds(3 * step, 3)
        copies = []
        for n in range(sends.shape[0]):
            index = jnp.clip(sends[n], 0, 15)
            copies.append(pltpu.make_async_copy(blk.at[index, part], sent.at[n, part], gone.at[step, n]))
            copies[-1].start()
        return copies

    blocks(0)
    fetch.wait()
    copies = send(0)

    for e in range(1, 5):
        rows, _, _, _, slopes, _ = les_element(um1, Shifted(ut1), mm, e, weights, coef, False)
        lamb_of(rows, slopes, lamb, e)

    blocks(1)
    for copy in copies + send(1):
        copy.wait()


class Shifted:
    def __init__(self, ref):
        self.ref = ref

    def __getitem__(self, at):
        return self.ref[at[0], at[1] - 1]


def les_out_kernel(sector, lm, um1, ut1, weights, coef, out, mm):
    for c in range(3):
        for az in range(sector):
            mm[c, 4 + az] = column(lm, c, az, sector)

    @pl.loop(1, 5)
    def _(e):
        rows, _, _, _, slopes, fluxes = les_element(um1, Shifted(ut1), mm, e, weights, coef, True)
        for c in range(3):
            for i in range(4):
                out[c, pl.ds(4 * (e - 1) + i, 8, stride=sector), :] = rows[c][i] - les_change(rows, slopes, fluxes, c, i)


def blend_kernel(sector, refs, got, own, up, down, mixed):
    for j in range(16):
        a = jnp.clip(refs[4 * j] * 2 + refs[4 * j + 1], 0, got.shape[0] - 1)
        b = jnp.clip(refs[4 * j + 2] * 2 + refs[4 * j + 3], 0, got.shape[0] - 1)
        fraction = refs[64 + j].astype(F32)
        for k in range(6):
            blend = (8.0 - fraction) * got[a, k].astype(F32) + fraction * got[b, k].astype(F32)
            mixed[k, j] = blend * 0.125
    for step in range(2):
        for c in range(3):
            tiles = turn([mixed[3 * step + c, j] for j in range(16)])
            for az in range(sector):
                own[step, c, az] = tiles[az]
                narrow = tiles[az].astype(BF16)
                if step == 0:
                    up[c * 16 + az] = narrow
                    down[c * 16 + az] = narrow
                elif az >= 8:
                    up[48 + c * 8 + az - 8] = narrow
                else:
                    down[48 + c * 8 + az] = narrow


def pack_entries(entries, order, mask, even, odd):
    right = mask[...] > 0.5
    results = []
    for way in range(2):
        tiles = []
        for n in range(len(entries) // 2):
            rows = [ref[at].astype(F32) for ref, at in entries[2 * n] + entries[2 * n + 1]]
            tiles.append(pack(rows, way == 1, CAA_WIDTH))
        x = jnp.concatenate(tiles, axis=0).astype(BF16)
        y = jnp.dot(x, order[way], preferred_element_type=F32)
        results.append([y[8 * n : 8 * n + 8] for n in range(len(tiles))])
    for n, (first, last) in enumerate(zip(*results)):
        even[n] = jnp.where(right, last, first).astype(BF16)
        odd[n] = jnp.where(right, first, last).astype(BF16)


def state_pack_kernel(sector, below, above, both, order, mask, even, odd):
    entries = []
    for f in range(7):
        for e in range(12):
            ref = (below, both, above)[e // 4]
            entries.append([(ref, f * sector + 4 * (e % 4) + i) for i in range(4)])
    pack_entries(entries, order, mask, even, odd)


def source_pack_kernel(sector, own, below, above, order, mask, even, odd):
    entries = []
    for c in range(3):
        for e in range(12):
            if 4 <= e < 8:
                entries.append([(own, (0, c, 4 * (e - 4) + i)) for i in range(4)])
            else:
                entries.append([(below if e < 4 else above, c * 16 + 4 * (e % 4) + i) for i in range(4)])
    for c in range(3):
        for e in range(2, 10):
            if 4 <= e < 8:
                entries.append([(own, (1, c, 4 * (e - 4) + i)) for i in range(4)])
            elif e < 4:
                entries.append([(below, 48 + c * 8 + 4 * (e - 2) + i) for i in range(4)])
            else:
                entries.append([(above, 48 + c * 8 + 4 * (e - 8) + i) for i in range(4)])
    pack_entries(entries, order, mask, even, odd)


CAA_RANGES = ((0, 12), (1, 11), (1, 11), (2, 10), (2, 10), (3, 9), (3, 9), (4, 8))


def caa_kernel(
    sector, w, m, own, below, above, caa_below, caa_above, state_odd, state_even, odd, even, mask, weights, coef, upward,
    out, wm, wt, mm, mt, sm, st,
):
    state_left, state_right = sides(mask, state_even, state_odd)
    from_left, from_right = sides(mask, even, odd)
    for f in range(7):
        for az in range(3 * sector):
            if az < sector:
                value = caa_below[f * sector + az].astype(F32)
            elif az < 2 * sector:
                value = column(w, f, az - sector, sector) if f < 4 else column(m, f - 4, az - sector, sector)
            else:
                value = caa_above[f * sector + az - 2 * sector].astype(F32)
            if f < 4:
                wm[0, f, az] = value
            else:
                mm[f - 4, az] = value * caa_step
        for e in range(12):
            value = acoustic_tile(state_left, state_right, 12 * f + e)
            if f < 4:
                wt[0, f, e] = value
            else:
                mt[f - 4, e] = value * caa_step
    for c in range(3):
        for az in range(16):
            sm[0, c, az] = below[c * 16 + az].astype(F32) * caa_step
            sm[0, c, 16 + az] = own[0, c, az] * caa_step
            sm[0, c, 32 + az] = above[c * 16 + az].astype(F32) * caa_step
            sm[1, c, 16 + az] = own[1, c, az] * caa_step
        for az in range(8):
            sm[1, c, 8 + az] = below[48 + c * 8 + az].astype(F32) * caa_step
            sm[1, c, 32 + az] = above[48 + c * 8 + az].astype(F32) * caa_step
        for e in range(12):
            st[0, c, e] = acoustic_tile(from_left, from_right, 12 * c + e) * caa_step
        for e in range(8):
            st[1, c, 2 + e] = acoustic_tile(from_left, from_right, 36 + 8 * c + e) * caa_step

    def along(tiles, which):
        x = jnp.concatenate(tiles, axis=0).astype(BF16)
        y = jnp.dot(x, weights[which], preferred_element_type=F32)
        y = y[:, :128] + y[:, 128:]
        return [y[8 * n : 8 * n + 8] for n in range(len(tiles))]

    def pair(now, source, e, final):
        rows = [[wm[now, f, 4 * e + i] for i in range(8)] for f in range(4)]
        tiles = [[wt[now, f, e + n] for n in range(2)] for f in range(4)]
        below, above, tile_below, tile_above = max(4 * e - 1, 0), min(4 * e + 8, 47), max(e - 1, 0), min(e + 2, 11)

        def mixed(values):
            p, v0, v1, v2 = values
            return [
                [mach_number * a + b for a, b in zip(p, v0)],
                [mach_number * b + a for a, b in zip(p, v0)],
                v1,
                v2,
            ]

        def update(values, metric, sources, stream, around, up, store):
            p, v0, v1, v2 = values
            for n in range(len(p)):
                m0, m1, m2 = metric(0, n), metric(1, n), metric(2, n)
                half = mach_number * m0
                store(0, n, p[n] - m0 * stream[0][n] - m1 * around[1][n] - m2 * up[1][n])
                store(1, n, v0[n] - m0 * stream[1][n] + sources(0, n))
                store(2, n, v1[n] - half * stream[2][n] - m1 * around[0][n] + sources(1, n))
                store(3, n, v2[n] - half * stream[3][n] - m2 * up[0][n] + sources(2, n))

        fields, halos = mixed(rows), mixed(tiles)
        x = [jnp.concatenate(rows[f] + tiles[f], axis=0).astype(BF16) for f in (0, 3)]
        y = jnp.dot(upward[...], jnp.concatenate(x, axis=1), preferred_element_type=F32)
        y = y[:80] + y[80:]
        up = [[y[8 * n : 8 * n + 8, 128 * f : 128 * f + 128] for n in range(10)] for f in range(2)]

        stream = along([row for values in fields for row in values], 0)
        stream = [[stream[8 * f + n] for n in range(8)] for f in range(4)]
        for f in range(4):
            for n in range(8):
                edge = lane_roll(halos[f][n // 4], -32 * (n % 4) - 16)
                stream[f][n] = stream[f][n] + coef[8] * edge
        around = [azimuth_main(rows[f], wm[now, f, below], wm[now, f, above]) for f in (0, 2)]

        def store(f, n, value):
            if final:
                out[f, pl.ds(4 * e + n - 16, 8, stride=sector), :] = value
            else:
                wm[1 - now, f, 4 * e + n] = value

        update(rows, lambda c, n: mm[c, 4 * e + n], lambda c, n: sm[source, c, 4 * e + n], stream, around, up, store)
        if final:
            return

        stream = along([tile for values in halos for tile in values], 1)
        stream = [[stream[2 * f + n] for n in range(2)] for f in range(4)]
        run = lanes_of() // 32
        for f in range(4):
            for n in range(2):
                edge = None
                for i in range(4):
                    moved = lane_roll(fields[f][4 * n + i], 32 * i + 16)
                    edge = moved if edge is None else jnp.where(run == i, moved, edge)
                stream[f][n] = stream[f][n] + coef[9] * edge
        around = []
        for f in (0, 2):
            values = []
            for n in range(2):
                before = wt[now, f, tile_below] if n == 0 else tiles[f][0]
                after = wt[now, f, tile_above] if n == 1 else tiles[f][1]
                total = coef[WHOLE_P] * lane_roll(before, -96) + coef[WHOLE_N] * lane_roll(after, 96)
                for k, offset in enumerate(OFFSETS):
                    total = total + coef[WHOLE_T + k] * lane_roll(tiles[f][n], -32 * offset)
                values.append(total)
            around.append(values)

        def store(f, n, value):
            wt[1 - now, f, e + n] = value

        up = [values[8:] for values in up]
        update(tiles, lambda c, n: mt[c, e + n], lambda c, n: st[source, c, e + n], stream, around, up, store)

    for step, (start, stop) in enumerate(CAA_RANGES):
        for e in range(start, stop, 2):
            pair(step % 2, step // 4, e, step == 7)


def call(kernel, name, outs, *args, smem=0, far=0, far_outs=0, scratch=()):
    whole, hbm = pl.BlockSpec(memory_space=pltpu.VMEM), pl.BlockSpec(memory_space=pltpu.HBM)
    args = [pltpu.with_memory_space_constraint(x, pltpu.HBM) if smem <= n < smem + far else x for n, x in enumerate(args)]
    specs = [pl.BlockSpec(memory_space=pltpu.SMEM)] * smem + [hbm] * far
    return pl.pallas_call(
        kernel,
        name=name,
        out_shape=[jax.ShapeDtypeStruct(shape, dtype) for shape, dtype in outs],
        in_specs=specs + [whole] * (len(args) - smem - far),
        out_specs=[hbm] * far_outs + [whole] * (len(outs) - far_outs),
        scratch_shapes=list(scratch),
        compiler_params=pltpu.CompilerParams(vmem_limit_bytes=VMEM_LIMIT),
    )(*args)


def swap_pairs(ours, theirs, axis):
    count = lax.axis_size(axis)
    edges = lambda start: [pair for a in range(start, count - 1, 2) for pair in ((a, a + 1), (a + 1, a))]
    odd = lax.ppermute(theirs, axis, edges(1))
    even = lax.ppermute(ours, axis, edges(0))
    return even, odd


def both_ways(low, high, axis, closed):
    count = lax.axis_size(axis)
    ends = count if closed else count - 1
    below = lax.ppermute(high, axis, [(i, (i + 1) % count) for i in range(ends)])
    above = lax.ppermute(low, axis, [((i + 1) % count, i) for i in range(ends)])
    return below, above


def body(les_velocity, les_metric, caa_state, caa_metric, intersection_refs, offsets, send_list):
    _, radial_nodes, sector, length = les_velocity.shape
    slabs = lax.axis_size("gx")
    assert (radial_nodes, sector, length) == (8, 16, 128)
    lines = radial_nodes * sector
    u, lm, w, m = (x.reshape(-1, lines, length) for x in (les_velocity, les_metric, caa_state, caa_metric))
    les_weights = jnp.asarray(np.stack([split_matrix(128), split_matrix(LES_WIDTH)]))
    les_coef = jnp.asarray(coefficients(LES_WIDTH))
    caa_weights, caa_coef = jnp.asarray(acoustic_weights()), jnp.asarray(acoustic_coefficients())
    upward, order = jnp.asarray(radial_matrix(10)), jnp.asarray(halo_order())
    own_row = lax.axis_index("sec") * slabs + lax.axis_index("gx")
    sends = lax.dynamic_slice_in_dim(send_list, own_row, 1, axis=0).reshape(-1)
    tile = (8, 128)
    mask = jnp.broadcast_to(((own_row + 1) % 2).astype(F32), tile)
    vmem = lambda *shape, dtype=F32: pltpu.VMEM((*shape, *tile), dtype)

    low, high = call(
        functools.partial(first_kernel, sector),
        "first",
        [((15, *tile), F32)] * 2,
        u, lm,
        far=2,
        scratch=[pltpu.VMEM(u.shape, F32), pltpu.VMEM(lm.shape, F32), pltpu.SemaphoreType.DMA((2,))],
    )
    before, after = both_ways(low, high, "az", True)
    even, odd = call(
        functools.partial(les_pack_kernel, sector),
        "les_pack",
        [((4, *tile), F32)] * 2,
        u, lm, before, after, mask,
    )
    even, odd = swap_pairs(even, odd, STREAM)
    sent, um1, ut1 = call(
        functools.partial(les_kernel, sector),
        "les",
        [((slabs * 2, 6, *tile), BF16), ((3, 24, *tile), F32), ((3, 4, *tile), F32)],
        sends, u, lm, before, after, odd, even, mask, les_weights, les_coef,
        far=1,
        far_outs=1,
        scratch=[
            vmem(3, 24), vmem(3, 6), vmem(3, 24), vmem(3, 6), vmem(3, 24), vmem(16, 6, dtype=BF16),
            pltpu.SMEM(sends.shape, jnp.int32), pltpu.SemaphoreType.DMA, pltpu.SemaphoreType.DMA((2, *sends.shape)),
        ],
    )
    got = lax.all_to_all(sent.reshape(slabs, 96, 128), "gx", 0, 0, tiled=True).reshape(slabs * 2, 6, *tile)

    (both,) = call(functools.partial(narrow_kernel, sector), "narrow", [((7 * sector, *tile), BF16)], w, m)
    caa_below, caa_above = both_ways(both, both, "az", True)
    (les_out,) = call(
        functools.partial(les_out_kernel, sector),
        "les_out",
        [((3, lines, length), F32)],
        lm, um1, ut1, les_weights, les_coef,
        scratch=[vmem(3, 24)],
    )
    even, odd = call(
        functools.partial(state_pack_kernel, sector),
        "state_pack",
        [((42, *tile), BF16)] * 2,
        caa_below, caa_above, both, order, mask,
    )
    state_even, state_odd = swap_pairs(even, odd, STREAM)
    table = jnp.concatenate([intersection_refs.reshape(-1), offsets])
    got, table, state_odd, state_even, les_out = lax.optimization_barrier((got, table, state_odd, state_even, les_out))

    own, up, down = call(
        functools.partial(blend_kernel, sector),
        "blend",
        [((2, 3, sector, *tile), F32), ((72, *tile), BF16), ((72, *tile), BF16)],
        table, got,
        smem=1,
        scratch=[vmem(6, 16)],
    )
    below, above = both_ways(down, up, "az", True)
    even, odd = call(
        functools.partial(source_pack_kernel, sector),
        "source_pack",
        [((30, *tile), BF16)] * 2,
        own, below, above, order, mask,
    )
    even, odd = swap_pairs(even, odd, STREAM)
    (caa_out,) = call(
        functools.partial(caa_kernel, sector),
        "caa",
        [((4, lines, length), F32)],
        w, m, own, below, above, caa_below, caa_above, state_odd, state_even, odd, even, mask, caa_weights, caa_coef, upward,
        scratch=[vmem(2, 4, 48), vmem(2, 4, 12), vmem(3, 48), vmem(3, 12), vmem(2, 3, 48), vmem(2, 3, 12)],
    )
    return les_out.reshape(les_velocity.shape), caa_out.reshape(caa_state.shape)


def solution(mesh):
    field = P(None, None, "az", STREAM)
    in_specs = (field, field, field, field, P(STREAM, None), P(STREAM), P())
    return jax.shard_map(body, mesh=mesh, in_specs=in_specs, out_specs=(field, field), check_vma=False)
```

```python
import functools

import jax
import jax.numpy as jnp
import numpy as np
from jax import lax
from jax.experimental import pallas as pl
from jax.experimental.pallas import tpu as pltpu
from jax.sharding import PartitionSpec as P


les_step = 0.02
caa_step = 0.01
mach_number = 0.5

STREAM = ("sec", "gx")
F32 = jnp.float32
BF16 = jnp.bfloat16
VMEM_LIMIT = 24 * 1024 * 1024


def slope_table():
    points = np.array([-1.0, -(0.2**0.5), 0.2**0.5, 1.0])
    identity = np.eye(4)
    differences = points[:, None] - points[None, :] + identity
    inverse_weights = 1.0 / np.prod(differences, axis=1)
    slope_matrix = inverse_weights[None, :] / inverse_weights[:, None] / differences
    slope_matrix = slope_matrix * (1.0 - identity)
    return slope_matrix - identity * slope_matrix.sum(axis=1)[:, None]


DM = slope_table() + np.diag([3.0, 0.0, 0.0, -3.0])
DM[np.abs(DM) < 1e-12] = 0.0


def lane_matrix(run):
    result = np.zeros((128, 128))
    for e in range(32):
        result[4 * e : 4 * e + 4, 4 * e : 4 * e + 4] = DM.T
        if (4 * e) % run:
            result[4 * e - 1, 4 * e] = -3.0
        if (4 * e + 4) % run:
            result[4 * e + 4, 4 * e + 3] = 3.0
    return result


def split_matrix(run):
    full = lane_matrix(run).astype(np.float32)
    high = full.astype(jnp.bfloat16)
    low = (full - high.astype(np.float32)).astype(jnp.bfloat16)
    return np.block([[high, low], [high, np.zeros_like(low)]])


OFFSETS = (-3, -2, -1, 1, 2, 3)
RAD, AZT, AZP, AZN, EDGE_M, EDGE_T = 0, 6, 12, 13, 14, 15
LES_WIDTH, CAA_WIDTH = 4, 16


def coefficients(width):
    c = np.zeros((16, 8, 128), np.float32)
    for n, k in enumerate(OFFSETS):
        for s in range(8):
            i = s % 4
            if 0 <= i + k <= 3:
                c[RAD + n, s, :] = DM[i, i + k]
        for lane in range(128):
            i = (lane % 64) // width
            if i <= 3 and 0 <= i + k <= 3:
                c[AZT + n, :, lane] = DM[i, i + k]
    c[RAD + OFFSETS.index(1), 3, :] = 3.0
    c[RAD + OFFSETS.index(-1), 4, :] = -3.0
    for lane in range(128):
        i = (lane % 64) // width
        if i == 0:
            c[AZP, :, lane] = -3.0
        if i == 3:
            c[AZN, :, lane] = 3.0
    c[EDGE_M, :, 127] = 3.0
    c[EDGE_M, :, 0] = -3.0
    for i in range(4):
        c[EDGE_T, :, width * i] = -3.0
        c[EDGE_T, :, 63 + width * (i + 1)] = 3.0
    return c


WHOLE_T, WHOLE_P, WHOLE_N = 0, 6, 7


def acoustic_coefficients():
    c = np.zeros((10, 8, 128), np.float32)
    for lane in range(128):
        i = lane // 32
        for n, k in enumerate(OFFSETS):
            if 0 <= i + k <= 3:
                c[WHOLE_T + n, :, lane] = DM[i, i + k]
        if i == 0:
            c[WHOLE_P, :, lane] = -3.0
        if i == 3:
            c[WHOLE_N, :, lane] = 3.0
    c[8, :, 127], c[8, :, 0] = 3.0, -3.0
    for i in range(4):
        c[9, :, 32 * i + 15], c[9, :, 32 * i + 16] = -3.0, 3.0
    return c


def two_terms(full):
    full = full.astype(np.float32)
    high = full.astype(jnp.bfloat16)
    return high, (full - high.astype(np.float32)).astype(jnp.bfloat16)


def acoustic_weights():
    natural = lane_matrix(16)
    lane = np.arange(128)
    reverse = 16 * (lane // 16) + 15 - lane % 16
    return np.stack([np.concatenate(two_terms(full), axis=1) for full in (lane_matrix(128), natural[np.ix_(reverse, reverse)])])


def radial_matrix(count):
    block = np.zeros((8, 8))
    block[:4, :4] = block[4:, 4:] = DM
    block[3, 4], block[4, 3] = 3.0, -3.0
    return np.concatenate(two_terms(np.kron(np.eye(count), block)), axis=0)


def halo_order():
    order = np.zeros((2, 128, 128), np.float32)
    for lane in range(128):
        i, half, k = lane // 32, (lane // 16) % 2, 15 - lane % 16
        order[0, 64 * half + 16 * i + k, lane] = 1.0
        order[1, 64 * (1 - half) + 16 * i + k, lane] = 1.0
    return order.astype(jnp.bfloat16)


def lanes_of():
    return lax.broadcasted_iota(jnp.int32, (8, 128), 1)


def lane_roll(x, shift):
    shift %= 128
    return pltpu.roll(x, shift, axis=1) if shift else x


def times(rows, weights):
    x = jnp.concatenate(rows, axis=0)
    high = x.astype(BF16)
    low = (x - high.astype(F32)).astype(BF16)
    y = jnp.dot(jnp.concatenate([high, low], axis=1), weights, preferred_element_type=F32)
    y = y[:, :128] + y[:, 128:]
    return [y[8 * n : 8 * n + 8] for n in range(len(rows))]


def edge_main(tile, i, width):
    return jnp.where(lanes_of() == 127, lane_roll(tile, 127 - width * i), lane_roll(tile, 65 - width * (i + 1)))


def stream_main(fields, halos, weights, coef, width):
    out = times([row for rows in fields for row in rows], weights)
    results = []
    at = 0
    for rows, tiles in zip(fields, halos):
        result = []
        for n in range(len(rows)):
            result.append(out[at] + coef[EDGE_M] * edge_main(tiles[n // 4], n % 4, width))
            at += 1
        results.append(result)
    return results


def stream_halo(fields, halos, weights, coef, width):
    lane = lanes_of()
    out = times([tile for tiles in halos for tile in tiles], weights)
    results = []
    at = 0
    for rows, tiles in zip(fields, halos):
        result = []
        for e in range(len(tiles)):
            edge = None
            for i in range(4):
                row, near, far = rows[4 * e + i], width * i, 63 + width * (i + 1)
                low, high = lane_roll(row, near + 1), lane_roll(row, far)
                edge = low if edge is None else jnp.where(lane == near, low, edge)
                edge = jnp.where(lane == far, high, edge)
            result.append(out[at] + coef[EDGE_T] * edge)
            at += 1
        results.append(result)
    return results


def azimuth_main(rows, before, after):
    out = []
    for e in range(len(rows) // 4):
        f = rows[4 * e : 4 * e + 4]
        prev = before if e == 0 else rows[4 * e - 1]
        following = after if 4 * e + 4 == len(rows) else rows[4 * e + 4]
        a, b, c = float(DM[0, 1]), float(DM[0, 2]), float(DM[0, 3])
        d, g, h = float(DM[1, 0]), float(DM[1, 2]), float(DM[1, 3])
        out.append(a * f[1] + b * f[2] + c * f[3] - 3.0 * prev)
        out.append(d * f[0] + g * f[2] + h * f[3])
        out.append(-(h * f[0] + g * f[1] + d * f[3]))
        out.append(3.0 * following - (c * f[0] + b * f[1] + a * f[2]))
    return out


def azimuth_halo(tiles, before, after, coef, width):
    out = []
    for e, tile in enumerate(tiles):
        prev = before if e == 0 else tiles[e - 1]
        following = after if e + 1 == len(tiles) else tiles[e + 1]
        total = coef[AZP] * lane_roll(prev, -3 * width) + coef[AZN] * lane_roll(following, 3 * width)
        for n, k in enumerate(OFFSETS):
            total = total + coef[AZT + n] * lane_roll(tile, -width * k)
        out.append(total)
    return out


def radial(tiles, coef):
    out = []
    for tile in tiles:
        total = None
        for n, k in enumerate(OFFSETS):
            term = coef[RAD + n] * pltpu.roll(tile, (-k) % 8, axis=0)
            total = term if total is None else total + term
        out.append(total)
    return out


def pack(rows, last, width):
    lane = lanes_of()
    out = None
    for g, row in enumerate(rows):
        moved = lane_roll(row, width * g + (width if last else 0))
        out = moved if out is None else jnp.where(lane >= width * g, moved, out)
    return out


class Side:
    def __init__(self, mask, first, second):
        self.mask, self.first, self.second = mask[...] > 0.5, first, second

    def __getitem__(self, at):
        return jnp.where(self.mask, self.first[at].astype(F32), self.second[at].astype(F32))


def sides(mask, even, odd):
    return Side(mask, odd, even), Side(mask, even, odd)


def halo_tile(from_left, from_right, n, width):
    count = 32 // width
    left, right = from_left[n // count].astype(F32), from_right[n // count].astype(F32)
    shift = 4 * width * (n % count)
    left, right = lane_roll(left, 64 - shift), lane_roll(right, -shift)
    lane = lanes_of()
    both = jnp.where(lane < 64, right, left)
    return jnp.where(lane % 64 < 4 * width, both, 0.0)


def acoustic_tile(from_left, from_right, n):
    left, right = from_left[n // 2].astype(F32), from_right[n // 2].astype(F32)
    if n % 2:
        left, right = lane_roll(left, 16), lane_roll(right, -16)
    return jnp.where(lanes_of() % 32 < 16, right, left)


def turn(tiles):
    group = lanes_of() // 8
    tiles = list(tiles)
    for bit in range(4):
        step = 1 << bit
        high = (group & step) != 0
        for p in range(16):
            if p & step:
                continue
            x, y = tiles[p], tiles[p | step]
            tiles[p] = jnp.where(high, lane_roll(y, 8 * step), x)
            tiles[p | step] = jnp.where(high, y, lane_roll(x, -8 * step))
    return tiles


def column(ref, c, az, sector):
    return ref[c, pl.ds(az, 8, stride=sector), :]


def first_kernel(sector, u_far, lm_far, mask, even, odd, u, lm, arrived):
    upper = mask[...] > 0.5
    copies = [pltpu.make_async_copy(a, b, arrived.at[n]) for n, (a, b) in enumerate([(u_far, u), (lm_far, lm)])]
    for copy in copies:
        copy.start()
    for copy in copies:
        copy.wait()
    for c in range(3):
        for n, low, high in [(4 * c + i, (u, i), (u, sector - 4 + i)) for i in range(4)] + [(12 + c, (lm, 0), (lm, sector - 1))]:
            low, high = column(low[0], c, low[1], sector), column(high[0], c, high[1], sector)
            even[n] = jnp.where(upper, high, low)
            odd[n] = jnp.where(upper, low, high)


def narrow_kernel(sector, w, m, both):
    for f in range(7):
        for az in range(sector):
            value = column(w, f, az, sector) if f < 4 else column(m, f - 4, az, sector)
            both[f * sector + az] = value.astype(BF16)


def les_pack_kernel(sector, u, lm, near_odd, near_even, mask_az, mask, even, odd):
    before, after = sides(mask_az, near_even, near_odd)
    right = mask[...] > 0.5
    entries = []
    for c in range(3):
        for e in range(-1, 5):
            if e < 0:
                entries.append([(before, 4 * c + i) for i in range(4)])
            elif e == 4:
                entries.append([(after, 4 * c + i) for i in range(4)])
            else:
                entries.append([(u, (c, pl.ds(4 * e + i, 8, stride=sector), slice(None))) for i in range(4)])
    for c in range(3):
        for e in range(4):
            entries.append([(lm, (c, pl.ds(4 * e + i, 8, stride=sector), slice(None))) for i in range(4)])
    for n in range(4):
        rows = [ref[at] for entry in entries[8 * n : 8 * n + 8] for ref, at in entry]
        first, last = pack(rows, False, LES_WIDTH), pack(rows, True, LES_WIDTH)
        even[n] = jnp.where(right, last, first)
        odd[n] = jnp.where(right, first, last)


def les_element(um, ut, mm, e, weights, coef, with_flux):
    rows = [[um[c, 4 * e + i] for i in range(4)] for c in range(3)]
    tiles = [[ut[c, e]] for c in range(3)]
    prev = [um[c, 4 * e - 1] for c in range(3)]
    following = [um[c, 4 * e + 4] for c in range(3)]
    metric = [[mm[c, 4 * e + i] for i in range(4)] for c in range(3)]
    fields, halos = list(rows), list(tiles)
    if with_flux:
        fields += [[x * y for x, y in zip(rows[0], rows[c])] for c in range(3)]
        halos += [[tiles[0][0] * tiles[c][0]] for c in range(3)]
    stream = stream_main(fields, halos, weights[0], coef, LES_WIDTH)
    scaled = lambda j, values: [a * b for a, b in zip(metric[j], values)]
    slopes = [[scaled(0, stream[c]) for c in range(3)], [], []]
    fluxes = [[scaled(0, stream[3 + c]) for c in range(3)] if with_flux else [], [], []]
    for c in range(3):
        slopes[1].append(scaled(1, azimuth_main(rows[c], prev[c], following[c])))
        slopes[2].append(scaled(2, radial(rows[c], coef)))
        if with_flux:
            product = [x * y for x, y in zip(rows[1], rows[c])]
            fluxes[1].append(scaled(1, azimuth_main(product, prev[1] * prev[c], following[1] * following[c])))
            fluxes[2].append(scaled(2, radial([x * y for x, y in zip(rows[2], rows[c])], coef)))
    return rows, tiles, fields, halos, slopes, fluxes


def les_change(rows, slopes, fluxes, c, i):
    total = None
    for j in range(3):
        term = fluxes[j][c][i] + rows[j][i] * slopes[j][c][i]
        total = term if total is None else total + term
    return (0.5 * les_step) * total


def lamb_of(rows, slopes, lamb, e):
    for i in range(4):
        first = slopes[1][2][i] - slopes[2][1][i]
        second = slopes[2][0][i] - slopes[0][2][i]
        third = slopes[0][1][i] - slopes[1][0][i]
        lamb[0, 4 * e + i] = second * rows[2][i] - third * rows[1][i]
        lamb[1, 4 * e + i] = third * rows[0][i] - first * rows[2][i]
        lamb[2, 4 * e + i] = first * rows[1][i] - second * rows[0][i]


def les_kernel(
    sector, sends_far, u, lm, near_odd, near_even, odd, even, mask_az, mask, weights, coef, sent, um1, ut1, um, ut, mm, mt, lamb, blk, sends, arrived,
):
    fetch = pltpu.make_async_copy(sends_far, sends, arrived)
    fetch.start()
    before, after = sides(mask_az, near_even, near_odd)
    from_left, from_right = sides(mask, even, odd)
    for c in range(3):
        for i in range(4):
            um[c, i] = before[4 * c + i]
            um[c, 4 + sector + i] = after[4 * c + i]
        mm[c, 3] = before[12 + c]
        mm[c, 4 + sector] = after[12 + c]
        for az in range(sector):
            um[c, 4 + az] = column(u, c, az, sector)
            mm[c, 4 + az] = column(lm, c, az, sector)
        for e in range(6):
            ut[c, e] = halo_tile(from_left, from_right, 6 * c + e, LES_WIDTH)
        for e in range(4):
            mt[c, e + 1] = halo_tile(from_left, from_right, 18 + 4 * c + e, LES_WIDTH)

    tiles, fields, ends = [], [], []
    for e, i in ((0, 3), (5, 0)):
        near = 4 if e == 0 else 3 + sector
        rows = [um[c, 4 * e + i] for c in range(3)]
        others = [[um[c, 4 * e + k] for k in range(4)] for c in range(3)]
        beyond = [um[c, near] for c in range(3)]
        halo = [ut[c, e] for c in range(3)]
        fields += rows + [rows[0] * rows[c] for c in range(3)]
        tiles += [(t, i) for t in halo + [halo[0] * halo[c] for c in range(3)]]
        ends.append((4 * e + i, i, rows, others, beyond))
    out = times(fields, weights[0])
    out = [y + coef[EDGE_M] * edge_main(t, i, LES_WIDTH) for y, (t, i) in zip(out, tiles)]
    for n, (at, i, rows, others, beyond) in enumerate(ends):
        metric = [mm[j, at] for j in range(3)]
        for c in range(3):
            slope = azimuth_main(others[c], beyond[c], beyond[c])[i]
            flux = azimuth_main([x * y for x, y in zip(others[1], others[c])], *[beyond[1] * beyond[c]] * 2)[i]
            total = metric[0] * (out[6 * n + 3 + c] + rows[0] * out[6 * n + c]) + metric[1] * (flux + rows[1] * slope)
            slope, flux = radial([rows[c], rows[2] * rows[c]], coef)
            total = total + metric[2] * (flux + rows[2] * slope)
            um1[c, at] = rows[c] - (0.5 * les_step) * total
        if i == 3:
            for c in range(3):
                for k in range(3):
                    um1[c, k] = rows[c]
                    um1[c, 5 + sector + k] = rows[c]

    for e in range(1, 5):
        rows, tiles, fields, halos, slopes, fluxes = les_element(um, ut, mm, e, weights, coef, True)
        lamb_of(rows, slopes, lamb, e)
        for c in range(3):
            for i in range(4):
                um1[c, 4 * e + i] = rows[c][i] - les_change(rows, slopes, fluxes, c, i)
        low = [ut[c, e - 1] for c in range(3)]
        high = [ut[c, e + 1] for c in range(3)]
        metric = [mt[c, e] for c in range(3)]
        stream = stream_halo(fields, halos, weights[1], coef, LES_WIDTH)
        for c in range(3):
            total = metric[0] * (stream[3 + c][0] + tiles[0][0] * stream[c][0])
            slope = azimuth_halo(tiles[c], low[c], high[c], coef, LES_WIDTH)[0]
            product = tiles[1][0] * tiles[c][0]
            flux = azimuth_halo([product], low[1] * low[c], high[1] * high[c], coef, LES_WIDTH)[0]
            total = total + metric[1] * (flux + tiles[1][0] * slope)
            slope, flux = radial([tiles[c][0], tiles[2][0] * tiles[c][0]], coef)
            total = total + metric[2] * (flux + tiles[2][0] * slope)
            ut1[c, e - 1] = tiles[c][0] - (0.5 * les_step) * total

    def blocks(step):
        for c in range(3):
            tiles = turn([lamb[c, 4 + az] for az in range(sector)])
            for j in range(16):
                blk[j, 3 * step + c] = tiles[j].astype(BF16)

    blocks(0)
    fetch.wait()

    for e in range(1, 5):
        rows, _, _, _, slopes, _ = les_element(um1, Shifted(ut1), mm, e, weights, coef, False)
        lamb_of(rows, slopes, lamb, e)

    blocks(1)
    for n in range(sends.shape[0]):
        index = jnp.clip(sends[n], 0, 15)
        for k in range(6):
            sent[n, k] = blk[index, k]


class Shifted:
    def __init__(self, ref):
        self.ref = ref

    def __getitem__(self, at):
        return self.ref[at[0], at[1] - 1]


def les_out_kernel(sector, lm, um1, ut1, weights, coef, out, mm):
    for c in range(3):
        for az in range(sector):
            mm[c, 4 + az] = column(lm, c, az, sector)

    @pl.loop(1, 5)
    def _(e):
        rows, _, _, _, slopes, fluxes = les_element(um1, Shifted(ut1), mm, e, weights, coef, True)
        for c in range(3):
            for i in range(4):
                out[c, pl.ds(4 * (e - 1) + i, 8, stride=sector), :] = rows[c][i] - les_change(rows, slopes, fluxes, c, i)


def blend_kernel(sector, refs, got, mask_az, own, even, odd, mixed):
    for j in range(16):
        a = jnp.clip(refs[4 * j] * 2 + refs[4 * j + 1], 0, got.shape[0] - 1)
        b = jnp.clip(refs[4 * j + 2] * 2 + refs[4 * j + 3], 0, got.shape[0] - 1)
        fraction = refs[64 + j].astype(F32)
        for k in range(6):
            blend = (8.0 - fraction) * got[a, k].astype(F32) + fraction * got[b, k].astype(F32)
            mixed[k, j] = blend * 0.125
    upper = mask_az[...] > 0.5
    for step in range(2):
        for c in range(3):
            tiles = turn([mixed[3 * step + c, j] for j in range(16)])
            for az in range(sector):
                own[step, c, az] = tiles[az]
            depth = DEPTHS[step]
            for n in range(depth):
                down, up = tiles[n], tiles[sector - depth + n]
                at = first_of(step, c) + n
                even[at] = jnp.where(upper, up, down).astype(BF16)
                odd[at] = jnp.where(upper, down, up).astype(BF16)


DEPTHS = (13, 5)


def first_of(step, c):
    return DEPTHS[step] * c + (3 * DEPTHS[0] if step else 0)


def source_row(below, above, step, c, az):
    depth = DEPTHS[step]
    if az < 0:
        return below, first_of(step, c) + max(az + depth, 0)
    return above, first_of(step, c) + min(az - 16, depth - 1)


def pack_entries(entries, order, mask, even, odd):
    right = mask[...] > 0.5
    results = []
    for way in range(2):
        tiles = []
        for n in range(len(entries) // 2):
            rows = [ref[at].astype(F32) for ref, at in entries[2 * n] + entries[2 * n + 1]]
            tiles.append(pack(rows, way == 1, CAA_WIDTH))
        x = jnp.concatenate(tiles, axis=0).astype(BF16)
        y = jnp.dot(x, order[way], preferred_element_type=F32)
        results.append([y[8 * n : 8 * n + 8] for n in range(len(tiles))])
    for n, (first, last) in enumerate(zip(*results)):
        even[n] = jnp.where(right, last, first).astype(BF16)
        odd[n] = jnp.where(right, first, last).astype(BF16)


def state_pack_kernel(sector, below, above, both, order, mask, even, odd):
    entries = []
    for f in range(7):
        for e in range(12):
            ref = (below, both, above)[e // 4]
            entries.append([(ref, f * sector + 4 * (e % 4) + i) for i in range(4)])
    pack_entries(entries, order, mask, even, odd)


def source_pack_kernel(sector, own, near_odd, near_even, order, mask_az, mask, even, odd):
    below, above = sides(mask_az, near_even, near_odd)
    entries = []
    for step, (start, stop) in enumerate(((0, 12), (2, 10))):
        for c in range(3):
            for e in range(start, stop):
                if 4 <= e < 8:
                    entries.append([(own, (step, c, 4 * (e - 4) + i)) for i in range(4)])
                else:
                    entries.append([source_row(below, above, step, c, 4 * (e - 4) + i) for i in range(4)])
    pack_entries(entries, order, mask, even, odd)


CAA_RANGES = ((0, 12), (1, 11), (1, 11), (2, 10), (2, 10), (3, 9), (3, 9), (4, 8))


def caa_kernel(
    sector, w, m, own, near_odd, near_even, mask_az, caa_below, caa_above, state_odd, state_even, odd, even, mask, weights, coef, upward,
    out, wm, wt, mm, mt, sm, st,
):
    below, above = sides(mask_az, near_even, near_odd)
    state_left, state_right = sides(mask, state_even, state_odd)
    from_left, from_right = sides(mask, even, odd)
    for f in range(7):
        for az in range(3 * sector):
            if az < sector:
                value = caa_below[f * sector + az].astype(F32)
            elif az < 2 * sector:
                value = column(w, f, az - sector, sector) if f < 4 else column(m, f - 4, az - sector, sector)
            else:
                value = caa_above[f * sector + az - 2 * sector].astype(F32)
            if f < 4:
                wm[0, f, az] = value
            else:
                mm[f - 4, az] = value * caa_step
        for e in range(12):
            value = acoustic_tile(state_left, state_right, 12 * f + e)
            if f < 4:
                wt[0, f, e] = value
            else:
                mt[f - 4, e] = value * caa_step
    for c in range(3):
        for az in range(16):
            sm[0, c, 16 + az] = own[0, c, az] * caa_step
            sm[1, c, 16 + az] = own[1, c, az] * caa_step
        for step, depth in enumerate((16, 8)):
            for az in [*range(-depth, 0), *range(16, 16 + depth)]:
                ref, at = source_row(below, above, step, c, az)
                sm[step, c, 16 + az] = ref[at] * caa_step
        for e in range(12):
            st[0, c, e] = acoustic_tile(from_left, from_right, 12 * c + e) * caa_step
        for e in range(8):
            st[1, c, 2 + e] = acoustic_tile(from_left, from_right, 36 + 8 * c + e) * caa_step

    def along(tiles, which):
        x = jnp.concatenate(tiles, axis=0).astype(BF16)
        y = jnp.dot(x, weights[which], preferred_element_type=F32)
        y = y[:, :128] + y[:, 128:]
        return [y[8 * n : 8 * n + 8] for n in range(len(tiles))]

    def pair(now, source, e, final):
        rows = [[wm[now, f, 4 * e + i] for i in range(8)] for f in range(4)]
        tiles = [[wt[now, f, e + n] for n in range(2)] for f in range(4)]
        below, above, tile_below, tile_above = max(4 * e - 1, 0), min(4 * e + 8, 47), max(e - 1, 0), min(e + 2, 11)

        def mixed(values):
            p, v0, v1, v2 = values
            return [
                [mach_number * a + b for a, b in zip(p, v0)],
                [mach_number * b + a for a, b in zip(p, v0)],
                v1,
                v2,
            ]

        def update(values, metric, sources, stream, around, up, store):
            p, v0, v1, v2 = values
            for n in range(len(p)):
                m0, m1, m2 = metric(0, n), metric(1, n), metric(2, n)
                half = mach_number * m0
                store(0, n, p[n] - m0 * stream[0][n] - m1 * around[1][n] - m2 * up[1][n])
                store(1, n, v0[n] - m0 * stream[1][n] + sources(0, n))
                store(2, n, v1[n] - half * stream[2][n] - m1 * around[0][n] + sources(1, n))
                store(3, n, v2[n] - half * stream[3][n] - m2 * up[0][n] + sources(2, n))

        fields, halos = mixed(rows), mixed(tiles)
        x = [jnp.concatenate(rows[f] + tiles[f], axis=0).astype(BF16) for f in (0, 3)]
        y = jnp.dot(upward[...], jnp.concatenate(x, axis=1), preferred_element_type=F32)
        y = y[:80] + y[80:]
        up = [[y[8 * n : 8 * n + 8, 128 * f : 128 * f + 128] for n in range(10)] for f in range(2)]

        stream = along([row for values in fields for row in values], 0)
        stream = [[stream[8 * f + n] for n in range(8)] for f in range(4)]
        for f in range(4):
            for n in range(8):
                edge = lane_roll(halos[f][n // 4], -32 * (n % 4) - 16)
                stream[f][n] = stream[f][n] + coef[8] * edge
        around = [azimuth_main(rows[f], wm[now, f, below], wm[now, f, above]) for f in (0, 2)]

        def store(f, n, value):
            if final:
                out[f, pl.ds(4 * e + n - 16, 8, stride=sector), :] = value
            else:
                wm[1 - now, f, 4 * e + n] = value

        update(rows, lambda c, n: mm[c, 4 * e + n], lambda c, n: sm[source, c, 4 * e + n], stream, around, up, store)
        if final:
            return

        stream = along([tile for values in halos for tile in values], 1)
        stream = [[stream[2 * f + n] for n in range(2)] for f in range(4)]
        run = lanes_of() // 32
        for f in range(4):
            for n in range(2):
                edge = None
                for i in range(4):
                    moved = lane_roll(fields[f][4 * n + i], 32 * i + 16)
                    edge = moved if edge is None else jnp.where(run == i, moved, edge)
                stream[f][n] = stream[f][n] + coef[9] * edge
        around = []
        for f in (0, 2):
            values = []
            for n in range(2):
                before = wt[now, f, tile_below] if n == 0 else tiles[f][0]
                after = wt[now, f, tile_above] if n == 1 else tiles[f][1]
                total = coef[WHOLE_P] * lane_roll(before, -96) + coef[WHOLE_N] * lane_roll(after, 96)
                for k, offset in enumerate(OFFSETS):
                    total = total + coef[WHOLE_T + k] * lane_roll(tiles[f][n], -32 * offset)
                values.append(total)
            around.append(values)

        def store(f, n, value):
            wt[1 - now, f, e + n] = value

        up = [values[8:] for values in up]
        update(tiles, lambda c, n: mt[c, e + n], lambda c, n: st[source, c, e + n], stream, around, up, store)

    for step, (start, stop) in enumerate(CAA_RANGES):
        for e in range(start, stop, 2):
            pair(step % 2, step // 4, e, step == 7)


def call(kernel, name, outs, *args, smem=0, far=0, free=0, scratch=()):
    whole, hbm = pl.BlockSpec(memory_space=pltpu.VMEM), pl.BlockSpec(memory_space=pltpu.HBM)
    args = [pltpu.with_memory_space_constraint(x, pltpu.HBM) if smem <= n < smem + far else x for n, x in enumerate(args)]
    specs = [pl.BlockSpec(memory_space=pltpu.SMEM)] * smem + [hbm] * far + [pl.BlockSpec(memory_space=pl.ANY)] * free
    return pl.pallas_call(
        kernel,
        name=name,
        out_shape=[jax.ShapeDtypeStruct(shape, dtype) for shape, dtype in outs],
        in_specs=specs + [whole] * (len(args) - smem - far - free),
        out_specs=[whole] * len(outs),
        scratch_shapes=list(scratch),
        compiler_params=pltpu.CompilerParams(vmem_limit_bytes=VMEM_LIMIT),
    )(*args)


def swap_pairs(ours, theirs, axis, closed):
    count = lax.axis_size(axis)
    ends = count if closed else count - 1
    edges = lambda start: [pair for a in range(start, ends, 2) for pair in ((a, (a + 1) % count), ((a + 1) % count, a))]
    odd = lax.ppermute(theirs, axis, edges(1))
    even = lax.ppermute(ours, axis, edges(0))
    return even, odd


def both_ways(low, high, axis, closed):
    count = lax.axis_size(axis)
    ends = count if closed else count - 1
    below = lax.ppermute(high, axis, [(i, (i + 1) % count) for i in range(ends)])
    above = lax.ppermute(low, axis, [((i + 1) % count, i) for i in range(ends)])
    return below, above


def body(les_velocity, les_metric, caa_state, caa_metric, intersection_refs, offsets, send_list):
    _, radial_nodes, sector, length = les_velocity.shape
    slabs = lax.axis_size("gx")
    assert (radial_nodes, sector, length) == (8, 16, 128)
    lines = radial_nodes * sector
    u, lm, w, m = (x.reshape(-1, lines, length) for x in (les_velocity, les_metric, caa_state, caa_metric))
    les_weights = jnp.asarray(np.stack([split_matrix(128), split_matrix(LES_WIDTH)]))
    les_coef = jnp.asarray(coefficients(LES_WIDTH))
    caa_weights, caa_coef = jnp.asarray(acoustic_weights()), jnp.asarray(acoustic_coefficients())
    upward, order = jnp.asarray(radial_matrix(10)), jnp.asarray(halo_order())
    own_row = lax.axis_index("sec") * slabs + lax.axis_index("gx")
    sends = lax.dynamic_slice_in_dim(send_list, own_row, 1, axis=0).reshape(-1)
    tile = (8, 128)
    mask = jnp.broadcast_to(((own_row + 1) % 2).astype(F32), tile)
    mask_az = jnp.broadcast_to(((lax.axis_index("az") + 1) % 2).astype(F32), tile)
    vmem = lambda *shape, dtype=F32: pltpu.VMEM((*shape, *tile), dtype)

    even, odd = call(
        functools.partial(first_kernel, sector),
        "first",
        [((15, *tile), F32)] * 2,
        u, lm, mask_az,
        far=2,
        scratch=[pltpu.VMEM(u.shape, F32), pltpu.VMEM(lm.shape, F32), pltpu.SemaphoreType.DMA((2,))],
    )
    near_even, near_odd = swap_pairs(even, odd, "az", True)
    even, odd = call(
        functools.partial(les_pack_kernel, sector),
        "les_pack",
        [((4, *tile), F32)] * 2,
        u, lm, near_odd, near_even, mask_az, mask,
    )
    even, odd = swap_pairs(even, odd, STREAM, False)
    sent, um1, ut1 = call(
        functools.partial(les_kernel, sector),
        "les",
        [((slabs * 2, 6, *tile), BF16), ((3, 24, *tile), F32), ((3, 4, *tile), F32)],
        sends, u, lm, near_odd, near_even, odd, even, mask_az, mask, les_weights, les_coef,
        free=1,
        scratch=[
            vmem(3, 24), vmem(3, 6), vmem(3, 24), vmem(3, 6), vmem(3, 24), vmem(16, 6, dtype=BF16),
            pltpu.SMEM(sends.shape, jnp.int32), pltpu.SemaphoreType.DMA,
        ],
    )
    got = lax.all_to_all(sent.reshape(slabs, 96, 128), "gx", 0, 0, tiled=True).reshape(slabs * 2, 6, *tile)

    (both,) = call(functools.partial(narrow_kernel, sector), "narrow", [((7 * sector, *tile), BF16)], w, m)
    caa_below, caa_above = both_ways(both, both, "az", True)
    (les_out,) = call(
        functools.partial(les_out_kernel, sector),
        "les_out",
        [((3, lines, length), F32)],
        lm, um1, ut1, les_weights, les_coef,
        scratch=[vmem(3, 24)],
    )
    even, odd = call(
        functools.partial(state_pack_kernel, sector),
        "state_pack",
        [((42, *tile), BF16)] * 2,
        caa_below, caa_above, both, order, mask,
    )
    state_even, state_odd = swap_pairs(even, odd, STREAM, False)
    table = jnp.concatenate([intersection_refs.reshape(-1), offsets])
    got, table, state_odd, state_even, les_out = lax.optimization_barrier((got, table, state_odd, state_even, les_out))

    own, even, odd = call(
        functools.partial(blend_kernel, sector),
        "blend",
        [((2, 3, sector, *tile), F32), ((54, *tile), BF16), ((54, *tile), BF16)],
        table, got, mask_az,
        smem=1,
        scratch=[vmem(6, 16)],
    )
    near_even, near_odd = swap_pairs(even, odd, "az", True)
    even, odd = call(
        functools.partial(source_pack_kernel, sector),
        "source_pack",
        [((30, *tile), BF16)] * 2,
        own, near_odd, near_even, order, mask_az, mask,
    )
    even, odd = swap_pairs(even, odd, STREAM, False)
    (caa_out,) = call(
        functools.partial(caa_kernel, sector),
        "caa",
        [((4, lines, length), F32)],
        w, m, own, near_odd, near_even, mask_az, caa_below, caa_above, state_odd, state_even, odd, even, mask, caa_weights, caa_coef, upward,
        scratch=[vmem(2, 4, 48), vmem(2, 4, 12), vmem(3, 48), vmem(3, 12), vmem(2, 3, 48), vmem(2, 3, 12)],
    )
    return les_out.reshape(les_velocity.shape), caa_out.reshape(caa_state.shape)


def solution(mesh):
    field = P(None, None, "az", STREAM)
    in_specs = (field, field, field, field, P(STREAM, None), P(STREAM), P())
    return jax.shard_map(body, mesh=mesh, in_specs=in_specs, out_specs=(field, field), check_vma=False)
```

```python
import functools

import jax
import jax.numpy as jnp
import numpy as np
from jax import lax
from jax.experimental import pallas as pl
from jax.experimental.pallas import tpu as pltpu
from jax.sharding import PartitionSpec as P


les_step = 0.02
caa_step = 0.01
mach_number = 0.5

STREAM = ("sec", "gx")
F32 = jnp.float32
BF16 = jnp.bfloat16
VMEM_LIMIT = 24 * 1024 * 1024


def slope_table():
    points = np.array([-1.0, -(0.2**0.5), 0.2**0.5, 1.0])
    identity = np.eye(4)
    differences = points[:, None] - points[None, :] + identity
    inverse_weights = 1.0 / np.prod(differences, axis=1)
    slope_matrix = inverse_weights[None, :] / inverse_weights[:, None] / differences
    slope_matrix = slope_matrix * (1.0 - identity)
    return slope_matrix - identity * slope_matrix.sum(axis=1)[:, None]


DM = slope_table() + np.diag([3.0, 0.0, 0.0, -3.0])
DM[np.abs(DM) < 1e-12] = 0.0


def lane_matrix(run):
    result = np.zeros((128, 128))
    for e in range(32):
        result[4 * e : 4 * e + 4, 4 * e : 4 * e + 4] = DM.T
        if (4 * e) % run:
            result[4 * e - 1, 4 * e] = -3.0
        if (4 * e + 4) % run:
            result[4 * e + 4, 4 * e + 3] = 3.0
    return result


def split_matrix(run):
    full = lane_matrix(run).astype(np.float32)
    high = full.astype(jnp.bfloat16)
    low = (full - high.astype(np.float32)).astype(jnp.bfloat16)
    return np.block([[high, low], [high, np.zeros_like(low)]])


OFFSETS = (-3, -2, -1, 1, 2, 3)
RAD, AZT, AZP, AZN, EDGE_M, EDGE_T = 0, 6, 12, 13, 14, 15
LES_WIDTH, CAA_WIDTH = 4, 16


def coefficients(width):
    c = np.zeros((16, 8, 128), np.float32)
    for n, k in enumerate(OFFSETS):
        for s in range(8):
            i = s % 4
            if 0 <= i + k <= 3:
                c[RAD + n, s, :] = DM[i, i + k]
        for lane in range(128):
            i = (lane % 64) // width
            if i <= 3 and 0 <= i + k <= 3:
                c[AZT + n, :, lane] = DM[i, i + k]
    c[RAD + OFFSETS.index(1), 3, :] = 3.0
    c[RAD + OFFSETS.index(-1), 4, :] = -3.0
    for lane in range(128):
        i = (lane % 64) // width
        if i == 0:
            c[AZP, :, lane] = -3.0
        if i == 3:
            c[AZN, :, lane] = 3.0
    c[EDGE_M, :, 127] = 3.0
    c[EDGE_M, :, 0] = -3.0
    for i in range(4):
        c[EDGE_T, :, width * i] = -3.0
        c[EDGE_T, :, 63 + width * (i + 1)] = 3.0
    return c


WHOLE_T, WHOLE_P, WHOLE_N = 0, 6, 7


def acoustic_coefficients():
    c = np.zeros((10, 8, 128), np.float32)
    for lane in range(128):
        i = lane // 32
        for n, k in enumerate(OFFSETS):
            if 0 <= i + k <= 3:
                c[WHOLE_T + n, :, lane] = DM[i, i + k]
        if i == 0:
            c[WHOLE_P, :, lane] = -3.0
        if i == 3:
            c[WHOLE_N, :, lane] = 3.0
    c[8, :, 127], c[8, :, 0] = 3.0, -3.0
    for i in range(4):
        c[9, :, 32 * i + 15], c[9, :, 32 * i + 16] = -3.0, 3.0
    return c


def two_terms(full):
    full = full.astype(np.float32)
    high = full.astype(jnp.bfloat16)
    return high, (full - high.astype(np.float32)).astype(jnp.bfloat16)


def acoustic_weights():
    natural = lane_matrix(16)
    lane = np.arange(128)
    reverse = 16 * (lane // 16) + 15 - lane % 16
    return np.stack([np.concatenate(two_terms(full), axis=1) for full in (lane_matrix(128), natural[np.ix_(reverse, reverse)])])


def radial_matrix(count):
    block = np.zeros((8, 8))
    block[:4, :4] = block[4:, 4:] = DM
    block[3, 4], block[4, 3] = 3.0, -3.0
    return np.concatenate(two_terms(np.kron(np.eye(count), block)), axis=0)


def halo_order():
    order = np.zeros((2, 128, 128), np.float32)
    for lane in range(128):
        i, half, k = lane // 32, (lane // 16) % 2, 15 - lane % 16
        order[0, 64 * half + 16 * i + k, lane] = 1.0
        order[1, 64 * (1 - half) + 16 * i + k, lane] = 1.0
    return order.astype(jnp.bfloat16)


def lanes_of():
    return lax.broadcasted_iota(jnp.int32, (8, 128), 1)


def lane_roll(x, shift):
    shift %= 128
    return pltpu.roll(x, shift, axis=1) if shift else x


def times(rows, weights):
    x = jnp.concatenate(rows, axis=0)
    high = x.astype(BF16)
    low = (x - high.astype(F32)).astype(BF16)
    y = jnp.dot(jnp.concatenate([high, low], axis=1), weights, preferred_element_type=F32)
    y = y[:, :128] + y[:, 128:]
    return [y[8 * n : 8 * n + 8] for n in range(len(rows))]


def edge_main(tile, i, width):
    return jnp.where(lanes_of() == 127, lane_roll(tile, 127 - width * i), lane_roll(tile, 65 - width * (i + 1)))


def stream_main(fields, halos, weights, coef, width):
    out = times([row for rows in fields for row in rows], weights)
    results = []
    at = 0
    for rows, tiles in zip(fields, halos):
        result = []
        for n in range(len(rows)):
            result.append(out[at] + coef[EDGE_M] * edge_main(tiles[n // 4], n % 4, width))
            at += 1
        results.append(result)
    return results


def stream_halo(fields, halos, weights, coef, width):
    lane = lanes_of()
    out = times([tile for tiles in halos for tile in tiles], weights)
    results = []
    at = 0
    for rows, tiles in zip(fields, halos):
        result = []
        for e in range(len(tiles)):
            edge = None
            for i in range(4):
                row, near, far = rows[4 * e + i], width * i, 63 + width * (i + 1)
                low, high = lane_roll(row, near + 1), lane_roll(row, far)
                edge = low if edge is None else jnp.where(lane == near, low, edge)
                edge = jnp.where(lane == far, high, edge)
            result.append(out[at] + coef[EDGE_T] * edge)
            at += 1
        results.append(result)
    return results


def azimuth_main(rows, before, after):
    out = []
    for e in range(len(rows) // 4):
        f = rows[4 * e : 4 * e + 4]
        prev = before if e == 0 else rows[4 * e - 1]
        following = after if 4 * e + 4 == len(rows) else rows[4 * e + 4]
        a, b, c = float(DM[0, 1]), float(DM[0, 2]), float(DM[0, 3])
        d, g, h = float(DM[1, 0]), float(DM[1, 2]), float(DM[1, 3])
        out.append(a * f[1] + b * f[2] + c * f[3] - 3.0 * prev)
        out.append(d * f[0] + g * f[2] + h * f[3])
        out.append(-(h * f[0] + g * f[1] + d * f[3]))
        out.append(3.0 * following - (c * f[0] + b * f[1] + a * f[2]))
    return out


def azimuth_halo(tiles, before, after, coef, width):
    out = []
    for e, tile in enumerate(tiles):
        prev = before if e == 0 else tiles[e - 1]
        following = after if e + 1 == len(tiles) else tiles[e + 1]
        total = coef[AZP] * lane_roll(prev, -3 * width) + coef[AZN] * lane_roll(following, 3 * width)
        for n, k in enumerate(OFFSETS):
            total = total + coef[AZT + n] * lane_roll(tile, -width * k)
        out.append(total)
    return out


def radial(tiles, coef):
    out = []
    for tile in tiles:
        total = None
        for n, k in enumerate(OFFSETS):
            term = coef[RAD + n] * pltpu.roll(tile, (-k) % 8, axis=0)
            total = term if total is None else total + term
        out.append(total)
    return out


def pack(rows, last, width):
    lane = lanes_of()
    out = None
    for g, row in enumerate(rows):
        moved = lane_roll(row, width * g + (width if last else 0))
        out = moved if out is None else jnp.where(lane >= width * g, moved, out)
    return out


class Side:
    def __init__(self, mask, first, second):
        self.mask, self.first, self.second = mask[...] > 0.5, first, second

    def __getitem__(self, at):
        return jnp.where(self.mask, self.first[at].astype(F32), self.second[at].astype(F32))


def sides(mask, even, odd):
    return Side(mask, odd, even), Side(mask, even, odd)


def halo_tile(from_left, from_right, n, width):
    count = 32 // width
    left, right = from_left[n // count].astype(F32), from_right[n // count].astype(F32)
    shift = 4 * width * (n % count)
    left, right = lane_roll(left, 64 - shift), lane_roll(right, -shift)
    lane = lanes_of()
    both = jnp.where(lane < 64, right, left)
    return jnp.where(lane % 64 < 4 * width, both, 0.0)


def acoustic_tile(from_left, from_right, n):
    left, right = from_left[n // 2].astype(F32), from_right[n // 2].astype(F32)
    if n % 2:
        left, right = lane_roll(left, 16), lane_roll(right, -16)
    return jnp.where(lanes_of() % 32 < 16, right, left)


def turn(tiles):
    group = lanes_of() // 8
    tiles = list(tiles)
    for bit in range(4):
        step = 1 << bit
        high = (group & step) != 0
        for p in range(16):
            if p & step:
                continue
            x, y = tiles[p], tiles[p | step]
            tiles[p] = jnp.where(high, lane_roll(y, 8 * step), x)
            tiles[p | step] = jnp.where(high, y, lane_roll(x, -8 * step))
    return tiles


def column(ref, c, az, sector):
    return ref[c, pl.ds(az, 8, stride=sector), :]


def first_kernel(sector, u_far, lm_far, low, high, u, lm, arrived):
    copies = [pltpu.make_async_copy(a, b, arrived.at[n]) for n, (a, b) in enumerate([(u_far, u), (lm_far, lm)])]
    for copy in copies:
        copy.start()
    for copy in copies:
        copy.wait()
    for c in range(3):
        for i in range(4):
            low[4 * c + i] = column(u, c, i, sector)
            high[4 * c + i] = column(u, c, sector - 4 + i, sector)
        low[12 + c] = column(lm, c, 0, sector)
        high[12 + c] = column(lm, c, sector - 1, sector)


def narrow_kernel(sector, w, m, both):
    for f in range(7):
        for az in range(sector):
            value = column(w, f, az, sector) if f < 4 else column(m, f - 4, az, sector)
            both[f * sector + az] = value.astype(BF16)


def les_pack_kernel(sector, u, lm, before, after, mask, even, odd):
    right = mask[...] > 0.5
    entries = []
    for c in range(3):
        for e in range(-1, 5):
            if e < 0:
                entries.append([(before, 4 * c + i) for i in range(4)])
            elif e == 4:
                entries.append([(after, 4 * c + i) for i in range(4)])
            else:
                entries.append([(u, (c, pl.ds(4 * e + i, 8, stride=sector), slice(None))) for i in range(4)])
    for c in range(3):
        for e in range(4):
            entries.append([(lm, (c, pl.ds(4 * e + i, 8, stride=sector), slice(None))) for i in range(4)])
    for n in range(4):
        rows = [ref[at] for entry in entries[8 * n : 8 * n + 8] for ref, at in entry]
        first, last = pack(rows, False, LES_WIDTH), pack(rows, True, LES_WIDTH)
        even[n] = jnp.where(right, last, first)
        odd[n] = jnp.where(right, first, last)


def les_element(um, ut, mm, e, weights, coef, with_flux):
    rows = [[um[c, 4 * e + i] for i in range(4)] for c in range(3)]
    tiles = [[ut[c, e]] for c in range(3)]
    prev = [um[c, 4 * e - 1] for c in range(3)]
    following = [um[c, 4 * e + 4] for c in range(3)]
    metric = [[mm[c, 4 * e + i] for i in range(4)] for c in range(3)]
    fields, halos = list(rows), list(tiles)
    if with_flux:
        fields += [[x * y for x, y in zip(rows[0], rows[c])] for c in range(3)]
        halos += [[tiles[0][0] * tiles[c][0]] for c in range(3)]
    stream = stream_main(fields, halos, weights[0], coef, LES_WIDTH)
    scaled = lambda j, values: [a * b for a, b in zip(metric[j], values)]
    slopes = [[scaled(0, stream[c]) for c in range(3)], [], []]
    fluxes = [[scaled(0, stream[3 + c]) for c in range(3)] if with_flux else [], [], []]
    for c in range(3):
        slopes[1].append(scaled(1, azimuth_main(rows[c], prev[c], following[c])))
        slopes[2].append(scaled(2, radial(rows[c], coef)))
        if with_flux:
            product = [x * y for x, y in zip(rows[1], rows[c])]
            fluxes[1].append(scaled(1, azimuth_main(product, prev[1] * prev[c], following[1] * following[c])))
            fluxes[2].append(scaled(2, radial([x * y for x, y in zip(rows[2], rows[c])], coef)))
    return rows, tiles, fields, halos, slopes, fluxes


def les_change(rows, slopes, fluxes, c, i):
    total = None
    for j in range(3):
        term = fluxes[j][c][i] + rows[j][i] * slopes[j][c][i]
        total = term if total is None else total + term
    return (0.5 * les_step) * total


def lamb_of(rows, slopes, lamb, e):
    for i in range(4):
        first = slopes[1][2][i] - slopes[2][1][i]
        second = slopes[2][0][i] - slopes[0][2][i]
        third = slopes[0][1][i] - slopes[1][0][i]
        lamb[0, 4 * e + i] = second * rows[2][i] - third * rows[1][i]
        lamb[1, 4 * e + i] = third * rows[0][i] - first * rows[2][i]
        lamb[2, 4 * e + i] = first * rows[1][i] - second * rows[0][i]


def les_kernel(
    sector, sends_far, u, lm, before, after, odd, even, mask, weights, coef, sent, um1, ut1, um, ut, mm, mt, lamb, blk, sends, arrived,
):
    fetch = pltpu.make_async_copy(sends_far, sends, arrived)
    fetch.start()
    from_left, from_right = sides(mask, even, odd)
    for c in range(3):
        for i in range(4):
            um[c, i] = before[4 * c + i]
            um[c, 4 + sector + i] = after[4 * c + i]
        mm[c, 3] = before[12 + c]
        mm[c, 4 + sector] = after[12 + c]
        for az in range(sector):
            um[c, 4 + az] = column(u, c, az, sector)
            mm[c, 4 + az] = column(lm, c, az, sector)
        for e in range(6):
            ut[c, e] = halo_tile(from_left, from_right, 6 * c + e, LES_WIDTH)
        for e in range(4):
            mt[c, e + 1] = halo_tile(from_left, from_right, 18 + 4 * c + e, LES_WIDTH)

    tiles, fields, ends = [], [], []
    for e, i in ((0, 3), (5, 0)):
        near = 4 if e == 0 else 3 + sector
        rows = [um[c, 4 * e + i] for c in range(3)]
        others = [[um[c, 4 * e + k] for k in range(4)] for c in range(3)]
        beyond = [um[c, near] for c in range(3)]
        halo = [ut[c, e] for c in range(3)]
        fields += rows + [rows[0] * rows[c] for c in range(3)]
        tiles += [(t, i) for t in halo + [halo[0] * halo[c] for c in range(3)]]
        ends.append((4 * e + i, i, rows, others, beyond))
    out = times(fields, weights[0])
    out = [y + coef[EDGE_M] * edge_main(t, i, LES_WIDTH) for y, (t, i) in zip(out, tiles)]
    for n, (at, i, rows, others, beyond) in enumerate(ends):
        metric = [mm[j, at] for j in range(3)]
        for c in range(3):
            slope = azimuth_main(others[c], beyond[c], beyond[c])[i]
            flux = azimuth_main([x * y for x, y in zip(others[1], others[c])], *[beyond[1] * beyond[c]] * 2)[i]
            total = metric[0] * (out[6 * n + 3 + c] + rows[0] * out[6 * n + c]) + metric[1] * (flux + rows[1] * slope)
            slope, flux = radial([rows[c], rows[2] * rows[c]], coef)
            total = total + metric[2] * (flux + rows[2] * slope)
            um1[c, at] = rows[c] - (0.5 * les_step) * total
        if i == 3:
            for c in range(3):
                for k in range(3):
                    um1[c, k] = rows[c]
                    um1[c, 5 + sector + k] = rows[c]

    for e in range(1, 5):
        rows, tiles, fields, halos, slopes, fluxes = les_element(um, ut, mm, e, weights, coef, True)
        lamb_of(rows, slopes, lamb, e)
        for c in range(3):
            for i in range(4):
                um1[c, 4 * e + i] = rows[c][i] - les_change(rows, slopes, fluxes, c, i)
        low = [ut[c, e - 1] for c in range(3)]
        high = [ut[c, e + 1] for c in range(3)]
        metric = [mt[c, e] for c in range(3)]
        stream = stream_halo(fields, halos, weights[1], coef, LES_WIDTH)
        for c in range(3):
            total = metric[0] * (stream[3 + c][0] + tiles[0][0] * stream[c][0])
            slope = azimuth_halo(tiles[c], low[c], high[c], coef, LES_WIDTH)[0]
            product = tiles[1][0] * tiles[c][0]
            flux = azimuth_halo([product], low[1] * low[c], high[1] * high[c], coef, LES_WIDTH)[0]
            total = total + metric[1] * (flux + tiles[1][0] * slope)
            slope, flux = radial([tiles[c][0], tiles[2][0] * tiles[c][0]], coef)
            total = total + metric[2] * (flux + tiles[2][0] * slope)
            ut1[c, e - 1] = tiles[c][0] - (0.5 * les_step) * total

    def blocks(step):
        for c in range(3):
            tiles = turn([lamb[c, 4 + az] for az in range(sector)])
            for j in range(16):
                blk[j, 3 * step + c] = tiles[j].astype(BF16)

    blocks(0)
    fetch.wait()

    for e in range(1, 5):
        rows, _, _, _, slopes, _ = les_element(um1, Shifted(ut1), mm, e, weights, coef, False)
        lamb_of(rows, slopes, lamb, e)

    blocks(1)
    for n in range(sends.shape[0]):
        index = jnp.clip(sends[n], 0, 15)
        for k in range(6):
            sent[n, k] = blk[index, k]


class Shifted:
    def __init__(self, ref):
        self.ref = ref

    def __getitem__(self, at):
        return self.ref[at[0], at[1] - 1]


def les_out_kernel(sector, lm, um1, ut1, weights, coef, out, mm):
    for c in range(3):
        for az in range(sector):
            mm[c, 4 + az] = column(lm, c, az, sector)

    @pl.loop(1, 5)
    def _(e):
        rows, _, _, _, slopes, fluxes = les_element(um1, Shifted(ut1), mm, e, weights, coef, True)
        for c in range(3):
            for i in range(4):
                out[c, pl.ds(4 * (e - 1) + i, 8, stride=sector), :] = rows[c][i] - les_change(rows, slopes, fluxes, c, i)


def blend_kernel(sector, refs, got, own, up, down, mixed):
    for j in range(16):
        a = jnp.clip(refs[4 * j] * 2 + refs[4 * j + 1], 0, got.shape[0] - 1)
        b = jnp.clip(refs[4 * j + 2] * 2 + refs[4 * j + 3], 0, got.shape[0] - 1)
        fraction = refs[64 + j].astype(F32)
        for k in range(6):
            blend = (8.0 - fraction) * got[a, k].astype(F32) + fraction * got[b, k].astype(F32)
            mixed[k, j] = blend * 0.125
    for step in range(2):
        for c in range(3):
            tiles = turn([mixed[3 * step + c, j] for j in range(16)])
            for az in range(sector):
                own[step, c, az] = tiles[az]
                narrow = tiles[az].astype(BF16)
                if step == 0:
                    up[c * 16 + az] = narrow
                    down[c * 16 + az] = narrow
                elif az >= 8:
                    up[48 + c * 8 + az - 8] = narrow
                else:
                    down[48 + c * 8 + az] = narrow


def pack_entries(entries, order, mask, even, odd):
    right = mask[...] > 0.5
    results = []
    for way in range(2):
        tiles = []
        for n in range(len(entries) // 2):
            rows = [ref[at].astype(F32) for ref, at in entries[2 * n] + entries[2 * n + 1]]
            tiles.append(pack(rows, way == 1, CAA_WIDTH))
        x = jnp.concatenate(tiles, axis=0).astype(BF16)
        y = jnp.dot(x, order[way], preferred_element_type=F32)
        results.append([y[8 * n : 8 * n + 8] for n in range(len(tiles))])
    for n, (first, last) in enumerate(zip(*results)):
        even[n] = jnp.where(right, last, first).astype(BF16)
        odd[n] = jnp.where(right, first, last).astype(BF16)


def state_pack_kernel(sector, below, above, both, order, mask, even, odd):
    entries = []
    for f in range(7):
        for e in range(12):
            ref = (below, both, above)[e // 4]
            entries.append([(ref, f * sector + 4 * (e % 4) + i) for i in range(4)])
    pack_entries(entries, order, mask, even, odd)


def source_pack_kernel(sector, own, below, above, order, mask, even, odd):
    entries = []
    for c in range(3):
        for e in range(12):
            if 4 <= e < 8:
                entries.append([(own, (0, c, 4 * (e - 4) + i)) for i in range(4)])
            else:
                entries.append([(below if e < 4 else above, c * 16 + 4 * (e % 4) + i) for i in range(4)])
    for c in range(3):
        for e in range(2, 10):
            if 4 <= e < 8:
                entries.append([(own, (1, c, 4 * (e - 4) + i)) for i in range(4)])
            elif e < 4:
                entries.append([(below, 48 + c * 8 + 4 * (e - 2) + i) for i in range(4)])
            else:
                entries.append([(above, 48 + c * 8 + 4 * (e - 8) + i) for i in range(4)])
    pack_entries(entries, order, mask, even, odd)


CAA_DEPTHS = (13, 12, 9, 8, 5, 4, 1, 0)
CAA_RANGES = ((0, 12), (1, 11), (1, 11), (2, 10), (2, 10), (3, 9), (3, 9), (4, 8))


def caa_kernel(
    sector, w, m, own, below, above, caa_below, caa_above, state_odd, state_even, odd, even, mask, weights, coef, upward,
    out, wm, wt, mm, mt, sm, st,
):
    state_left, state_right = sides(mask, state_even, state_odd)
    from_left, from_right = sides(mask, even, odd)
    for f in range(7):
        for az in range(3 * sector):
            if az < sector:
                value = caa_below[f * sector + az].astype(F32)
            elif az < 2 * sector:
                value = column(w, f, az - sector, sector) if f < 4 else column(m, f - 4, az - sector, sector)
            else:
                value = caa_above[f * sector + az - 2 * sector].astype(F32)
            if f < 4:
                wm[0, f, az] = value
            else:
                mm[f - 4, az] = value * caa_step
        for e in range(12):
            value = acoustic_tile(state_left, state_right, 12 * f + e)
            if f < 4:
                wt[0, f, e] = value
            else:
                mt[f - 4, e] = value * caa_step
    for c in range(3):
        for az in range(16):
            sm[0, c, az] = below[c * 16 + az].astype(F32) * caa_step
            sm[0, c, 16 + az] = own[0, c, az] * caa_step
            sm[0, c, 32 + az] = above[c * 16 + az].astype(F32) * caa_step
            sm[1, c, 16 + az] = own[1, c, az] * caa_step
        for az in range(8):
            sm[1, c, 8 + az] = below[48 + c * 8 + az].astype(F32) * caa_step
            sm[1, c, 32 + az] = above[48 + c * 8 + az].astype(F32) * caa_step
        for e in range(12):
            st[0, c, e] = acoustic_tile(from_left, from_right, 12 * c + e) * caa_step
        for e in range(8):
            st[1, c, 2 + e] = acoustic_tile(from_left, from_right, 36 + 8 * c + e) * caa_step

    def along(tiles, which):
        x = jnp.concatenate(tiles, axis=0).astype(BF16)
        y = jnp.dot(x, weights[which], preferred_element_type=F32)
        y = y[:, :128] + y[:, 128:]
        return [y[8 * n : 8 * n + 8] for n in range(len(tiles))]

    def pair(now, source, e, final, depth):
        rows = [[wm[now, f, 4 * e + i] for i in range(8)] for f in range(4)]
        tiles = [[wt[now, f, e + n] for n in range(2)] for f in range(4)]
        below, above, tile_below, tile_above = max(4 * e - 1, 0), min(4 * e + 8, 47), max(e - 1, 0), min(e + 2, 11)

        def mixed(values):
            p, v0, v1, v2 = values
            return [
                [mach_number * a + b for a, b in zip(p, v0)],
                [mach_number * b + a for a, b in zip(p, v0)],
                v1,
                v2,
            ]

        def update(needed, values, metric, sources, stream, around, up, store):
            p, v0, v1, v2 = values
            for n in needed:
                m0, m1, m2 = metric(0, n), metric(1, n), metric(2, n)
                half = mach_number * m0
                store(0, n, p[n] - m0 * stream[0][n] - m1 * around[1][n] - m2 * up[1][n])
                store(1, n, v0[n] - m0 * stream[1][n] + sources(0, n))
                store(2, n, v1[n] - half * stream[2][n] - m1 * around[0][n] + sources(1, n))
                store(3, n, v2[n] - half * stream[3][n] - m2 * up[0][n] + sources(2, n))

        fields, halos = mixed(rows), mixed(tiles)
        x = [jnp.concatenate(rows[f] + tiles[f], axis=0).astype(BF16) for f in (0, 3)]
        y = jnp.dot(upward[...], jnp.concatenate(x, axis=1), preferred_element_type=F32)
        y = y[:80] + y[80:]
        up = [[y[8 * n : 8 * n + 8, 128 * f : 128 * f + 128] for n in range(10)] for f in range(2)]

        stream = along([row for values in fields for row in values], 0)
        stream = [[stream[8 * f + n] for n in range(8)] for f in range(4)]
        for f in range(4):
            for n in range(8):
                edge = lane_roll(halos[f][n // 4], -32 * (n % 4) - 16)
                stream[f][n] = stream[f][n] + coef[8] * edge
        around = [azimuth_main(rows[f], wm[now, f, below], wm[now, f, above]) for f in (0, 2)]

        def store(f, n, value):
            if final:
                out[f, pl.ds(4 * e + n - 16, 8, stride=sector), :] = value
            else:
                wm[1 - now, f, 4 * e + n] = value

        for n in range(8):
            if not 16 - depth <= 4 * e + n < 32 + depth:
                for f in range(4):
                    wm[1 - now, f, 4 * e + n] = rows[f][n]
        needed = [n for n in range(8) if 16 - depth <= 4 * e + n < 32 + depth]
        update(needed, rows, lambda c, n: mm[c, 4 * e + n], lambda c, n: sm[source, c, 4 * e + n], stream, around, up, store)
        if final:
            return

        stream = along([tile for values in halos for tile in values], 1)
        stream = [[stream[2 * f + n] for n in range(2)] for f in range(4)]
        run = lanes_of() // 32
        for f in range(4):
            for n in range(2):
                edge = None
                for i in range(4):
                    moved = lane_roll(fields[f][4 * n + i], 32 * i + 16)
                    edge = moved if edge is None else jnp.where(run == i, moved, edge)
                stream[f][n] = stream[f][n] + coef[9] * edge
        around = []
        for f in (0, 2):
            values = []
            for n in range(2):
                before = wt[now, f, tile_below] if n == 0 else tiles[f][0]
                after = wt[now, f, tile_above] if n == 1 else tiles[f][1]
                total = coef[WHOLE_P] * lane_roll(before, -96) + coef[WHOLE_N] * lane_roll(after, 96)
                for k, offset in enumerate(OFFSETS):
                    total = total + coef[WHOLE_T + k] * lane_roll(tiles[f][n], -32 * offset)
                values.append(total)
            around.append(values)

        def store(f, n, value):
            wt[1 - now, f, e + n] = value

        up = [values[8:] for values in up]
        update(range(2), tiles, lambda c, n: mt[c, e + n], lambda c, n: st[source, c, e + n], stream, around, up, store)

    for step, (start, stop) in enumerate(CAA_RANGES):
        for e in range(start, stop, 2):
            pair(step % 2, step // 4, e, step == 7, CAA_DEPTHS[step])


def call(kernel, name, outs, *args, smem=0, far=0, free=0, scratch=()):
    whole, hbm = pl.BlockSpec(memory_space=pltpu.VMEM), pl.BlockSpec(memory_space=pltpu.HBM)
    args = [pltpu.with_memory_space_constraint(x, pltpu.HBM) if smem <= n < smem + far else x for n, x in enumerate(args)]
    specs = [pl.BlockSpec(memory_space=pltpu.SMEM)] * smem + [hbm] * far + [pl.BlockSpec(memory_space=pl.ANY)] * free
    return pl.pallas_call(
        kernel,
        name=name,
        out_shape=[jax.ShapeDtypeStruct(shape, dtype) for shape, dtype in outs],
        in_specs=specs + [whole] * (len(args) - smem - far - free),
        out_specs=[whole] * len(outs),
        scratch_shapes=list(scratch),
        compiler_params=pltpu.CompilerParams(vmem_limit_bytes=VMEM_LIMIT),
    )(*args)


def swap_pairs(ours, theirs, axis):
    count = lax.axis_size(axis)
    edges = lambda start: [pair for a in range(start, count - 1, 2) for pair in ((a, a + 1), (a + 1, a))]
    odd = lax.ppermute(theirs, axis, edges(1))
    even = lax.ppermute(ours, axis, edges(0))
    return even, odd


def both_ways(low, high, axis, closed):
    count = lax.axis_size(axis)
    ends = count if closed else count - 1
    below = lax.ppermute(high, axis, [(i, (i + 1) % count) for i in range(ends)])
    above = lax.ppermute(low, axis, [((i + 1) % count, i) for i in range(ends)])
    return below, above


def body(les_velocity, les_metric, caa_state, caa_metric, intersection_refs, offsets, send_list):
    _, radial_nodes, sector, length = les_velocity.shape
    slabs = lax.axis_size("gx")
    assert (radial_nodes, sector, length) == (8, 16, 128)
    lines = radial_nodes * sector
    u, lm, w, m = (x.reshape(-1, lines, length) for x in (les_velocity, les_metric, caa_state, caa_metric))
    les_weights = jnp.asarray(np.stack([split_matrix(128), split_matrix(LES_WIDTH)]))
    les_coef = jnp.asarray(coefficients(LES_WIDTH))
    caa_weights, caa_coef = jnp.asarray(acoustic_weights()), jnp.asarray(acoustic_coefficients())
    upward, order = jnp.asarray(radial_matrix(10)), jnp.asarray(halo_order())
    own_row = lax.axis_index("sec") * slabs + lax.axis_index("gx")
    sends = lax.dynamic_slice_in_dim(send_list, own_row, 1, axis=0).reshape(-1)
    tile = (8, 128)
    mask = jnp.broadcast_to(((own_row + 1) % 2).astype(F32), tile)
    vmem = lambda *shape, dtype=F32: pltpu.VMEM((*shape, *tile), dtype)

    low, high = call(
        functools.partial(first_kernel, sector),
        "first",
        [((15, *tile), F32)] * 2,
        u, lm,
        far=2,
        scratch=[pltpu.VMEM(u.shape, F32), pltpu.VMEM(lm.shape, F32), pltpu.SemaphoreType.DMA((2,))],
    )
    before, after = both_ways(low, high, "az", True)
    even, odd = call(
        functools.partial(les_pack_kernel, sector),
        "les_pack",
        [((4, *tile), F32)] * 2,
        u, lm, before, after, mask,
    )
    even, odd = swap_pairs(even, odd, STREAM)
    sent, um1, ut1 = call(
        functools.partial(les_kernel, sector),
        "les",
        [((slabs * 2, 6, *tile), BF16), ((3, 24, *tile), F32), ((3, 4, *tile), F32)],
        sends, u, lm, before, after, odd, even, mask, les_weights, les_coef,
        free=1,
        scratch=[
            vmem(3, 24), vmem(3, 6), vmem(3, 24), vmem(3, 6), vmem(3, 24), vmem(16, 6, dtype=BF16),
            pltpu.SMEM(sends.shape, jnp.int32), pltpu.SemaphoreType.DMA,
        ],
    )
    got = lax.all_to_all(sent.reshape(slabs, 96, 128), "gx", 0, 0, tiled=True).reshape(slabs * 2, 6, *tile)

    (both,) = call(functools.partial(narrow_kernel, sector), "narrow", [((7 * sector, *tile), BF16)], w, m)
    caa_below, caa_above = both_ways(both, both, "az", True)
    (les_out,) = call(
        functools.partial(les_out_kernel, sector),
        "les_out",
        [((3, lines, length), F32)],
        lm, um1, ut1, les_weights, les_coef,
        scratch=[vmem(3, 24)],
    )
    even, odd = call(
        functools.partial(state_pack_kernel, sector),
        "state_pack",
        [((42, *tile), BF16)] * 2,
        caa_below, caa_above, both, order, mask,
    )
    state_even, state_odd = swap_pairs(even, odd, STREAM)
    table = jnp.concatenate([intersection_refs.reshape(-1), offsets])
    got, table, state_odd, state_even, les_out = lax.optimization_barrier((got, table, state_odd, state_even, les_out))

    own, up, down = call(
        functools.partial(blend_kernel, sector),
        "blend",
        [((2, 3, sector, *tile), F32), ((72, *tile), BF16), ((72, *tile), BF16)],
        table, got,
        smem=1,
        scratch=[vmem(6, 16)],
    )
    below, above = both_ways(down, up, "az", True)
    even, odd = call(
        functools.partial(source_pack_kernel, sector),
        "source_pack",
        [((30, *tile), BF16)] * 2,
        own, below, above, order, mask,
    )
    even, odd = swap_pairs(even, odd, STREAM)
    (caa_out,) = call(
        functools.partial(caa_kernel, sector),
        "caa",
        [((4, lines, length), F32)],
        w, m, own, below, above, caa_below, caa_above, state_odd, state_even, odd, even, mask, caa_weights, caa_coef, upward,
        scratch=[vmem(2, 4, 48), vmem(2, 4, 12), vmem(3, 48), vmem(3, 12), vmem(2, 3, 48), vmem(2, 3, 12)],
    )
    return les_out.reshape(les_velocity.shape), caa_out.reshape(caa_state.shape)


def solution(mesh):
    field = P(None, None, "az", STREAM)
    in_specs = (field, field, field, field, P(STREAM, None), P(STREAM), P())
    return jax.shard_map(body, mesh=mesh, in_specs=in_specs, out_specs=(field, field), check_vma=False)
```
